32 devices in a mesh: rep: 2 (over core), shard: 16 (over z, y, x).
Axes of the slice: x: 2, y: 2, z: 4, core: 2. Of those that a mesh axis runs over, the one named last changes fastest.
Arguments:
- incoming_tokens: bfloat16 [16384, 768], P(('rep', 'shard')), may hold values from -6 to 6
- mentor_outputs: bfloat16 [16384, 768], P(('rep', 'shard')), may hold values from -6 to 6
- counting_flags: int32 [16384], P(('rep', 'shard')), may hold values from 0 to 1, as said below
- opening_scale_factor: bfloat16 [768], P('shard'), may hold values from 0.5 to 1.5
- opening_offset_vector: bfloat16 [768], P('shard'), may hold values from -1.796875 to 1.796875
- query_key_value_map: bfloat16 [768, 2304], P('shard'), may hold values from -0.21875 to 0.21875
- asking_offset: bfloat16 [768], P('shard'), may hold values from -1.796875 to 1.796875
- content_offset: bfloat16 [768], P('shard'), may hold values from -0.29882812 to 0.29882812
- attend_result_map: bfloat16 [768, 768], P('shard'), may hold values from -4 to 4
- attend_result_offset: bfloat16 [768], P('shard'), may hold values from -1.796875 to 1.796875
- latter_scale_factor: bfloat16 [768], P('shard'), may hold values from 0.5 to 1.5
- latter_offset_vector: bfloat16 [768], P('shard'), may hold values from -1.796875 to 1.796875
- widen_projection: bfloat16 [768, 3072], P('shard'), may hold values from -0.21875 to 0.21875
- hidden_offset: bfloat16 [3072], P('shard'), may hold values from -1.796875 to 1.796875
- narrow_projection: bfloat16 [3072, 768], P('shard'), may hold values from -0.109375 to 0.109375
- narrow_offset: bfloat16 [768], P('shard'), may hold values from -1.796875 to 1.796875
Outputs:
- distill_loss: float32 [], replicated
- layer_output: bfloat16 [16384, 768], P(('rep', 'shard'))
- states_gradient: bfloat16 [16384, 768], P(('rep', 'shard'))
- pregain_gradient: float32 [768], P('shard')
- preshift_gradient: float32 [768], P('shard')
- inward_gradient: float32 [768, 2304], P('shard')
- querybias_gradient: float32 [768], P('shard')
- valuebias_gradient: float32 [768], P('shard')
- outward_gradient: float32 [768, 768], P('shard')
- outbias_gradient: float32 [768], P('shard')
- midgain_gradient: float32 [768], P('shard')
- midshift_gradient: float32 [768], P('shard')
- expand_gradient: float32 [768, 3072], P('shard')
- expandbias_gradient: float32 [3072], P('shard')
- shrink_gradient: float32 [3072, 768], P('shard')
- shrinkbias_gradient: float32 [768], P('shard')
The draws below stay inside these ranges and needn't reach their ends.
Inputs may be any that keep to these rules, and one draw needn't show every extreme that they name: `counting_flags`: 1 marks a token that counts in the loss, 0 one that does not.
All inputs are finite; a program needn't handle non-finite values.
Results may differ from the reference program's by a relative error of at most 0.01.
Values may be sent and summed in bfloat16 or wider, within the bound.
No kernel may reach another device: no remote copies, remote signals or barrier semaphores. Data moves between devices by JAX's collectives and lax.ppermute only.
A program may use at most 448 MiB of HBM per device.

```python
import jax
import jax.numpy as jnp
from jax import lax

H = 12
HD = 64
EMBED_SIZE = 768
FF = 3072
TOK_DEV = 512
SPLIT = 8
SEQ = 4096
BLOCK = 256
QROWS = 512
TOKENS = 16384
N_REP = 2
N_SHARD = 16


def draw_counting_flags(key, part):
    position = jnp.arange(TOKENS, dtype=jnp.int32)
    lottery = jax.random.randint(key, (TOKENS,), 0, 4 * TOKENS, dtype=jnp.int32)
    return (lottery < TOKENS + 2 * position).astype(jnp.int32)


def strengthened(drawn, own_key, source, target, shards_of, factor):
    owner, partner = [(jnp.arange(drawn.shape[dim]) // (drawn.shape[dim] // shards_of)).reshape([-1 if axis == dim else 1 for axis in range(drawn.ndim)]) for dim in (source, target)]
    chosen = jax.random.permutation(own_key, shards_of)[partner]
    strong = (owner == chosen) | (owner == (partner + shards_of // 2) % shards_of)
    return jnp.where(strong, factor * drawn, drawn)


def levels(stream_key, dims, pieces, smallest, largest):
    def one(axis_at, blocks):
        steps = jax.random.uniform(jax.random.fold_in(jax.random.fold_in(stream_key, 6), axis_at), (blocks,), jnp.float32, smallest / len(pieces), largest / len(pieces))
        return jnp.repeat(jnp.exp(steps), dims[axis_at] // blocks).reshape((-1,) + (1,) * (len(dims) - axis_at - 1))

    level = one(*pieces[0])
    for cut in pieces[1:]:
        level = level * one(*cut)
    return level


def normal_values(key, dims, width, limit, split=(), kind=jnp.bfloat16):
    values = jax.random.normal(key, dims, jnp.float32) * width
    if len(split) > 0:
        values = levels(key, dims, split, -0.22, 0.18) * values
    return jnp.clip(values, min=-limit, max=limit).astype(kind)


def noise_with(own_key, extent, scale, limit, cuts, heavy, kind=jnp.bfloat16):
    values = scale * jax.random.normal(own_key, extent, jnp.float32)
    if cuts:
        values = values * levels(own_key, extent, cuts, -0.22, 0.18)
    return jnp.clip(strengthened(values, jax.random.fold_in(own_key, 3), *heavy), -limit, limit).astype(kind)


def setup_inputs(seed: int = 0) -> dict:
    seeds = jax.random.split(jax.random.key(seed), 17)
    incoming_tokens = normal_values(seeds[0], (TOKENS, EMBED_SIZE), 1.0, 6.0, ((0, 32),))
    mentor_outputs = noise_with(seeds[1], (TOKENS, EMBED_SIZE), 1.0, 6.0, ((0, 32),), (0, 1, 32, 2.75))
    counting_flags = draw_counting_flags(jax.random.fold_in(seeds[16], 71), 0)
    opening_scale_factor = jnp.clip(1.0 + 0.1 * jax.random.normal(seeds[3], (EMBED_SIZE,), jnp.float32), 0.5, 1.5).astype(jnp.bfloat16)
    opening_offset_vector = normal_values(seeds[4], (EMBED_SIZE,), 0.3, 1.796875, ((0, 16),))
    query_key_value_map = normal_values(seeds[5], (EMBED_SIZE, 3 * EMBED_SIZE), EMBED_SIZE ** -0.5, 0.21875, ((0, 16),))
    asking_offset = normal_values(seeds[6], (EMBED_SIZE,), 0.3, 1.796875, ((0, 16),))
    content_offset = normal_values(seeds[7], (EMBED_SIZE,), 0.05, 0.29882812, ((0, 16),))
    attend_result_map = normal_values(seeds[8], (EMBED_SIZE, EMBED_SIZE), (max(EMBED_SIZE // 384, 1)) ** -0.5, 4.0, ((0, 16),))
    attend_result_offset = normal_values(seeds[9], (EMBED_SIZE,), 0.3, 1.796875, ((0, 16),))
    latter_scale_factor = jnp.clip(1.0 + 0.1 * jax.random.normal(seeds[10], (EMBED_SIZE,), jnp.float32), 0.5, 1.5).astype(jnp.bfloat16)
    latter_offset_vector = normal_values(seeds[11], (EMBED_SIZE,), 0.3, 1.796875, ((0, 16),))
    widen_projection = normal_values(seeds[12], (EMBED_SIZE, FF), EMBED_SIZE ** -0.5, 0.21875, ((0, 16),))
    hidden_offset = normal_values(seeds[13], (FF,), 0.3, 1.796875, ((0, 16),))
    narrow_projection = normal_values(seeds[14], (FF, EMBED_SIZE), FF ** -0.5, 0.109375, ((0, 16),))
    narrow_offset = normal_values(seeds[15], (EMBED_SIZE,), 0.3, 1.796875, ((0, 16),))
    return {"incoming_tokens": incoming_tokens, "mentor_outputs": mentor_outputs, "counting_flags": counting_flags, "opening_scale_factor": opening_scale_factor, "opening_offset_vector": opening_offset_vector, "query_key_value_map": query_key_value_map, "asking_offset": asking_offset, "content_offset": content_offset, "attend_result_map": attend_result_map, "attend_result_offset": attend_result_offset, "latter_scale_factor": latter_scale_factor, "latter_offset_vector": latter_offset_vector, "widen_projection": widen_projection, "hidden_offset": hidden_offset, "narrow_projection": narrow_projection, "narrow_offset": narrow_offset}


@jax.custom_vjp
def low(v):
    return lax.optimization_barrier(v.astype(jnp.bfloat16)).astype(jnp.float32)

@jax.custom_vjp
def low_back(v):
    return v

def low_keep(v):
    return (low(v), None)

def low_pass(kept, grad):
    return (grad,)

def back_keep(v):
    return (v, None)

def back_low(kept, grad):
    return (low(grad),)
low.defvjp(low_keep, low_pass)
low_back.defvjp(back_keep, back_low)
EPSILON = 1e-05
HIGHEST = lax.Precision.HIGHEST

def rescale_centering(values, gain, shift):
    center = values - lax.optimization_barrier(jnp.mean(values, axis=-1, keepdims=True))
    spread = lax.optimization_barrier(jnp.mean(center * center, axis=-1, keepdims=True))
    return center * lax.rsqrt(spread + EPSILON) * gain + shift

def attend_block(queries, keys_all, values_all, first_row):
    block_q = lax.dynamic_slice_in_dim(queries, first_row, QROWS, 0)
    scores = jnp.einsum('qhe,khe->hqk', block_q, keys_all, precision=HIGHEST) * HD ** (-0.5)
    scores = low_back(scores)
    query_place = first_row + jnp.arange(QROWS, dtype=jnp.int32)
    key_place = jnp.arange(SEQ, dtype=jnp.int32)
    allowed = key_place[None, :] // BLOCK <= query_place[:, None] // BLOCK
    masked = jnp.where(allowed[None], scores, -1e+30)
    row_peak = lax.optimization_barrier(jnp.max(masked, axis=-1, keepdims=True))
    exponent = jnp.exp(masked - row_peak)
    probs = exponent / lax.optimization_barrier(jnp.sum(exponent, axis=-1, keepdims=True))
    probs_low = low(probs)
    return jnp.einsum('hqk,khe->qhe', probs_low, values_all, precision=HIGHEST)

def forward(token_stretch, learnable_collection):
    opening_scale_factor, opening_offset_vector, query_key_value_map, asking_offset, content_offset, attend_result_map, attend_result_offset, latter_scale_factor, latter_offset_vector, widen_projection, hidden_offset, narrow_projection, narrow_offset = learnable_collection
    initial_rescaled = low(rescale_centering(token_stretch, opening_scale_factor, opening_offset_vector))
    packed_bias = jnp.concatenate([asking_offset, jnp.zeros_like(asking_offset), content_offset])
    projected = low(low_back(jnp.dot(initial_rescaled, query_key_value_map, precision=HIGHEST) + packed_bias))
    queries = projected[:, :EMBED_SIZE].reshape(SEQ, H, HD)
    keys_all = projected[:, EMBED_SIZE:2 * EMBED_SIZE].reshape(SEQ, H, HD)
    values_all = projected[:, 2 * EMBED_SIZE:].reshape(SEQ, H, HD)
    blockwise = jax.checkpoint(attend_block)
    starts = jnp.arange(SEQ // QROWS, dtype=jnp.int32) * QROWS
    blocks = lax.map(lambda start: blockwise(queries, keys_all, values_all, start), starts)
    mixed = low(low_back(blocks.reshape(SEQ, EMBED_SIZE)))
    branch = low_back(jnp.dot(mixed, attend_result_map, precision=HIGHEST) + attend_result_offset)
    middle = token_stretch + branch
    normed_two = low(rescale_centering(middle, latter_scale_factor, latter_offset_vector))
    pre_act = low_back(jnp.dot(normed_two, widen_projection, precision=HIGHEST) + hidden_offset)
    hidden = low(jax.nn.gelu(pre_act, approximate=True))
    branch_two = low_back(jnp.dot(hidden, narrow_projection, precision=HIGHEST) + narrow_offset)
    return middle + branch_two

def into_sequences(values):
    rest = values.shape[1:]
    grouped = values.reshape((N_REP, N_SHARD * TOK_DEV) + rest)
    grouped = jnp.roll(grouped, -(SPLIT // 2) * TOK_DEV, axis=1)
    return grouped.reshape((TOKENS // SEQ, SEQ) + rest)

def from_sequences(values):
    rest = values.shape[2:]
    grouped = values.reshape((N_REP, N_SHARD * TOK_DEV) + rest)
    grouped = jnp.roll(grouped, SPLIT // 2 * TOK_DEV, axis=1)
    return grouped.reshape((TOKENS,) + rest)

def reference(incoming_tokens, mentor_outputs, counting_flags, opening_scale_factor, opening_offset_vector, query_key_value_map, asking_offset, content_offset, attend_result_map, attend_result_offset, latter_scale_factor, latter_offset_vector, widen_projection, hidden_offset, narrow_projection, narrow_offset):
    learnable_collection = tuple((coefficient_table.astype(jnp.float32) for coefficient_table in (opening_scale_factor, opening_offset_vector, query_key_value_map, asking_offset, content_offset, attend_result_map, attend_result_offset, latter_scale_factor, latter_offset_vector, widen_projection, hidden_offset, narrow_projection, narrow_offset)))
    count = jnp.sum(counting_flags.astype(jnp.float32))
    seq_states = into_sequences(incoming_tokens.astype(jnp.float32))
    seq_teacher = into_sequences(mentor_outputs.astype(jnp.float32))
    seq_valid = into_sequences(counting_flags.astype(jnp.float32))

    def one_sequence(carry, inputs):
        squares_total, grad_totals = carry
        token_stretch, target, weight_rows = inputs

        def scaled_loss(piece_in, params_in):
            output = forward(piece_in, params_in)
            mismatch = output - target
            squares = jnp.sum(weight_rows[:, None] * mismatch * mismatch)
            return ((output, squares * (TOKENS / count)), squares)
        (output, scaled), pullback, squares = jax.vjp(scaled_loss, token_stretch, learnable_collection, has_aux=True)
        piece_grad, param_grads = pullback((jnp.zeros_like(output), jnp.ones_like(scaled)))
        new_totals = tuple((total + part for total, part in zip(grad_totals, param_grads)))
        return ((squares_total + squares, new_totals), (output.astype(jnp.bfloat16), piece_grad.astype(jnp.bfloat16)))
    start_totals = tuple((jnp.zeros_like(coefficient_table) for coefficient_table in learnable_collection))
    (squares_total, grads), (outputs, piece_grads) = lax.scan(one_sequence, (jnp.zeros((), jnp.float32), start_totals), (seq_states, seq_teacher, seq_valid))
    distill_loss = squares_total / count
    return (distill_loss, from_sequences(outputs), from_sequences(piece_grads), grads[0], grads[1], grads[2], grads[3], grads[4], grads[5], grads[6], grads[7], grads[8], grads[9], grads[10], grads[11], grads[12])
```

```python
from functools import partial

import jax
import jax.numpy as jnp
from jax import lax
from jax.experimental import pallas as pl
from jax.experimental.pallas import tpu as pltpu
from jax.sharding import PartitionSpec as P

H = 12
HD = 64
SPLIT = 8
BLOCK = 256
QUAD = SPLIT // 2
HL = H // QUAD
EPSILON = 1e-05
F32 = jnp.float32
BF16 = jnp.bfloat16
VMEM_LIMIT = 56 * 1024 * 1024


def dg(left, right, left_dim, right_dim):
    return lax.dot_general(
        left, right, (((left_dim,), (right_dim,)), ((), ())), preferred_element_type=F32
    )


def trade(array, mask):
    size = lax.axis_size("shard")
    return lax.ppermute(array, "shard", [(i, i ^ mask) for i in range(size)])


def trade_rep(array):
    return lax.ppermute(array, "rep", [(0, 1), (1, 0)])


def to_late(array):
    size = lax.axis_size("shard")
    pairs = [(i, (i + QUAD) % size) for i in range(size) if (i // QUAD) % 2 == 1]
    return lax.ppermute(array, "shard", pairs)


def to_early(array):
    size = lax.axis_size("shard")
    pairs = [(i, (i - QUAD) % size) for i in range(size) if (i // QUAD) % 2 == 0]
    return lax.ppermute(array, "shard", pairs)


def in_order(pieces, place):
    low, high = place & 1, place >> 1
    first = jnp.where(
        low == 1,
        jnp.stack([pieces[1], pieces[0], pieces[3], pieces[2]]),
        jnp.stack(pieces),
    )
    return jnp.where(high == 1, jnp.concatenate([first[2:], first[:2]]), first)


def pair_in_order(bit, own, other):
    return jnp.where(bit == 1, jnp.stack([other, own]), jnp.stack([own, other]))


def normalize(values):
    center = values - jnp.mean(values, axis=-1, keepdims=True)
    spread = jnp.mean(center * center, axis=-1, keepdims=True)
    factor = lax.rsqrt(spread + EPSILON)
    return (center * factor, factor)


def column_sums(values):
    return jnp.sum(values.astype(F32), axis=0)


def enter(place, pieces, weight, bias, gain, shift):
    length, width = pieces[0].shape
    cols = 3 * HL * HD

    def kernel(place_ref, x0, x1, x2, x3, w_ref, bias_ref, gain_ref, shift_ref, xn_ref, pt_ref, xs, wt):
        step = pl.program_id(0)

        @pl.when(step == 0)
        def _():
            wt[...] = w_ref[:, :cols].T

        for number, ref in enumerate((x0, x1, x2, x3)):

            @pl.when(step == number)
            def _():
                xs[...] = ref[...].astype(F32)

        normal, _ = normalize(xs[...])
        normed = (normal * gain_ref[...] + shift_ref[...]).astype(BF16)
        xn_ref[...] = normed
        out = (dg(wt[...], normed, 1, 1) + bias_ref[...]).astype(BF16)
        head_rows = HL * HD
        pt_ref[:head_rows] = (out[:head_rows].astype(F32) * HD ** (-0.5)).astype(BF16)
        pt_ref[head_rows:] = out[head_rows:]

    whole = lambda array: pl.BlockSpec(array.shape, lambda p, c: (0,) * array.ndim)
    return pl.pallas_call(
        kernel,
        grid_spec=pltpu.PrefetchScalarGridSpec(
            num_scalar_prefetch=1,
            grid=(QUAD,),
            in_specs=[whole(a) for a in (*pieces, weight, bias, gain, shift)],
            out_specs=[
                pl.BlockSpec((length, width), lambda p, c: (c[0] ^ p, 0)),
                pl.BlockSpec((cols, length), lambda p, c: (0, c[0] ^ p)),
            ],
            scratch_shapes=[pltpu.VMEM((length, width), F32), pltpu.VMEM((cols, width), BF16)],
        ),
        out_shape=[
            jax.ShapeDtypeStruct((QUAD * length, width), BF16),
            jax.ShapeDtypeStruct((cols, QUAD * length), BF16),
        ],
        compiler_params=pltpu.CompilerParams(vmem_limit_bytes=VMEM_LIMIT),
        name="enter",
    )(place, *pieces, weight, bias, gain, shift)


def own_forward(heads):
    tokens = heads.shape[2]

    def kernel(q_ref, k_ref, v_ref, o_ref, l_ref):
        for block in range(tokens // BLOCK):
            limit = (block + 1) * BLOCK
            here = slice(block * BLOCK, limit)
            scores = dg(k_ref[0, :, :limit], q_ref[0, :, here], 0, 0)
            peak = jnp.max(scores, axis=0, keepdims=True)
            probs = jnp.exp(scores - peak)
            mass = jnp.sum(probs, axis=0, keepdims=True)
            o_ref[0, :, here] = dg(v_ref[0, :, :limit], probs.astype(BF16), 1, 0) / mass
            l_ref[0, :, here] = peak + jnp.log(mass)

    spec = lambda first: pl.BlockSpec((1, HD, tokens), lambda h: (h + first, 0, 0))
    return pl.pallas_call(
        kernel,
        grid=(HL,),
        in_specs=[spec(0), spec(HL), spec(2 * HL)],
        out_specs=[spec(0), pl.BlockSpec((1, 1, tokens), lambda h: (h, 0, 0))],
        out_shape=[
            jax.ShapeDtypeStruct((HL, HD, tokens), F32),
            jax.ShapeDtypeStruct((HL, 1, tokens), F32),
        ],
        compiler_params=pltpu.CompilerParams(vmem_limit_bytes=VMEM_LIMIT),
        name="own_forward",
    )(heads, heads, heads)


def late_unit(rows, tokens):
    return pl.BlockSpec((1, rows, tokens // 2), lambda u: ((3 + u) // 2, 0, (3 + u) % 2))


def unit(rows, tokens):
    return pl.BlockSpec((1, rows, tokens // 2), lambda u: (u, 0, 0))


def pair_specs(tokens):
    spec = lambda index: pl.BlockSpec((1, HD, tokens), index)
    return [
        spec(lambda u: (HL + u // 2, 0, 0)),
        spec(lambda u: (2 * HL + u // 2, 0, 0)),
        spec(lambda u: ((u + 1) // 2, 0, 0)),
        spec(lambda u: (2 + (u + 1) // 2, 0, 0)),
    ]


SCALAR = pl.BlockSpec(memory_space=pltpu.SMEM)


def cross_forward(late, heads, q_sent, pair_sent):
    tokens = heads.shape[2]

    def kernel(late_ref, q_own, q_got, k_own, v_own, k_got, v_got, o_ref, l_ref, qs, ks, vs):
        @pl.when(late_ref[0] == 1)
        def _():
            qs[...] = q_own[0]
            ks[...] = k_got[0]
            vs[...] = v_got[0]

        @pl.when(late_ref[0] == 0)
        def _():
            qs[...] = q_got[0]
            ks[...] = k_own[0]
            vs[...] = v_own[0]

        for block in range(tokens // 2 // BLOCK):
            here = slice(block * BLOCK, (block + 1) * BLOCK)
            scores = dg(ks[...], qs[:, here], 0, 0)
            peak = jnp.max(scores, axis=0, keepdims=True)
            probs = jnp.exp(scores - peak)
            mass = jnp.sum(probs, axis=0, keepdims=True)
            o_ref[0, :, here] = dg(vs[...], probs.astype(BF16), 1, 0) / mass
            l_ref[0, :, here] = peak + jnp.log(mass)

    return pl.pallas_call(
        kernel,
        grid=(3,),
        in_specs=[SCALAR, late_unit(HD, tokens), unit(HD, tokens), *pair_specs(tokens)],
        out_specs=[unit(HD, tokens), unit(1, tokens)],
        out_shape=[
            jax.ShapeDtypeStruct((3, HD, tokens // 2), F32),
            jax.ShapeDtypeStruct((3, 1, tokens // 2), F32),
        ],
        scratch_shapes=[
            pltpu.VMEM((HD, tokens // 2), BF16),
            pltpu.VMEM((HD, tokens), BF16),
            pltpu.VMEM((HD, tokens), BF16),
        ],
        compiler_params=pltpu.CompilerParams(vmem_limit_bytes=VMEM_LIMIT),
        name="cross_forward",
    )(late, heads, q_sent, heads, heads, pair_sent, pair_sent)


def merge(late, o_own, l_own, o_got, l_got, o_here, l_here):
    tokens = o_own.shape[2]

    def kernel(late_ref, o_ref, l_ref, og_ref, lg_ref, oh_ref, lh_ref, out_ref, low_ref, total_ref):
        got = pl.program_id(0) < 3
        other = jnp.where(got, og_ref[0].astype(F32), oh_ref[0])
        level = jnp.where(got, lg_ref[0], lh_ref[0])
        level = jnp.where(late_ref[0] == 1, level, -1e30)
        own_level = l_ref[0]
        peak = jnp.maximum(own_level, level)
        own_part = jnp.exp(own_level - peak)
        part = jnp.exp(level - peak)
        mass = own_part + part
        out = o_ref[0] * (own_part / mass) + other * (part / mass)
        out_ref[0] = out
        low_ref[0] = out.astype(BF16)
        total_ref[0] = peak + jnp.log(mass)

    half = lambda rows: pl.BlockSpec((1, rows, tokens // 2), lambda u: (u // 2, 0, u % 2))
    got = lambda rows: pl.BlockSpec((1, rows, tokens // 2), lambda u: (jnp.minimum(u, 2), 0, 0))
    here = lambda rows: pl.BlockSpec((1, rows, tokens // 2), lambda u: (jnp.maximum(u - 3, 0), 0, 0))
    return pl.pallas_call(
        kernel,
        grid=(6,),
        in_specs=[SCALAR, half(HD), half(1), got(HD), got(1), here(HD), here(1)],
        out_specs=[half(HD), half(HD), half(1)],
        out_shape=[
            jax.ShapeDtypeStruct(o_own.shape, F32),
            jax.ShapeDtypeStruct(o_own.shape, BF16),
            jax.ShapeDtypeStruct(l_own.shape, F32),
        ],
        name="merge",
    )(late, o_own, l_own, o_got, l_got, o_here, l_here)


def grad_block(q, g, k, v, level, inner):
    probs = jnp.exp(dg(k, q, 0, 0) - level)
    score_grad = (probs * (dg(v, g, 0, 0) - inner)).astype(BF16)
    query_grad = dg(k, score_grad, 1, 0) * HD ** (-0.5)
    return query_grad, dg(q, score_grad, 1, 1), dg(g, probs.astype(BF16), 1, 1)


def own_backward(heads, grads, levels, inners):
    tokens = heads.shape[2]

    def kernel(q_ref, k_ref, v_ref, g_ref, l_ref, d_ref, dq_ref, dk_ref, dv_ref):
        dk_ref[...] = jnp.zeros_like(dk_ref)
        dv_ref[...] = jnp.zeros_like(dv_ref)
        for block in range(tokens // BLOCK):
            limit = (block + 1) * BLOCK
            here = slice(block * BLOCK, limit)
            dq, dk, dv = grad_block(
                q_ref[0, :, here],
                g_ref[0, :, here],
                k_ref[0, :, :limit],
                v_ref[0, :, :limit],
                l_ref[0, :, here],
                d_ref[0, :, here],
            )
            dq_ref[0, :, here] = dq
            dk_ref[0, :, :limit] += dk
            dv_ref[0, :, :limit] += dv

    spec = lambda first: pl.BlockSpec((1, HD, tokens), lambda h: (h + first, 0, 0))
    row = pl.BlockSpec((1, 1, tokens), lambda h: (h, 0, 0))
    return pl.pallas_call(
        kernel,
        grid=(HL,),
        in_specs=[spec(0), spec(HL), spec(2 * HL), spec(0), row, row],
        out_specs=[spec(0)] * 3,
        out_shape=[jax.ShapeDtypeStruct((HL, HD, tokens), F32)] * 3,
        compiler_params=pltpu.CompilerParams(vmem_limit_bytes=VMEM_LIMIT),
        name="own_backward",
    )(heads, heads, heads, grads, levels, inners)


def cross_backward(late, heads, grads, levels, inners, q_sent, pair_sent, g_sent, stats_sent):
    tokens = heads.shape[2]

    def kernel(
        late_ref, q_own, g_own, l_own, d_own, q_got, g_got, l_got, d_got, k_own, v_own, k_got, v_got,
        dq_ref, dk_ref, dv_ref, qs, gs, ls, ds, ks, vs,
    ):
        @pl.when(late_ref[0] == 1)
        def _():
            qs[...] = q_own[0]
            gs[...] = g_own[0]
            ls[...] = l_own[0]
            ds[...] = d_own[0]
            ks[...] = k_got[0]
            vs[...] = v_got[0]

        @pl.when(late_ref[0] == 0)
        def _():
            qs[...] = q_got[0]
            gs[...] = g_got[0]
            ls[...] = l_got[0]
            ds[...] = d_got[0]
            ks[...] = k_own[0]
            vs[...] = v_own[0]

        for block in range(tokens // 2 // BLOCK):
            here = slice(block * BLOCK, (block + 1) * BLOCK)
            dq, dk, dv = grad_block(qs[:, here], gs[:, here], ks[...], vs[...], ls[:, here], ds[:, here])
            dq_ref[0, :, here] = dq
            if block == 0:
                dk_ref[0] = dk
                dv_ref[0] = dv
            else:
                dk_ref[0] += dk
                dv_ref[0] += dv

    whole = pl.BlockSpec((1, HD, tokens), lambda u: (u, 0, 0))
    stat = lambda first: pl.BlockSpec((1, 1, tokens // 2), lambda u: (u + first, 0, 0))
    return pl.pallas_call(
        kernel,
        grid=(3,),
        in_specs=[
            SCALAR,
            late_unit(HD, tokens),
            late_unit(HD, tokens),
            late_unit(1, tokens),
            late_unit(1, tokens),
            unit(HD, tokens),
            unit(HD, tokens),
            stat(0),
            stat(3),
            *pair_specs(tokens),
        ],
        out_specs=[unit(HD, tokens), whole, whole],
        out_shape=[
            jax.ShapeDtypeStruct((3, HD, tokens // 2), F32),
            jax.ShapeDtypeStruct((3, HD, tokens), F32),
            jax.ShapeDtypeStruct((3, HD, tokens), F32),
        ],
        scratch_shapes=[
            pltpu.VMEM((HD, tokens // 2), BF16),
            pltpu.VMEM((HD, tokens // 2), BF16),
            pltpu.VMEM((1, tokens // 2), F32),
            pltpu.VMEM((1, tokens // 2), F32),
            pltpu.VMEM((HD, tokens), BF16),
            pltpu.VMEM((HD, tokens), BF16),
        ],
        compiler_params=pltpu.CompilerParams(vmem_limit_bytes=VMEM_LIMIT),
        name="cross_backward",
    )(
        late, heads, grads, levels, inners, q_sent, g_sent, stats_sent, stats_sent,
        heads, heads, pair_sent, pair_sent,
    )


def combine(late, own, here, dq_got, pair_got):
    dq_own, dk_own, dv_own = own
    dq_here, dk_here, dv_here = here
    tokens = dq_own.shape[2]
    half = tokens // 2

    def kernel(late_ref, dqo, dko, dvo, dqh, dkh, dvh, dqg, pg, out_ref):
        is_late = late_ref[0] == 1
        for h in range(HL):
            for s in range(2):
                number = 2 * h + s
                other = dqg[number].astype(F32) if number < 3 else dqh[number - 3]
                span = slice(s * half, (s + 1) * half)
                out_ref[h, :, span] = (dqo[h, :, span] + jnp.where(is_late, other, 0.0)).astype(BF16)
        for part, (mine, cross) in enumerate(((dko, dkh), (dvo, dvh))):
            first = 2 * part
            extra = (
                cross[0] + cross[1],
                cross[2] + pg[first].astype(F32),
                pg[first + 1].astype(F32),
            )
            for h in range(HL):
                total = mine[h] + jnp.where(is_late, 0.0, extra[h])
                out_ref[(1 + part) * HL + h] = total.astype(BF16)

    vmem = pl.BlockSpec(memory_space=pltpu.VMEM)
    return pl.pallas_call(
        kernel,
        in_specs=[SCALAR] + [vmem] * 8,
        out_specs=vmem,
        out_shape=jax.ShapeDtypeStruct((3 * HL, HD, tokens), BF16),
        compiler_params=pltpu.CompilerParams(vmem_limit_bytes=VMEM_LIMIT),
        name="combine",
    )(late, dq_own, dk_own, dv_own, dq_here, dk_here, dv_here, dq_got, pair_got)


def leave(place, pieces, normed, heads_grad, weight):
    length, width = pieces[0].shape
    cols = heads_grad.shape[0]

    def kernel(place_ref, x0, x1, x2, x3, xn_ref, g_ref, w_ref, a0, a1, a2, a3, dw_ref, gain_ref, shift_ref, bias_ref, xs, dw):
        step = pl.program_id(0)
        for number, ref in enumerate((x0, x1, x2, x3)):

            @pl.when(step == number)
            def _():
                xs[...] = ref[...].astype(F32)

        @pl.when(step == 0)
        def _():
            dw[...] = jnp.zeros_like(dw)
            gain_ref[...] = jnp.zeros_like(gain_ref)
            shift_ref[...] = jnp.zeros_like(shift_ref)
            bias_ref[...] = jnp.zeros_like(bias_ref)

        grad = g_ref[...]
        back = dg(grad, w_ref[:, :cols], 0, 1)
        normal, _ = normalize(xs[...])
        gain_ref[...] += jnp.sum(back * normal, axis=0, keepdims=True)
        shift_ref[...] += jnp.sum(back, axis=0, keepdims=True)
        bias_ref[...] += jnp.sum(grad.astype(F32), axis=1, keepdims=True)
        dw[...] += dg(xn_ref[...], grad, 0, 1)
        for number, ref in enumerate((a0, a1, a2, a3)):

            @pl.when(step == number)
            def _():
                ref[...] = back.astype(ref.dtype)

        @pl.when(step == QUAD - 1)
        def _():
            dw_ref[...] = dw[...].astype(BF16)

    whole = lambda shape: pl.BlockSpec(shape, lambda p, c: (0, 0))
    block = (length, width)
    return pl.pallas_call(
        kernel,
        grid_spec=pltpu.PrefetchScalarGridSpec(
            num_scalar_prefetch=1,
            grid=(QUAD,),
            in_specs=[whole(block)] * 4
            + [
                pl.BlockSpec(block, lambda p, c: (c[0] ^ p, 0)),
                pl.BlockSpec((cols, length), lambda p, c: (0, c[0] ^ p)),
                whole(weight.shape),
            ],
            out_specs=[whole(block)] * 4
            + [whole((width, cols)), whole((1, width)), whole((1, width)), whole((cols, 1))],
            scratch_shapes=[pltpu.VMEM(block, F32), pltpu.VMEM((width, cols), F32)],
        ),
        out_shape=[
            jax.ShapeDtypeStruct(block, F32),
            *[jax.ShapeDtypeStruct(block, BF16)] * 3,
            jax.ShapeDtypeStruct((width, cols), BF16),
            jax.ShapeDtypeStruct((1, width), F32),
            jax.ShapeDtypeStruct((1, width), F32),
            jax.ShapeDtypeStruct((cols, 1), F32),
        ],
        compiler_params=pltpu.CompilerParams(vmem_limit_bytes=VMEM_LIMIT),
        name="leave",
    )(place, *pieces, normed, heads_grad, weight)


def quad_columns(rows, width):
    count = rows.shape[0]
    parts = rows.reshape(count, 3, QUAD, width // QUAD)
    return parts.transpose(2, 0, 1, 3).reshape(QUAD, count, 3 * width // QUAD)


def from_quad_columns(parts, width):
    count = parts.shape[1]
    split = parts.reshape(QUAD, count, 3, width // QUAD).transpose(1, 2, 0, 3)
    return split.reshape(count, 3 * width)


def fetch_entry(place, quad, qkv, vectors, counts):
    shards, reps = lax.axis_size("shard"), lax.axis_size("rep")
    quads = shards // QUAD
    width = qkv.shape[1] // 3
    cols = 3 * width // QUAD
    sizes = [v.shape[0] for v in vectors]
    if reps != 2 or quads & (quads - 1):
        mine = lax.dynamic_index_in_dim(
            quad_columns(lax.all_gather(qkv, "shard", axis=0, tiled=True), width), place, 0, False
        )
        whole = [lax.all_gather(v, "shard", axis=0, tiled=True) for v in vectors]
        count = lax.psum(jnp.sum(counts), ("rep", "shard"))
        return jnp.pad(mine, ((0, 0), (0, 64))), whole, count
    rep = lax.axis_index("rep")
    rows = qkv.shape[0] // 2
    packed = jnp.concatenate([*vectors, counts.astype(BF16)])
    used = sum(sizes)
    packed = jnp.pad(packed, (0, rows * 64 - packed.shape[0])).reshape(rows, 64)
    half = quad_columns(lax.dynamic_slice_in_dim(qkv, rep * rows, rows, 0), width)
    payload = jnp.concatenate([half, jnp.broadcast_to(packed, (QUAD, rows, 64))], axis=2)
    take = lambda index: lax.dynamic_index_in_dim(payload, index, 0, False)
    pieces = [take(place)] + [trade(take(place ^ j), j) for j in range(1, QUAD)]
    held = in_order(pieces, place)[None]
    for bit in reversed(range(quads.bit_length() - 1)):
        other = trade(held, QUAD << bit)
        held = pair_in_order((quad >> bit) & 1, held, other)
        held = held.transpose(1, 0, 2, 3, 4).reshape(-1, QUAD, rows, cols + 64)
    both = pair_in_order(rep, held, trade_rep(held))
    both = both.reshape(2, shards, rows, cols + 64)
    weight = both.transpose(1, 0, 2, 3).reshape(shards * 2 * rows, cols + 64)
    flat = both[0, :, :, cols:].reshape(shards, rows * 64)
    whole, start = [], 0
    for size in sizes:
        whole.append(flat[:, start : start + size].reshape(-1))
        start += size
    counted = both[:, :, :, cols:].reshape(2 * shards, rows * 64)[:, used : used + counts.shape[0]]
    return weight, whole, jnp.sum(counted.astype(F32))


def sum_everywhere(value):
    shards, reps = lax.axis_size("shard"), lax.axis_size("rep")
    if reps != 2 or shards & (shards - 1):
        return lax.psum(value, ("rep", "shard"))
    value = value + trade_rep(value)
    for bit in range(shards.bit_length() - 1):
        value = value + trade(value, 1 << bit)
    return value


def reduce_entry(place, quad, weight_grad, vectors):
    shards, reps = lax.axis_size("shard"), lax.axis_size("rep")
    quads = shards // QUAD
    width, cols = weight_grad.shape
    sizes = [v.shape[0] // shards for v in vectors]
    spread = jnp.concatenate([v.reshape(shards, -1) for v in vectors], axis=1).astype(BF16)
    if reps != 2 or quads & (quads - 1):
        laid = jnp.zeros((QUAD, width, cols), BF16)
        laid = from_quad_columns(lax.dynamic_update_index_in_dim(laid, weight_grad, place, 0), width)
        grad = lax.psum_scatter(laid, "shard", scatter_dimension=0, tiled=True)
        grad = lax.psum(grad, "rep").astype(F32)
        total = lax.psum_scatter(spread, "shard", scatter_dimension=0, tiled=True)
        total = lax.psum(total, "rep").astype(F32).reshape(-1)
    else:
        rep = lax.axis_index("rep")
        rows = width // shards // 2
        slots = jnp.pad(spread, ((0, 0), (0, rows * 64 - spread.shape[1]))).reshape(shards, 1, rows, 64)
        slots = jnp.broadcast_to(slots, (shards, 2, rows, 64))
        payload = jnp.concatenate([weight_grad.reshape(shards, 2, rows, cols), slots], axis=3)

        def halve(array, bit, send):
            keep = jnp.where(bit == 1, array[:, 1], array[:, 0])
            give = jnp.where(bit == 1, array[:, 0], array[:, 1])
            return (keep.astype(F32) + send(give).astype(F32)).astype(BF16)

        held = halve(payload, rep, trade_rep)
        for bit in range(quads.bit_length() - 1):
            held = held.reshape(-1, 2, QUAD * rows, cols + 64)
            held = halve(held, (quad >> bit) & 1, partial(trade, mask=QUAD << bit))
        held = held.reshape(QUAD, rows, cols + 64)
        take = lambda index: lax.dynamic_index_in_dim(held, index, 0, False)
        pieces = [take(place)] + [trade(take(place ^ j), j) for j in range(1, QUAD)]
        ordered = in_order(pieces, place)
        grad = from_quad_columns(ordered[:, :, :cols], width)
        grad = pair_in_order(rep, grad, trade_rep(grad)).reshape(2 * rows, 3 * width).astype(F32)
        total = jnp.sum(ordered[:, :, cols:].astype(F32), axis=0).reshape(-1)
    whole, start = [], 0
    for size in sizes:
        whole.append(total[start : start + size])
        start += size
    return grad, whole


def rep_part(array):
    reps = lax.axis_size("rep")
    rows = array.shape[0] // reps
    return lax.dynamic_slice_in_dim(array, lax.axis_index("rep") * rows, rows, 0)


def fetch_rest(wide, outward, narrow):
    shards, reps = lax.axis_size("shard"), lax.axis_size("rep")
    wide, outward, narrow = rep_part(wide), rep_part(outward), rep_part(narrow)
    rows, ff = wide.shape
    width = outward.shape[1]
    times = narrow.shape[0] // rows
    folded = narrow.reshape(times, rows, width).transpose(1, 0, 2).reshape(rows, times * width)
    packed = jnp.concatenate([wide, outward, folded], axis=1)
    full = lax.all_gather(packed, ("shard", "rep"), axis=0, tiled=True)
    unfolded = full[:, ff + width :].reshape(shards * reps, rows, times, width).transpose(0, 2, 1, 3)
    return full[:, :ff], full[:, ff : ff + width], unfolded.reshape(ff, width)


def reduce_rest(wide, outward, narrow):
    shards, reps = lax.axis_size("shard"), lax.axis_size("rep")
    width, ff = wide.shape
    devices = shards * reps
    rows = width // devices
    times = ff // width
    folded = narrow.reshape(devices, times, rows, width).transpose(0, 2, 1, 3).reshape(width, times * width)
    packed = jnp.concatenate([wide, outward, folded], axis=1)
    part = lax.psum_scatter(packed, ("shard", "rep"), scatter_dimension=0, tiled=True)
    if reps == 2:
        full = pair_in_order(lax.axis_index("rep"), part, trade_rep(part))
    else:
        full = lax.all_gather(part, "rep", axis=0, tiled=False)
    full = full.astype(F32)
    unfolded = full[:, :, ff + width :].reshape(reps, rows, times, width).transpose(0, 2, 1, 3)
    return (
        full[:, :, :ff].reshape(reps * rows, ff),
        full[:, :, ff : ff + width].reshape(reps * rows, width),
        unfolded.reshape(reps * rows * times, width),
    )


def local(
    incoming_tokens,
    mentor_outputs,
    counting_flags,
    opening_scale_factor,
    opening_offset_vector,
    query_key_value_map,
    asking_offset,
    content_offset,
    attend_result_map,
    attend_result_offset,
    latter_scale_factor,
    latter_offset_vector,
    widen_projection,
    hidden_offset,
    narrow_projection,
    narrow_offset,
):
    shards = lax.axis_size("shard")
    length, width = incoming_tokens.shape
    tokens = QUAD * length
    head_rows = HL * HD
    me = lax.axis_index("shard")
    place, quad = me % QUAD, me // QUAD
    place_arg = place.reshape(1).astype(jnp.int32)
    late = (quad % 2 == 0).reshape(1).astype(jnp.int32)
    groups = [[QUAD * g + i for i in range(QUAD)] for g in range(shards // QUAD)]

    pieces = [incoming_tokens] + [trade(incoming_tokens, j) for j in range(1, QUAD)]
    flags = counting_flags.astype(F32)
    counts = jnp.sum(flags.reshape(-1, min(256, length)), axis=1)
    entry_weight, vectors, count_all = fetch_entry(
        place,
        quad,
        query_key_value_map,
        [
            opening_scale_factor,
            opening_offset_vector,
            asking_offset,
            content_offset,
            attend_result_offset,
            latter_scale_factor,
            latter_offset_vector,
            narrow_offset,
            hidden_offset,
        ],
        counts,
    )
    pregain, preshift, querybias, valuebias, outbias, midgain, midshift, shrinkbias, expandbias = (
        v.astype(F32) for v in vectors
    )
    wide_full, outward_full, narrow_full = fetch_rest(
        widen_projection, attend_result_map, narrow_projection
    )

    own_rows = lambda v: lax.dynamic_slice_in_dim(v, place * head_rows, head_rows, 0)
    bias = jnp.concatenate([own_rows(querybias), jnp.zeros((head_rows,), F32), own_rows(valuebias)])
    normed_one, projected = enter(
        place_arg, pieces, entry_weight, bias[:, None], pregain[None], preshift[None]
    )
    heads = projected.reshape(3 * HL, HD, tokens)
    half = tokens // 2

    def sent_units(array):
        return jnp.stack([array[0, :, :half], array[0, :, half:], array[1, :, :half]])

    q_sent = to_early(sent_units(heads))
    pair_sent = to_late(jnp.concatenate([heads[HL + 1 : 2 * HL], heads[2 * HL + 1 :]]))
    o_own, l_own = own_forward(heads)
    o_here, l_here = cross_forward(late, heads, q_sent, pair_sent)
    o_got, l_got = to_late(o_here.astype(BF16)), to_late(l_here)
    mixed_wide, mixed_low, levels = merge(late, o_own, l_own, o_got, l_got, o_here, l_here)
    mixed = lax.all_to_all(
        mixed_low.reshape(head_rows, tokens), "shard", 1, 0, axis_index_groups=groups, tiled=True
    )

    inputs = incoming_tokens.astype(F32)
    middle = inputs + (dg(mixed, outward_full, 0, 0) + outbias)
    normal_two, factor_two = normalize(middle)
    normed_two = (normal_two * midgain + midshift).astype(BF16)
    pre_act = dg(normed_two, wide_full, 1, 0) + expandbias
    activation, gelu_back = jax.vjp(partial(jax.nn.gelu, approximate=True), pre_act)
    hidden = activation.astype(BF16)
    output = middle + (dg(hidden, narrow_full, 1, 0) + shrinkbias)
    weight_rows = flags[:, None]
    mismatch = output - mentor_outputs.astype(F32)
    squares = jnp.sum(weight_rows * mismatch * mismatch)
    distill_loss = sum_everywhere(squares.reshape(1))[0] / count_all
    token_total = length * lax.axis_size("rep") * shards
    output_grad = 2.0 * token_total / count_all * weight_rows * mismatch

    branch_two_grad = output_grad.astype(BF16)
    shrinkbias_grad = column_sums(branch_two_grad)
    shrink_grad = dg(hidden, branch_two_grad, 0, 0)
    hidden_grad = dg(branch_two_grad, narrow_full, 1, 1)
    pre_grad = gelu_back(hidden_grad)[0].astype(BF16)
    expandbias_grad = column_sums(pre_grad)
    expand_grad = dg(normed_two, pre_grad, 0, 0)
    normed_two_grad = dg(pre_grad, wide_full, 1, 1)
    midgain_grad = jnp.sum(normed_two_grad * normal_two, axis=0)
    midshift_grad = jnp.sum(normed_two_grad, axis=0)
    scaled = normed_two_grad * midgain
    middle_grad = output_grad + factor_two * (
        scaled
        - jnp.mean(scaled, axis=-1, keepdims=True)
        - normal_two * jnp.mean(scaled * normal_two, axis=-1, keepdims=True)
    )
    branch_grad = middle_grad.astype(BF16)
    outbias_grad = column_sums(branch_grad)
    outward_grad = dg(mixed, branch_grad, 1, 0)
    rest = reduce_rest(expand_grad.astype(BF16), outward_grad.astype(BF16), shrink_grad.astype(BF16))
    mixed_grad = dg(outward_full, branch_grad, 1, 1).astype(BF16)
    grads = lax.all_to_all(mixed_grad, "shard", 0, 1, axis_index_groups=groups, tiled=True)
    grads = grads.reshape(HL, HD, tokens)

    inners = jnp.sum(grads.astype(F32) * mixed_wide, axis=1, keepdims=True)
    g_sent = to_early(sent_units(grads))
    stats_sent = to_early(jnp.concatenate([sent_units(levels), sent_units(inners)]))
    here = cross_backward(late, heads, grads, levels, inners, q_sent, pair_sent, g_sent, stats_sent)
    dq_here, dk_here, dv_here = here
    dq_got = to_late(dq_here.astype(BF16))
    pair_got = to_early(
        jnp.stack([dk_here[0], dk_here[1] + dk_here[2], dv_here[0], dv_here[1] + dv_here[2]]).astype(BF16)
    )
    own = own_backward(heads, grads, levels, inners)
    heads_grad = combine(late, own, here, dq_got, pair_got).reshape(3 * head_rows, tokens)

    *shares, inward_part, pregain_part, preshift_part, bias_part = leave(
        place_arg, pieces, normed_one, heads_grad, entry_weight
    )
    normed_one_grad = shares[0]
    for j in range(1, QUAD):
        normed_one_grad = normed_one_grad + trade(shares[j], j).astype(F32)

    spread = lambda v: lax.dynamic_update_slice_in_dim(
        jnp.zeros((width,), F32), v, place * head_rows, 0
    )
    inward_grad, vector_grads = reduce_entry(
        place,
        quad,
        inward_part,
        [
            pregain_part.reshape(-1),
            preshift_part.reshape(-1),
            spread(bias_part[:head_rows, 0]),
            spread(bias_part[2 * head_rows :, 0]),
            outbias_grad,
            midgain_grad,
            midshift_grad,
            shrinkbias_grad,
            expandbias_grad,
        ],
    )
    normal_one, factor_one = normalize(inputs)
    scaled_one = normed_one_grad * pregain
    input_part = factor_one * (
        scaled_one
        - jnp.mean(scaled_one, axis=-1, keepdims=True)
        - normal_one * jnp.mean(scaled_one * normal_one, axis=-1, keepdims=True)
    )
    states_gradient = (middle_grad + input_part).astype(BF16)
    return (
        distill_loss,
        output.astype(BF16),
        states_gradient,
        vector_grads[0],
        vector_grads[1],
        inward_grad,
        vector_grads[2],
        vector_grads[3],
        rest[1],
        vector_grads[4],
        vector_grads[5],
        vector_grads[6],
        rest[0],
        vector_grads[8],
        rest[2],
        vector_grads[7],
    )


def solution(mesh):
    rows, vector, matrix = P(("rep", "shard"), None), P("shard"), P("shard", None)
    return jax.shard_map(
        local,
        mesh=mesh,
        in_specs=(
            rows,
            rows,
            P(("rep", "shard")),
            vector,
            vector,
            matrix,
            vector,
            vector,
            matrix,
            vector,
            vector,
            vector,
            matrix,
            vector,
            matrix,
            vector,
        ),
        out_specs=(
            P(),
            rows,
            rows,
            vector,
            vector,
            matrix,
            vector,
            vector,
            matrix,
            vector,
            vector,
            vector,
            matrix,
            vector,
            matrix,
            vector,
        ),
        check_vma=False,
    )
```

```python
from functools import partial

import jax
import jax.numpy as jnp
from jax import lax
from jax.experimental import pallas as pl
from jax.experimental.pallas import tpu as pltpu
from jax.sharding import PartitionSpec as P

H = 12
HD = 64
SPLIT = 8
BLOCK = 256
QUAD = SPLIT // 2
HL = H // QUAD
EPSILON = 1e-05
F32 = jnp.float32
BF16 = jnp.bfloat16
VMEM_LIMIT = 56 * 1024 * 1024


def dg(left, right, left_dim, right_dim):
    return lax.dot_general(
        left, right, (((left_dim,), (right_dim,)), ((), ())), preferred_element_type=F32
    )


def trade(array, mask):
    size = lax.axis_size("shard")
    return lax.ppermute(array, "shard", [(i, i ^ mask) for i in range(size)])


def trade_rep(array):
    return lax.ppermute(array, "rep", [(0, 1), (1, 0)])


def to_late(array):
    size = lax.axis_size("shard")
    pairs = [(i, (i + QUAD) % size) for i in range(size) if (i // QUAD) % 2 == 1]
    return lax.ppermute(array, "shard", pairs)


def to_early(array):
    size = lax.axis_size("shard")
    pairs = [(i, (i - QUAD) % size) for i in range(size) if (i // QUAD) % 2 == 0]
    return lax.ppermute(array, "shard", pairs)


def in_order(pieces, place):
    step = 1
    while step < len(pieces):
        pieces = [
            jnp.where(place & step != 0, pieces[j ^ step], pieces[j]) for j in range(len(pieces))
        ]
        step *= 2
    return jnp.stack(pieces)


def together(*values):
    return lax.optimization_barrier(values)


def pair_in_order(bit, own, other):
    return jnp.where(bit == 1, jnp.stack([other, own]), jnp.stack([own, other]))


def normalize(values):
    center = values - jnp.mean(values, axis=-1, keepdims=True)
    spread = jnp.mean(center * center, axis=-1, keepdims=True)
    factor = lax.rsqrt(spread + EPSILON)
    return (center * factor, factor)


def column_sums(values):
    return jnp.sum(values.astype(F32), axis=0)


def params():
    return pltpu.CompilerParams(vmem_limit_bytes=VMEM_LIMIT)


SHORT = pl.CostEstimate(flops=1, transcendentals=0, bytes_accessed=1)


def load_tokens(step, refs, out):
    x_ref, *halves = refs
    half = halves[0].shape[0]
    low, high = slice(0, half), slice(half, 2 * half)
    sources = [(x_ref.at[low], x_ref.at[high]), *zip(halves[0::2], halves[1::2])]
    for number, (top, bottom) in enumerate(sources):

        @pl.when(step == number)
        def _():
            out[low] = top[...].astype(F32)
            out[high] = bottom[...].astype(F32)


def enter(place, pieces, weight, bias, gain, shift):
    length, width = pieces[0].shape
    cols = 3 * HL * HD
    tokens = QUAD * length

    def kernel(
        place_ref, x0, x1, x2, x3, x4, x5, x6, w_ref, bias_ref, gain_ref, shift_ref,
        xn_ref, pt_ref, q_ref, pair_ref, xs, wt,
    ):
        step = pl.program_id(0)
        block = place_ref[0] ^ step

        @pl.when(step == 0)
        def _():
            wt[...] = w_ref[:, :cols].T

        load_tokens(step, (x0, x1, x2, x3, x4, x5, x6), xs)
        normal, _ = normalize(xs[...])
        normed = (normal * gain_ref[...] + shift_ref[...]).astype(BF16)
        xn_ref[...] = normed
        out = (dg(wt[...], normed, 1, 1) + bias_ref[...]).astype(BF16)
        head_rows = HL * HD
        queries = (out[:head_rows].astype(F32) * HD ** (-0.5)).astype(BF16)
        pt_ref[:head_rows] = queries
        pt_ref[head_rows:] = out[head_rows:]
        side = block // 2
        span = pl.ds(pl.multiple_of((block % 2) * length, length), length)
        q_ref[side, :, span] = queries[:HD]

        @pl.when(side == 0)
        def _():
            q_ref[2, :, span] = queries[HD : 2 * HD]

        span = pl.ds(pl.multiple_of(block * length, length), length)
        for number, head in enumerate((HL + 1, HL + 2, 2 * HL + 1, 2 * HL + 2)):
            pair_ref[number, :, span] = out[head * HD : (head + 1) * HD]

    whole = lambda array: pl.BlockSpec(array.shape, lambda p, c: (0,) * len(array.shape))
    q_shape = jax.ShapeDtypeStruct((3, HD, tokens // 2), BF16)
    pair_shape = jax.ShapeDtypeStruct((4, HD, tokens), BF16)
    return pl.pallas_call(
        kernel,
        grid_spec=pltpu.PrefetchScalarGridSpec(
            num_scalar_prefetch=1,
            grid=(QUAD,),
            in_specs=[whole(a) for a in (*pieces, weight, bias, gain, shift)],
            out_specs=[
                pl.BlockSpec((length, width), lambda p, c: (c[0] ^ p, 0)),
                pl.BlockSpec((cols, length), lambda p, c: (0, c[0] ^ p)),
                whole(q_shape),
                whole(pair_shape),
            ],
            scratch_shapes=[pltpu.VMEM((length, width), F32), pltpu.VMEM((cols, width), BF16)],
        ),
        out_shape=[
            jax.ShapeDtypeStruct((tokens, width), BF16),
            jax.ShapeDtypeStruct((cols, tokens), BF16),
            q_shape,
            pair_shape,
        ],
        compiler_params=params(),
        cost_estimate=SHORT,
        name="enter",
    )(place, *pieces, weight, bias, gain, shift)


def softmax_blocks(q, keys, values, masked):
    following = dg(keys[0], q, 0, 0)
    for number, value in enumerate(values):
        scores = following
        if number + 1 < len(keys):
            following = dg(keys[number + 1], q, 0, 0)
        if masked and number == 0:
            row = lax.broadcasted_iota(jnp.int32, scores.shape, 0) // BLOCK
            col = lax.broadcasted_iota(jnp.int32, scores.shape, 1) // BLOCK
            scores = jnp.where(row <= col, scores, -1e30)
        top = jnp.max(scores, axis=0, keepdims=True)
        if number == 0:
            peak = top
            probs = jnp.exp(scores - peak)
            mass = jnp.sum(probs, axis=0, keepdims=True)
            total = dg(value, probs.astype(BF16), 1, 0)
        else:
            higher = jnp.maximum(peak, top)
            fade = jnp.exp(peak - higher)
            probs = jnp.exp(scores - higher)
            mass = mass * fade + jnp.sum(probs, axis=0, keepdims=True)
            total = total * fade + dg(value, probs.astype(BF16), 1, 0)
            peak = higher
    return total / mass, peak + jnp.log(mass)


WIDE = 2 * BLOCK


def own_forward(heads):
    tokens = heads.shape[2]

    def kernel(q_ref, k_ref, v_ref, o_ref, l_ref):
        for block in range(tokens // WIDE):
            order = [block, *range(block)]
            spans = [slice(i * WIDE, (i + 1) * WIDE) for i in order]
            out, level = softmax_blocks(
                q_ref[0, :, spans[0]],
                [k_ref[0, :, span] for span in spans],
                [v_ref[0, :, span] for span in spans],
                True,
            )
            o_ref[0, :, spans[0]] = out
            l_ref[0, :, spans[0]] = level

    spec = lambda first: pl.BlockSpec((1, HD, tokens), lambda h: (h + first, 0, 0))
    return pl.pallas_call(
        kernel,
        grid=(HL,),
        in_specs=[spec(0), spec(HL), spec(2 * HL)],
        out_specs=[spec(0), pl.BlockSpec((1, 1, tokens), lambda h: (h, 0, 0))],
        out_shape=[
            jax.ShapeDtypeStruct((HL, HD, tokens), F32),
            jax.ShapeDtypeStruct((HL, 1, tokens), F32),
        ],
        compiler_params=params(),
        cost_estimate=SHORT,
        name="own_forward",
    )(heads, heads, heads)


def late_unit(rows, tokens):
    return pl.BlockSpec((1, rows, tokens // 2), lambda u: ((3 + u) // 2, 0, (3 + u) % 2))


def unit(rows, tokens):
    return pl.BlockSpec((1, rows, tokens // 2), lambda u: (u, 0, 0))


def pair_specs(tokens):
    spec = lambda index: pl.BlockSpec((1, HD, tokens), index)
    return [
        spec(lambda u: (HL + u // 2, 0, 0)),
        spec(lambda u: (2 * HL + u // 2, 0, 0)),
        spec(lambda u: ((u + 1) // 2, 0, 0)),
        spec(lambda u: (2 + (u + 1) // 2, 0, 0)),
    ]


SCALAR = pl.BlockSpec(memory_space=pltpu.SMEM)
EXTRA = 16


def put_wide(ref, lead, row, cols, value):
    high = value.astype(BF16)
    ref[(*lead, slice(row, row + 1), cols)] = high
    ref[(*lead, slice(row + 1, row + 2), cols)] = (value - high.astype(F32)).astype(BF16)


def get_wide(ref, lead, row, cols):
    high = ref[(*lead, slice(row, row + 1), cols)].astype(F32)
    return high + ref[(*lead, slice(row + 1, row + 2), cols)].astype(F32)


def cross_forward(late, heads, q_sent, pair_sent):
    tokens = heads.shape[2]

    def kernel(late_ref, q_own, q_got, k_own, v_own, k_got, v_got, o_ref, low_ref, l_ref, qs, ks, vs):
        @pl.when(late_ref[0] == 1)
        def _():
            qs[...] = q_own[0]
            ks[...] = k_got[0]
            vs[...] = v_got[0]

        @pl.when(late_ref[0] == 0)
        def _():
            qs[...] = q_got[0]
            ks[...] = k_own[0]
            vs[...] = v_own[0]

        spans = [slice(i * WIDE, (i + 1) * WIDE) for i in range(tokens // WIDE)]

        @pl.loop(0, tokens // 2 // WIDE)
        def _(block):
            here = pl.ds(pl.multiple_of(block * WIDE, WIDE), WIDE)
            out, level = softmax_blocks(
                qs[:, here], [ks[:, span] for span in spans], [vs[:, span] for span in spans], False
            )
            o_ref[0, :, here] = out
            low_ref[0, :HD, here] = out.astype(BF16)
            put_wide(low_ref, (0,), HD, here, level)
            l_ref[0, :, here] = level

    return pl.pallas_call(
        kernel,
        grid=(3,),
        in_specs=[SCALAR, late_unit(HD, tokens), unit(HD, tokens), *pair_specs(tokens)],
        out_specs=[unit(HD, tokens), unit(HD + EXTRA, tokens), unit(1, tokens)],
        out_shape=[
            jax.ShapeDtypeStruct((3, HD, tokens // 2), F32),
            jax.ShapeDtypeStruct((3, HD + EXTRA, tokens // 2), BF16),
            jax.ShapeDtypeStruct((3, 1, tokens // 2), F32),
        ],
        scratch_shapes=[
            pltpu.VMEM((HD, tokens // 2), BF16),
            pltpu.VMEM((HD, tokens), BF16),
            pltpu.VMEM((HD, tokens), BF16),
        ],
        compiler_params=params(),
        cost_estimate=SHORT,
        name="cross_forward",
    )(late, heads, q_sent, heads, heads, pair_sent, pair_sent)


def merge(late, o_own, l_own, o_got, o_here, l_here):
    tokens = o_own.shape[2]
    length, half = tokens // QUAD, tokens // 2

    def kernel(late_ref, o_ref, l_ref, og_ref, oh_ref, lh_ref, out_ref, low_ref, total_ref):
        is_late = late_ref[0] == 1
        for h in range(HL):
            for block in range(QUAD):
                side = block // 2
                number = 2 * h + side
                span = slice((block % 2) * length, (block % 2 + 1) * length)
                here = slice(block * length, (block + 1) * length)
                if number < 3:
                    other = og_ref[number, :HD, span].astype(F32)
                    level = get_wide(og_ref, (number,), HD, span)
                else:
                    other, level = oh_ref[number - 3, :, span], lh_ref[number - 3, :, span]
                level = jnp.where(is_late, level, -1e30)
                own_level = l_ref[h, :, here]
                peak = jnp.maximum(own_level, level)
                own_part = jnp.exp(own_level - peak)
                part = jnp.exp(level - peak)
                mass = own_part + part
                out = o_ref[h, :, here] * (own_part / mass) + other * (part / mass)
                out_ref[block, h * HD : (h + 1) * HD] = out
                low_ref[block, h * HD : (h + 1) * HD] = out.astype(BF16)
                total_ref[h, :, here] = peak + jnp.log(mass)

    vmem = pl.BlockSpec(memory_space=pltpu.VMEM)
    return pl.pallas_call(
        kernel,
        in_specs=[SCALAR] + [vmem] * 5,
        out_specs=[vmem] * 3,
        out_shape=[
            jax.ShapeDtypeStruct((QUAD, HL * HD, length), F32),
            jax.ShapeDtypeStruct((QUAD, HL * HD, length), BF16),
            jax.ShapeDtypeStruct(l_own.shape, F32),
        ],
        compiler_params=params(),
        cost_estimate=SHORT,
        name="merge",
    )(late, o_own, l_own, o_got, o_here, l_here)


def prepare(grads, mixed, levels):
    _, _, length = grads.shape
    tokens = QUAD * length

    def kernel(g_ref, o_ref, l_ref, d_ref, gs_ref):
        for h in range(HL):
            rows = slice(h * HD, (h + 1) * HD)
            for block in range(QUAD):
                inner = jnp.sum(g_ref[block, rows].astype(F32) * o_ref[block, rows], axis=0, keepdims=True)
                d_ref[h, :, block * length : (block + 1) * length] = inner
        for number in range(3):
            h, side = number // 2, number % 2
            gs_ref[number, :, :HD] = g_ref[2 * side : 2 * side + 2, h * HD : (h + 1) * HD]
            for part in range(2):
                start = (2 * side + part) * length
                span = slice(start, start + length)
                put_wide(gs_ref, (number, part), HD, slice(None), l_ref[h, :, span])
                put_wide(gs_ref, (number, part), HD + 2, slice(None), d_ref[h, :, span])

    vmem = pl.BlockSpec(memory_space=pltpu.VMEM)
    return pl.pallas_call(
        kernel,
        in_specs=[vmem] * 3,
        out_specs=[vmem] * 2,
        out_shape=[
            jax.ShapeDtypeStruct(levels.shape, F32),
            jax.ShapeDtypeStruct((3, 2, HD + EXTRA, length), BF16),
        ],
        compiler_params=params(),
        cost_estimate=SHORT,
        name="prepare",
    )(grads, mixed, levels)


def grad_block(q, g, k, v, level, inner):
    probs = jnp.exp(dg(k, q, 0, 0) - level)
    score_grad = (probs * (dg(v, g, 0, 0) - inner)).astype(BF16)
    query_grad = dg(k, score_grad, 1, 0) * HD ** (-0.5)
    return query_grad, dg(q, score_grad, 1, 1), dg(g, probs.astype(BF16), 1, 1)


def own_backward(heads, grads, levels, inners, first, count):
    tokens = heads.shape[2]
    length = grads.shape[2]
    half = tokens // 2

    def kernel(q_ref, k_ref, v_ref, g_ref, l_ref, d_ref, dq_ref, dk_ref, dv_ref):
        dk_ref[...] = jnp.zeros_like(dk_ref)
        dv_ref[...] = jnp.zeros_like(dv_ref)

        def rows(start, key_start, key_count):
            aligned = lambda number: pl.multiple_of(number, BLOCK)
            here = pl.ds(aligned(start), BLOCK)
            there = pl.ds(aligned(key_start), key_count)
            dq, dk, dv = grad_block(
                q_ref[0, :, here],
                g_ref[start // length, :, pl.ds(aligned(start % length), BLOCK)],
                k_ref[0, :, there],
                v_ref[0, :, there],
                l_ref[0, :, here],
                d_ref[0, :, here],
            )
            dk_ref[0, :, there] += dk
            dv_ref[0, :, there] += dv
            return here, dq

        @pl.loop(0, 2)
        def _(side):
            for block in range(half // BLOCK):
                here, dq = rows(side * half + block * BLOCK, side * half, (block + 1) * BLOCK)
                dq_ref[0, :, here] = dq

        @pl.loop(0, half // BLOCK)
        def _(block):
            here, dq = rows(half + block * BLOCK, 0, half)
            dq_ref[0, :, here] += dq

    spec = lambda part: pl.BlockSpec((1, HD, tokens), lambda h: (h + part * HL + first, 0, 0))
    row = pl.BlockSpec((1, 1, tokens), lambda h: (h + first, 0, 0))
    out = pl.BlockSpec((1, HD, tokens), lambda h: (h, 0, 0))
    return pl.pallas_call(
        kernel,
        grid=(count,),
        in_specs=[
            spec(0),
            spec(1),
            spec(2),
            pl.BlockSpec((QUAD, HD, length), lambda h: (0, h + first, 0)),
            row,
            row,
        ],
        out_specs=[out] * 3,
        out_shape=[jax.ShapeDtypeStruct((count, HD, tokens), F32)] * 3,
        compiler_params=params(),
        cost_estimate=SHORT,
        name="own_backward",
    )(heads, heads, heads, grads, levels, inners)


def cross_backward(late, heads, grads, levels, inners, q_sent, pair_sent, g_sent):
    tokens = heads.shape[2]
    length = grads.shape[2]

    def kernel(
        late_ref, q_own, g_own, l_own, d_own, q_got, g_got, k_own, v_own, k_got, v_got,
        dq_ref, low_ref, dk_ref, dv_ref, pair_ref, qs, gs, ls, ds, ks, vs,
    ):
        @pl.when(late_ref[0] == 1)
        def _():
            qs[...] = q_own[0]
            gs[...] = g_own[...]
            ls[...] = l_own[0]
            ds[...] = d_own[0]
            ks[...] = k_got[0]
            vs[...] = v_got[0]

        @pl.when(late_ref[0] == 0)
        def _():
            qs[...] = q_got[0]
            gs[...] = g_got[0, :, :HD]
            for part in range(2):
                span = slice(part * length, (part + 1) * length)
                ls[:, span] = get_wide(g_got, (0, part), HD, slice(None))
                ds[:, span] = get_wide(g_got, (0, part), HD + 2, slice(None))
            ks[...] = k_own[0]
            vs[...] = v_own[0]

        number = pl.program_id(0)
        dk_ref[number] = jnp.zeros((HD, tokens), F32)
        dv_ref[number] = jnp.zeros((HD, tokens), F32)

        @pl.loop(0, tokens // 2 // BLOCK)
        def _(block):
            here = pl.ds(pl.multiple_of(block * BLOCK, BLOCK), BLOCK)
            there = pl.ds(pl.multiple_of(block * BLOCK % length, BLOCK), BLOCK)
            dq, dk, dv = grad_block(
                qs[:, here], gs[block * BLOCK // length, :, there], ks[...], vs[...], ls[:, here], ds[:, here]
            )
            dq_ref[0, :, here] = dq
            low_ref[0, :, here] = dq.astype(BF16)
            dk_ref[number] += dk
            dv_ref[number] += dv

        @pl.when(number == 2)
        def _():
            for first, ref in ((0, dk_ref), (2, dv_ref)):
                pair_ref[first] = ref[0].astype(BF16)
                pair_ref[first + 1] = (ref[1] + ref[2]).astype(BF16)

    whole = lambda count: pl.BlockSpec((count, HD, tokens), lambda u: (0, 0, 0))
    return pl.pallas_call(
        kernel,
        grid=(3,),
        in_specs=[
            SCALAR,
            late_unit(HD, tokens),
            pl.BlockSpec((2, HD, length), lambda u: ((3 + u) % 2, (3 + u) // 2, 0)),
            late_unit(1, tokens),
            late_unit(1, tokens),
            unit(HD, tokens),
            pl.BlockSpec((1, 2, HD + EXTRA, length), lambda u: (u, 0, 0, 0)),
            *pair_specs(tokens),
        ],
        out_specs=[unit(HD, tokens), unit(HD, tokens), whole(3), whole(3), whole(4)],
        out_shape=[
            jax.ShapeDtypeStruct((3, HD, tokens // 2), F32),
            jax.ShapeDtypeStruct((3, HD, tokens // 2), BF16),
            jax.ShapeDtypeStruct((3, HD, tokens), F32),
            jax.ShapeDtypeStruct((3, HD, tokens), F32),
            jax.ShapeDtypeStruct((4, HD, tokens), BF16),
        ],
        scratch_shapes=[
            pltpu.VMEM((HD, tokens // 2), BF16),
            pltpu.VMEM((2, HD, length), BF16),
            pltpu.VMEM((1, tokens // 2), F32),
            pltpu.VMEM((1, tokens // 2), F32),
            pltpu.VMEM((HD, tokens), BF16),
            pltpu.VMEM((HD, tokens), BF16),
        ],
        compiler_params=params(),
        cost_estimate=SHORT,
        name="cross_backward",
    )(
        late, heads, grads, levels, inners, q_sent, g_sent,
        heads, heads, pair_sent, pair_sent,
    )


def leave_tokens(place, late, pieces, own, here, dq_got, pair_got, weight):
    length, width = pieces[0].shape
    half = length // 2
    cols = 3 * HL * HD
    dq_here, dk_here, dv_here = here

    def kernel(
        place_ref, late_ref, x0, x1, x2, x3, x4, x5, x6, dq0, dk0, dv0, dq1, dk1, dv1, dqh, dkh, dvh, dqg, pg, w_ref,
        keep, a1, a2, a3, b1, b2, b3, grads, gain_ref, shift_ref, bias_ref, xs, backs,
    ):
        step = pl.program_id(0)
        block = place_ref[0] ^ step
        is_late = late_ref[0] == 1
        load_tokens(step, (x0, x1, x2, x3, x4, x5, x6), xs)

        @pl.when(step == 0)
        def _():
            gain_ref[...] = jnp.zeros_like(gain_ref)
            shift_ref[...] = jnp.zeros_like(shift_ref)
            bias_ref[...] = jnp.zeros_like(bias_ref)

        early_heads = dq0.shape[0]
        head_of = lambda low, high, h: low[h] if h < early_heads else high[h - early_heads]
        side = block // 2
        span = pl.ds(pl.multiple_of((block % 2) * length, length), length)
        others = (
            dqg[side, :, span].astype(F32),
            jnp.where(side == 0, dqg[2, :, span].astype(F32), dqh[0, :, span]),
            dqh[1 + side, :, span],
        )
        for h in range(HL):
            mine = head_of(dq0, dq1, h)
            grads[h * HD : (h + 1) * HD] = (mine + jnp.where(is_late, others[h], 0.0)).astype(BF16)
        for part, (low, high, cross) in enumerate(((dk0, dk1, dkh), (dv0, dv1, dvh))):
            extra = (
                cross[0] + cross[1],
                cross[2] + pg[2 * part].astype(F32),
                pg[2 * part + 1].astype(F32),
            )
            for h in range(HL):
                first = ((1 + part) * HL + h) * HD
                mine = head_of(low, high, h)
                grads[first : first + HD] = (mine + jnp.where(is_late, 0.0, extra[h])).astype(BF16)

        grad = grads[...]
        back = dg(grad, w_ref[:, :cols], 0, 1)
        normal, _ = normalize(xs[...])
        gain_ref[...] += jnp.sum(back * normal, axis=0, keepdims=True)
        shift_ref[...] += jnp.sum(back, axis=0, keepdims=True)
        bias_ref[...] += jnp.sum(grad.astype(F32), axis=1, keepdims=True)
        backs[...] = back

        @pl.when(step == 0)
        def _():
            keep[...] = backs[...]

        for number, (top, bottom) in enumerate(((a1, b1), (a2, b2), (a3, b3)), 1):

            @pl.when(step == number)
            def _():
                top[...] = backs[:half].astype(BF16)
                bottom[...] = backs[half:].astype(BF16)

    whole = lambda array: pl.BlockSpec(array.shape, lambda p, c: (0,) * len(array.shape))
    block_of = lambda count: pl.BlockSpec((count, HD, length), lambda p, c: (0, 0, c[0] ^ p))
    out_shape = [
        jax.ShapeDtypeStruct((length, width), F32),
        *[jax.ShapeDtypeStruct((half, width), BF16)] * 6,
        jax.ShapeDtypeStruct((cols, QUAD * length), BF16),
        jax.ShapeDtypeStruct((1, width), F32),
        jax.ShapeDtypeStruct((1, width), F32),
        jax.ShapeDtypeStruct((cols, 1), F32),
    ]
    out_specs = [whole(o) for o in out_shape]
    out_specs[7] = pl.BlockSpec((cols, length), lambda p, c: (0, c[0] ^ p))
    return pl.pallas_call(
        kernel,
        grid_spec=pltpu.PrefetchScalarGridSpec(
            num_scalar_prefetch=1,
            grid=(QUAD,),
            in_specs=[
                SCALAR,
                *[whole(p) for p in pieces],
                *[block_of(part.shape[0]) for part in own],
                whole(dq_here),
                *[block_of(3)] * 2,
                whole(dq_got),
                block_of(4),
                whole(weight),
            ],
            out_specs=out_specs,
            scratch_shapes=[pltpu.VMEM((length, width), F32), pltpu.VMEM((length, width), F32)],
        ),
        out_shape=out_shape,
        compiler_params=params(),
        cost_estimate=SHORT,
        name="leave_tokens",
    )(place, late, *pieces, *own, dq_here, dk_here, dv_here, dq_got, pair_got, weight)


def leave_weight(normed, grads, length):
    width, cols = normed.shape[1], grads.shape[0]
    steps = normed.shape[0] // length

    def kernel(xn_ref, g_ref, out_ref, total):
        step = pl.program_id(0)
        share = dg(xn_ref[...], g_ref[...], 0, 1)

        @pl.when(step == 0)
        def _():
            total[...] = share

        @pl.when(step > 0)
        def _():
            total[...] += share

        @pl.when(step == steps - 1)
        def _():
            out_ref[...] = total[...].astype(BF16)

    return pl.pallas_call(
        kernel,
        grid=(steps,),
        in_specs=[
            pl.BlockSpec((length, width), lambda i: (i, 0)),
            pl.BlockSpec((cols, length), lambda i: (0, i)),
        ],
        out_specs=pl.BlockSpec((width, cols), lambda i: (0, 0)),
        out_shape=jax.ShapeDtypeStruct((width, cols), BF16),
        scratch_shapes=[pltpu.VMEM((width, cols), F32)],
        compiler_params=params(),
        cost_estimate=SHORT,
        name="leave_weight",
    )(normed, grads)


def unpack(place, rep, held, got):
    quads, rows, cols = held[0].shape
    part = cols // 9
    width = 2 * part

    def kernel(place_ref, rep_ref, *refs):
        ours, theirs, (wide_ref, outward_ref, narrow_ref) = refs[:QUAD], refs[QUAD:-3], refs[-3:]

        def emit(first, second):
            wide_ref[:, 0] = first[:, :, : 4 * width]
            outward_ref[:, 0, :, :part] = first[:, :, 4 * width :]
            outward_ref[:, 0, :, part:] = second[:, :, 4 * width :]
            for i in range(4):
                narrow_ref[:, 0, i] = second[:, :, i * width : (i + 1) * width]

        for j in range(QUAD):
            here = pl.program_id(0) == j
            pl.when(here & (rep_ref[0] == 0))(partial(emit, ours[j], theirs[j]))
            pl.when(here & (rep_ref[0] == 1))(partial(emit, theirs[j], ours[j]))

    group = max(1, quads // 2)

    def source(j):
        last = quads // group - 1
        index = lambda p, q, c: (jnp.where(p < j, 0, jnp.where(p == j, q, last)), 0, 0)
        return pl.BlockSpec((group, rows, cols), index)

    shards = QUAD * quads
    wide, outward, narrow = pl.pallas_call(
        kernel,
        grid_spec=pltpu.PrefetchScalarGridSpec(
            num_scalar_prefetch=1,
            grid=(QUAD, quads // group),
            in_specs=[SCALAR] + [source(j) for j in range(QUAD)] * 2,
            out_specs=[
                pl.BlockSpec((group, 1, rows, 4 * width), lambda p, q, c: (q, c[0] ^ p, 0, 0)),
                pl.BlockSpec((group, 1, rows, width), lambda p, q, c: (q, c[0] ^ p, 0, 0)),
                pl.BlockSpec((group, 1, 4, rows, width), lambda p, q, c: (q, c[0] ^ p, 0, 0, 0)),
            ],
        ),
        out_shape=[
            jax.ShapeDtypeStruct((quads, QUAD, rows, 4 * width), BF16),
            jax.ShapeDtypeStruct((quads, QUAD, rows, width), BF16),
            jax.ShapeDtypeStruct((quads, QUAD, 4, rows, width), BF16),
        ],
        compiler_params=params(),
        cost_estimate=SHORT,
        name="unpack",
    )(place, rep, *held, *got)
    depth = shards * rows
    return (
        wide.reshape(depth, 4 * width),
        outward.reshape(depth, width),
        narrow.reshape(4 * depth, width),
    )


def entry_payload(rep, qkv, vectors, flags):
    depth, width = qkv.shape[0], qkv.shape[1] // 3
    rows = depth // 2
    part = width // QUAD
    chunks = flags.shape[0]

    def kernel(rep_ref, w_ref, *refs):
        *vector_refs, flag_ref, out_ref = refs

        def emit(low):
            for member in range(QUAD):
                for i in range(3):
                    start = i * width + member * part
                    out_ref[member, :, i * part : (i + 1) * part] = w_ref[
                        low : low + rows, start : start + part
                    ]

        pl.when(rep_ref[0] == 0)(partial(emit, 0))
        pl.when(rep_ref[0] == 1)(partial(emit, rows))
        out_ref[:, :, 3 * part :] = jnp.zeros((QUAD, rows, 64), BF16)
        row = 0
        for ref in vector_refs:
            for start in range(0, ref.shape[1], depth):
                for member in range(QUAD):
                    out_ref[member, row : row + 1, 3 * part : 3 * part + depth] = ref[
                        :, start : start + depth
                    ]
                row += 1
        counts = jnp.sum(flag_ref[...].astype(F32), axis=1, keepdims=True).astype(BF16)
        for member in range(QUAD):
            out_ref[member, row : row + chunks, 3 * part : 3 * part + 1] = counts

    vmem = pl.BlockSpec(memory_space=pltpu.VMEM)
    return pl.pallas_call(
        kernel,
        in_specs=[SCALAR] + [vmem] * (len(vectors) + 2),
        out_specs=vmem,
        out_shape=jax.ShapeDtypeStruct((QUAD, rows, 3 * part + 64), BF16),
        cost_estimate=SHORT,
        name="entry_payload",
    )(rep, qkv, *[v[None] for v in vectors], flags)


def rest_grads(first, place, shards, normed, pre_grad, hidden, branch_two, mixed, branch, share=None):
    length, width = normed.shape
    part = width // 2
    rows = width // shards
    quads = shards // QUAD
    steps = 4

    def kernel(first_ref, place_ref, n_ref, p_ref, h_ref, b_ref, m_ref, g_ref, *refs):
        *share_ref, out_ref, nt = refs
        step = pl.program_id(0)

        def store(number, shard, low, count, value):
            slot = ((shard % QUAD) ^ place_ref[0]) * quads + shard // QUAD
            here = pl.ds(pl.multiple_of(slot * rows, rows), rows)
            columns = pl.ds(low, count)
            if share_ref:
                value = value + share_ref[0][here, columns].astype(F32)
            out_ref[here, columns] = value.astype(BF16)

        def outward(low):
            block = dg(m_ref[...], g_ref[:, low : low + part], 1, 0)
            for shard in range(shards):
                store(shard, shard, 4 * width, part, block[shard * rows : (shard + 1) * rows])

        @pl.when(first_ref[0] == 1)
        def _():
            @pl.when(step == 0)
            def _():
                nt[...] = n_ref[...].T
                outward(0)

            block = dg(nt[...], p_ref[...], 1, 0)
            start = pl.multiple_of(step * width, width)
            for shard in range(shards):
                store(shard, shard, start, width, block[shard * rows : (shard + 1) * rows])

        @pl.when(first_ref[0] == 0)
        def _():
            @pl.when(step == 0)
            def _():
                outward(part)

            block = dg(h_ref[...].T, b_ref[...], 1, 0)
            for number in range(width // rows):
                shard = step * (width // (4 * rows)) + number // 4
                store(number, shard, number % 4 * width, width, block[number * rows : (number + 1) * rows])

    whole = lambda array: pl.BlockSpec(array.shape, lambda i: (0,) * len(array.shape))
    chunk = pl.BlockSpec((length, width), lambda i: (0, i))
    out_shape = jax.ShapeDtypeStruct((width, 9 * part), BF16)
    extra = [] if share is None else [share]
    return pl.pallas_call(
        kernel,
        grid=(steps,),
        in_specs=[SCALAR, SCALAR, whole(normed), chunk, chunk, whole(branch_two), whole(mixed), whole(branch)]
        + [whole(array) for array in extra],
        out_specs=whole(out_shape),
        out_shape=out_shape,
        scratch_shapes=[pltpu.VMEM((width, length), BF16)],
        compiler_params=params(),
        cost_estimate=SHORT,
        name="rest_grads",
    )(first, place, normed, pre_grad, hidden, branch_two, mixed, branch, *extra)


def quad_columns(rows, width):
    count = rows.shape[0]
    parts = rows.reshape(count, 3, QUAD, width // QUAD)
    return parts.transpose(2, 0, 1, 3).reshape(QUAD, count, 3 * width // QUAD)


def from_quad_columns(parts, width):
    count = parts.shape[1]
    split = parts.reshape(QUAD, count, 3, width // QUAD).transpose(1, 2, 0, 3)
    return split.reshape(count, 3 * width)


def quads_next(held, quad, bit):
    both = pair_in_order((quad >> bit) & 1, held, trade(held, QUAD << bit))
    return jnp.swapaxes(both, 0, 1).reshape(-1, *held.shape[1:])


def swap_quads(array):
    size = lax.axis_size("shard")
    groups = [[place + QUAD * q for q in range(size // QUAD)] for place in range(QUAD)]
    return lax.all_to_all(array, "shard", 0, 0, axis_index_groups=groups, tiled=True)


def swap_quad(array):
    size = lax.axis_size("shard")
    groups = [[QUAD * q + place for place in range(QUAD)] for q in range(size // QUAD)]
    return lax.all_to_all(array, "shard", 0, 0, axis_index_groups=groups, tiled=True)


def is_power(number):
    return number & (number - 1) == 0


def fetch_entry_plain(place, qkv, vectors, flags):
    width = qkv.shape[1] // 3
    mine = lax.dynamic_index_in_dim(
        quad_columns(lax.all_gather(qkv, "shard", axis=0, tiled=True), width), place, 0, False
    )
    whole = [lax.all_gather(v, "shard", axis=0, tiled=True) for v in vectors]
    count = lax.psum(jnp.sum(flags.astype(F32)), ("rep", "shard"))
    return jnp.pad(mine, ((0, 0), (0, 64))), whole, count


def fetch_entry_last(held, sizes, depth, chunks):
    quads, _, rows, cols = held.shape
    shards = quads * QUAD
    both = pair_in_order(lax.axis_index("rep"), held, trade_rep(held)).reshape(2, shards, rows, cols)
    weight = both.transpose(1, 0, 2, 3).reshape(shards * 2 * rows, cols)
    slots = both[..., cols - 64 :]
    whole, row = [], 0
    for size in sizes:
        count = size // depth
        whole.append(slots[0, :, row : row + count, :depth].reshape(-1))
        row += count
    counted = slots[:, :, row : row + chunks, 0]
    return weight, whole, jnp.sum(counted.astype(F32))


def split_low(values):
    high = lax.reduce_precision(values, 8, 7)
    return jnp.concatenate([high, values - high], axis=-2).astype(BF16)


def joined(slots):
    rows = slots.shape[-2] // 2
    slots = slots.astype(F32)
    return slots[..., :rows, :] + slots[..., rows:, :]


def reduce_entry(place, quad, weight_grad, vectors, squares, second):
    shards, reps = lax.axis_size("shard"), lax.axis_size("rep")
    quads = shards // QUAD
    width, cols = weight_grad.shape
    sizes = [v.shape[0] // shards for v in vectors]
    spread = jnp.concatenate([v.reshape(shards, -1) for v in vectors], axis=1)
    if reps != 2 or not is_power(quads):
        laid = jnp.zeros((QUAD, width, cols), BF16)
        laid = from_quad_columns(lax.dynamic_update_index_in_dim(laid, weight_grad, place, 0), width)
        grad = lax.psum_scatter(laid, "shard", scatter_dimension=0, tiled=True)
        grad = lax.psum(grad, "rep").astype(F32)
        total = lax.psum_scatter(spread.astype(BF16), "shard", scatter_dimension=0, tiled=True)
        total = lax.psum(total, "rep").astype(F32).reshape(-1)
        squares = lax.psum(squares, ("rep", "shard"))
        second = second()
    else:
        rep = lax.axis_index("rep")
        rows = width // shards // 2
        room = rows // 2 * 64
        spread = jnp.concatenate([spread, jnp.broadcast_to(squares, (shards, 1))], axis=1)
        spread = jnp.pad(spread, ((0, 0), (0, room - spread.shape[1])))
        slots = split_low(spread.reshape(shards, 1, rows // 2, 64))
        slots = jnp.broadcast_to(slots, (shards, 2, rows, 64))
        payload = jnp.concatenate([weight_grad.reshape(shards, 2, rows, cols), slots], axis=3)

        def add(arrays):
            total = sum(a[..., :cols].astype(F32) for a in arrays).astype(BF16)
            return jnp.concatenate([total, split_low(sum(joined(a[..., cols:]) for a in arrays))], axis=-1)

        side = lambda number: jnp.where(rep == 1, payload[:, number], payload[:, 1 - number])
        held = add([side(1), trade_rep(side(0))])
        held = swap_quads(held.reshape(quads, QUAD, rows, cols + 64))
        second = second()
        held, second = together(add([held[q] for q in range(quads)]), second)
        ordered = swap_quad(held)
        grad = from_quad_columns(ordered[:, :, :cols], width)
        grad = pair_in_order(rep, grad, trade_rep(grad)).reshape(2 * rows, 3 * width).astype(F32)
        total = jnp.sum(joined(ordered[:, :, cols:]), axis=0).reshape(-1)
        squares = total[sum(sizes)]
    whole, start = [], 0
    for size in sizes:
        whole.append(total[start : start + size])
        start += size
    return grad, whole, squares, second


def rep_part(array):
    reps = lax.axis_size("rep")
    rows = array.shape[0] // reps
    return lax.dynamic_slice_in_dim(array, lax.axis_index("rep") * rows, rows, 0)


def whole_tiles(rows):
    quads = lax.axis_size("shard") // QUAD
    return lax.axis_size("rep") == 2 and is_power(quads) and rows % 16 == 0


def pack_rest(wide, outward, narrow):
    rows = wide.shape[0]
    width = outward.shape[1]
    times = narrow.shape[0] // rows
    first = lax.axis_index("rep") == 0
    part = width // 2
    folded = narrow.reshape(times, rows, width).transpose(1, 0, 2).reshape(rows, times * width)
    return jnp.concatenate(
        [jnp.where(first, wide, folded), jnp.where(first, outward[:, :part], outward[:, part:])], axis=1
    )


def fetch_rest_plain(wide, outward, narrow):
    shards, reps = lax.axis_size("shard"), lax.axis_size("rep")
    wide, outward, narrow = rep_part(wide), rep_part(outward), rep_part(narrow)
    rows, ff = wide.shape
    width = outward.shape[1]
    times = narrow.shape[0] // rows
    folded = narrow.reshape(times, rows, width).transpose(1, 0, 2).reshape(rows, times * width)
    packed = jnp.concatenate([wide, outward, folded], axis=1)
    full = lax.all_gather(packed, ("shard", "rep"), axis=0, tiled=True)
    unfolded = full[:, ff + width :].reshape(shards * reps, rows, times, width).transpose(0, 2, 1, 3)
    return full[:, :ff], full[:, ff : ff + width], unfolded.reshape(ff, width)


def unpack_grads(mine):
    rows, cols = mine.shape
    part = cols // 9
    width, ff = 2 * part, 8 * part
    first, second = pair_in_order(lax.axis_index("rep"), mine, trade_rep(mine)).astype(F32)
    unfolded = second[:, :ff].reshape(rows, 4, width).transpose(1, 0, 2)
    return (
        first[:, :ff],
        jnp.concatenate([first[:, ff:], second[:, ff:]], axis=1),
        unfolded.reshape(rows * 4, width),
    )


def reduce_rest_plain(normed, pre_grad, hidden, branch_two, mixed, branch):
    shards, reps = lax.axis_size("shard"), lax.axis_size("rep")
    width, ff = normed.shape[1], hidden.shape[1]
    narrow = dg(hidden, branch_two, 0, 0).astype(BF16)
    wide = dg(normed, pre_grad, 0, 0).astype(BF16)
    outward = dg(mixed, branch, 1, 0).astype(BF16)
    devices = shards * reps
    rows = width // devices
    times = ff // width
    folded = narrow.reshape(devices, times, rows, width).transpose(0, 2, 1, 3).reshape(width, times * width)
    packed = jnp.concatenate([wide, outward, folded], axis=1)
    part = lax.psum_scatter(packed, ("shard", "rep"), scatter_dimension=0, tiled=True)
    full = lax.all_gather(part, "rep", axis=0, tiled=False).astype(F32)
    unfolded = full[:, :, ff + width :].reshape(reps, rows, times, width).transpose(0, 2, 1, 3)
    return (
        full[:, :, :ff].reshape(reps * rows, ff),
        full[:, :, ff : ff + width].reshape(reps * rows, width),
        unfolded.reshape(reps * rows * times, width),
    )


def local(
    incoming_tokens,
    mentor_outputs,
    counting_flags,
    opening_scale_factor,
    opening_offset_vector,
    query_key_value_map,
    asking_offset,
    content_offset,
    attend_result_map,
    attend_result_offset,
    latter_scale_factor,
    latter_offset_vector,
    widen_projection,
    hidden_offset,
    narrow_projection,
    narrow_offset,
):
    shards = lax.axis_size("shard")
    length, width = incoming_tokens.shape
    tokens = QUAD * length
    head_rows = HL * HD
    me = lax.axis_index("shard")
    place, quad = me % QUAD, me // QUAD
    place_arg = place.reshape(1).astype(jnp.int32)
    late = (quad % 2 == 0).reshape(1).astype(jnp.int32)
    quads = shards // QUAD
    fast = whole_tiles(query_key_value_map.shape[0])
    rep = lax.axis_index("rep")
    one = lambda number: number.reshape(1).astype(jnp.int32)
    flags = counting_flags.astype(F32)
    flag_rows = counting_flags.reshape(-1, min(256, length))
    vectors = [
        opening_scale_factor,
        opening_offset_vector,
        asking_offset,
        content_offset,
        attend_result_offset,
        latter_scale_factor,
        latter_offset_vector,
        narrow_offset,
        hidden_offset,
    ]
    rest_weights = (widen_projection, attend_result_map, narrow_projection)
    half = length // 2
    a, b = incoming_tokens[:half], incoming_tokens[half:]
    a1, b2 = trade(a, 1), trade(b, 2)
    if fast:
        bits = range(quads.bit_length() - 1)[::-1]
        payload = entry_payload(one(rep), query_key_value_map, vectors, flag_rows)
        a, b, a1, b2, payload = together(a, b, a1, b2, payload)
        a2, b1 = trade(a, 2), trade(b, 1)
        held = swap_quad(payload)[None]
        stack = quads_next(pack_rest(*rest_weights)[None], quad, bits[0])
        a1, b2, a2, b1, held, stack = together(a1, b2, a2, b1, held, stack)
        for bit in bits:
            held = quads_next(held, quad, bit)
        sizes, depth = [v.shape[0] for v in vectors], query_key_value_map.shape[0]
        entry_weight, vectors, count_all = fetch_entry_last(held, sizes, depth, flag_rows.shape[0])
        _, stack = together(held, stack)
        for bit in bits[1:]:
            stack = quads_next(stack, quad, bit)
    else:
        entry_weight, vectors, count_all = fetch_entry_plain(place, query_key_value_map, vectors, flag_rows)
        wide_full, outward_full, narrow_full = fetch_rest_plain(*rest_weights)
        a2, b1 = trade(a, 2), trade(b, 1)
    pieces = [incoming_tokens, a1, b1, a2, b2, trade(a1, 2), trade(b2, 1)]
    pregain, preshift, querybias, valuebias, outbias, midgain, midshift, shrinkbias, expandbias = (
        v.astype(F32) for v in vectors
    )
    own_rows = lambda v: lax.dynamic_slice_in_dim(v, place * head_rows, head_rows, 0)
    bias = jnp.concatenate([own_rows(querybias), jnp.zeros((head_rows,), F32), own_rows(valuebias)])
    normed_one, projected, q_send, pair_send = enter(
        place_arg, pieces, entry_weight, bias[:, None], pregain[None], preshift[None]
    )
    heads = projected.reshape(3 * HL, HD, tokens)
    q_sent, pair_sent = to_early(q_send), to_late(pair_send)
    if fast:
        _, stack = together(heads, stack)
        rest_held = [stack] + [trade(stack, j) for j in range(1, QUAD)]
    o_own, l_own = own_forward(heads)
    q_sent, pair_sent, l_own = together(q_sent, pair_sent, l_own)
    o_here, o_low, l_here = cross_forward(late, heads, q_sent, pair_sent)
    o_got = to_late(o_low)
    mixed_wide, mixed_low, levels = merge(late, o_own, l_own, o_got, o_here, l_here)
    mixed = swap_quad(mixed_low).reshape(width, length)
    if fast:
        _, *rest_held = together(mixed_low, *rest_held)
        rest_got = [trade_rep(array) for array in rest_held]
        wide_full, outward_full, narrow_full = unpack(place_arg, one(rep), rest_held, rest_got)

    inputs = incoming_tokens.astype(F32)
    middle = inputs + (dg(mixed, outward_full, 0, 0) + outbias)
    normal_two, factor_two = normalize(middle)
    normed_two = (normal_two * midgain + midshift).astype(BF16)
    pre_act = dg(normed_two, wide_full, 1, 0) + expandbias
    activation, gelu_back = jax.vjp(partial(jax.nn.gelu, approximate=True), pre_act)
    hidden = activation.astype(BF16)
    output = middle + (dg(hidden, narrow_full, 1, 0) + shrinkbias)
    weight_rows = flags[:, None]
    mismatch = output - mentor_outputs.astype(F32)
    squares = jnp.sum(weight_rows * mismatch * mismatch)
    token_total = length * lax.axis_size("rep") * shards
    output_grad = 2.0 * token_total / count_all * weight_rows * mismatch

    branch_two_grad = output_grad.astype(BF16)
    shrinkbias_grad = column_sums(branch_two_grad)
    hidden_grad = dg(branch_two_grad, narrow_full, 1, 1)
    pre_grad = gelu_back(hidden_grad)[0].astype(BF16)
    expandbias_grad = column_sums(pre_grad)
    normed_two_grad = dg(pre_grad, wide_full, 1, 1)
    midgain_grad = jnp.sum(normed_two_grad * normal_two, axis=0)
    midshift_grad = jnp.sum(normed_two_grad, axis=0)
    scaled = normed_two_grad * midgain
    middle_grad = output_grad + factor_two * (
        scaled
        - jnp.mean(scaled, axis=-1, keepdims=True)
        - normal_two * jnp.mean(scaled * normal_two, axis=-1, keepdims=True)
    )
    branch_grad = middle_grad.astype(BF16)
    outbias_grad = column_sums(branch_grad)
    mixed_grad = dg(outward_full, branch_grad, 1, 1).astype(BF16)
    grads = swap_quad(mixed_grad.reshape(QUAD, head_rows, length))
    if fast:
        grads_of = lambda first, normed, other=None: rest_grads(
            one(first), place_arg, shards, normed, pre_grad, hidden, branch_two_grad, mixed, branch_grad, other
        )
        share = grads_of(rep == 1, normed_two)
        grads, share = together(grads, share)
        share = trade_rep(share)
    else:
        rest = reduce_rest_plain(normed_two, pre_grad, hidden, branch_two_grad, mixed, branch_grad)
    inners, g_send = prepare(grads, mixed_wide, levels)
    g_sent = to_early(g_send)
    own_first = own_backward(heads, grads, levels, inners, 0, 1)
    if fast:
        g_sent, share, *own_first = together(g_sent, share, *own_first)
        share = grads_of(rep == 0, normed_two, share)
        g_sent, share = together(g_sent, share)
        share = share.reshape(QUAD, quads, width // shards, -1)
        side = quads // 2
        got_a = trade(jnp.stack([share[1, :side], share[3, :side]]), 1)
        got_b = trade(share[2:, side:], 2)
    dq_here, dq_low, dk_here, dv_here, pair_back = cross_backward(
        late, heads, grads, levels, inners, q_sent, pair_sent, g_sent
    )
    levels, pair_back = together(levels, pair_back)
    dq_got, pair_got = to_late(dq_low), to_early(pair_back)
    if fast:
        last_a = (share[2, :side].astype(F32) + got_a[1].astype(F32)).astype(BF16)
        last_b = (share[1, side:].astype(F32) + got_b[1].astype(F32)).astype(BF16)
        levels, pair_back, last_a, last_b = together(levels, pair_back, last_a, last_b)
        last_a, last_b = trade(last_a, 2), trade(last_b, 1)
    own_last = own_backward(heads, grads, levels, inners, 1, HL - 1)
    own_last = together(*own_last, dq_got, pair_got)
    *own_last, dq_got, pair_got = own_last
    if fast:
        parts = (share[0, :side], got_a[0], last_a), (share[0, side:], got_b[0], last_b)
        share = jnp.concatenate([sum(p.astype(F32) for p in part).astype(BF16) for part in parts])
        dq_last, share = together(own_last[0], share)
        own_last = [dq_last, *own_last[1:]]
        share = swap_quads(share)
    *shares, heads_grad, pregain_part, preshift_part, bias_part = leave_tokens(
        place_arg,
        late,
        pieces,
        [*own_first, *own_last],
        (dq_here, dk_here, dv_here),
        dq_got,
        pair_got,
        entry_weight,
    )
    inward_part = leave_weight(normed_one, heads_grad, length)
    half = length // 2
    keep, a_parts, b_parts = shares[0], shares[1:4], shares[4:7]
    first_a, first_b = trade(a_parts[2], 1), trade(b_parts[2], 2)
    if fast:
        inward_part, share, first_a, first_b = together(inward_part, share, first_a, first_b)
    wide = lambda array: array.astype(F32)

    def second_step():
        return (
            trade(a_parts[0], 1),
            trade(b_parts[1], 2),
            trade((wide(a_parts[1]) + wide(first_a)).astype(BF16), 2),
            trade((wide(b_parts[0]) + wide(first_b)).astype(BF16), 1),
        )

    spread = lambda v: lax.dynamic_update_slice_in_dim(
        jnp.zeros((width,), F32), v, place * head_rows, 0
    )
    inward_grad, vector_grads, squares_all, arrived = reduce_entry(
        place,
        quad,
        inward_part,
        [
            pregain_part.reshape(-1),
            preshift_part.reshape(-1),
            spread(bias_part[:head_rows, 0]),
            spread(bias_part[2 * head_rows :, 0]),
            outbias_grad,
            midgain_grad,
            midshift_grad,
            shrinkbias_grad,
            expandbias_grad,
        ],
        squares,
        second_step,
    )
    normed_one_grad = jnp.concatenate(
        [
            keep[:half] + wide(arrived[0]) + wide(arrived[2]),
            keep[half:] + wide(arrived[1]) + wide(arrived[3]),
        ]
    )
    if fast:
        rest = unpack_grads(jnp.sum(share.astype(F32), axis=0).astype(BF16))
    distill_loss = squares_all / count_all
    normal_one, factor_one = normalize(inputs)
    scaled_one = normed_one_grad * pregain
    input_part = factor_one * (
        scaled_one
        - jnp.mean(scaled_one, axis=-1, keepdims=True)
        - normal_one * jnp.mean(scaled_one * normal_one, axis=-1, keepdims=True)
    )
    states_gradient = (middle_grad + input_part).astype(BF16)
    return (
        distill_loss,
        output.astype(BF16),
        states_gradient,
        vector_grads[0],
        vector_grads[1],
        inward_grad,
        vector_grads[2],
        vector_grads[3],
        rest[1],
        vector_grads[4],
        vector_grads[5],
        vector_grads[6],
        rest[0],
        vector_grads[8],
        rest[2],
        vector_grads[7],
    )


def solution(mesh):
    rows, vector, matrix = P(("rep", "shard"), None), P("shard"), P("shard", None)
    return jax.shard_map(
        local,
        mesh=mesh,
        in_specs=(
            rows,
            rows,
            P(("rep", "shard")),
            vector,
            vector,
            matrix,
            vector,
            vector,
            matrix,
            vector,
            vector,
            vector,
            matrix,
            vector,
            matrix,
            vector,
        ),
        out_specs=(
            P(),
            rows,
            rows,
            vector,
            vector,
            matrix,
            vector,
            vector,
            matrix,
            vector,
            vector,
            vector,
            matrix,
            vector,
            matrix,
            vector,
        ),
        check_vma=False,
    )
```

```python
from functools import partial

import jax
import jax.numpy as jnp
from jax import lax
from jax.experimental import pallas as pl
from jax.experimental.pallas import tpu as pltpu
from jax.sharding import PartitionSpec as P

H = 12
HD = 64
SPLIT = 8
BLOCK = 256
QUAD = SPLIT // 2
HL = H // QUAD
EPSILON = 1e-05
F32 = jnp.float32
BF16 = jnp.bfloat16
VMEM_LIMIT = 56 * 1024 * 1024


def dg(left, right, left_dim, right_dim):
    return lax.dot_general(
        left, right, (((left_dim,), (right_dim,)), ((), ())), preferred_element_type=F32
    )


def trade(array, mask):
    size = lax.axis_size("shard")
    return lax.ppermute(array, "shard", [(i, i ^ mask) for i in range(size)])


def trade_rep(array):
    return lax.ppermute(array, "rep", [(0, 1), (1, 0)])


def to_late(array):
    size = lax.axis_size("shard")
    pairs = [(i, (i + QUAD) % size) for i in range(size) if (i // QUAD) % 2 == 1]
    return lax.ppermute(array, "shard", pairs)


def to_early(array):
    size = lax.axis_size("shard")
    pairs = [(i, (i - QUAD) % size) for i in range(size) if (i // QUAD) % 2 == 0]
    return lax.ppermute(array, "shard", pairs)


def swap_sides(array):
    size = lax.axis_size("shard")
    step = lambda i: QUAD if (i // QUAD) % 2 == 1 else -QUAD
    return lax.ppermute(array, "shard", [(i, (i + step(i)) % size) for i in range(size)])


def in_order(pieces, place):
    step = 1
    while step < len(pieces):
        pieces = [
            jnp.where(place & step != 0, pieces[j ^ step], pieces[j]) for j in range(len(pieces))
        ]
        step *= 2
    return jnp.stack(pieces)


def together(*values):
    return lax.optimization_barrier(values)


def pair_in_order(bit, own, other):
    return jnp.where(bit == 1, jnp.stack([other, own]), jnp.stack([own, other]))


def normalize(values):
    center = values - jnp.mean(values, axis=-1, keepdims=True)
    spread = jnp.mean(center * center, axis=-1, keepdims=True)
    factor = lax.rsqrt(spread + EPSILON)
    return (center * factor, factor)


def column_sums(values):
    return jnp.sum(values.astype(F32), axis=0)


def params():
    return pltpu.CompilerParams(vmem_limit_bytes=VMEM_LIMIT)


SHORT = pl.CostEstimate(flops=1, transcendentals=0, bytes_accessed=1)


def load_tokens(step, refs, out):
    x_ref, a1, b2, a23, b13 = refs
    half = x_ref.shape[0] // 2
    low, high = slice(0, half), slice(half, 2 * half)
    sources = (
        (x_ref.at[low], x_ref.at[high]),
        (a1, b13.at[low]),
        (a23.at[low], b2),
        (a23.at[high], b13.at[high]),
    )
    for number, (top, bottom) in enumerate(sources):

        @pl.when(step == number)
        def _():
            out[low] = top[...].astype(F32)
            out[high] = bottom[...].astype(F32)


def enter(place, late, pieces, weight, bias, gain, shift):
    length, width = pieces[0].shape
    cols = 3 * HL * HD
    tokens = QUAD * length

    def kernel(
        place_ref, late_ref, x0, x1, x2, x3, x4, w_ref, bias_ref, gain_ref, shift_ref,
        n_ref, pt_ref, swap_ref, pair_ref, xs, wt,
    ):
        step = pl.program_id(0)
        block = place_ref[0] ^ step

        @pl.when(step == 0)
        def _():
            wt[...] = w_ref[:, :cols].T

        load_tokens(step, (x0, x1, x2, x3, x4), xs)
        normal, _ = normalize(xs[...])
        normed = (normal * gain_ref[...] + shift_ref[...]).astype(BF16)
        n_ref[...] = normal.astype(BF16)
        out = (dg(wt[...], normed, 1, 1) + bias_ref[...]).astype(BF16)
        head_rows = HL * HD
        queries = (out[:head_rows].astype(F32) * HD ** (-0.5)).astype(BF16)
        pt_ref[:head_rows] = queries
        pt_ref[head_rows:] = out[head_rows:]
        side = block // 2
        span = pl.ds(pl.multiple_of((block % 2) * length, length), length)
        take = lambda number: out[number * HD : (number + 1) * HD]

        @pl.when(late_ref[0] == 1)
        def _():
            swap_ref[side, :, span] = queries[:HD]

            @pl.when(side == 0)
            def _():
                swap_ref[2, :, span] = queries[HD : 2 * HD]
                swap_ref[3, :, span] = jnp.zeros_like(queries[:HD])

        @pl.when(late_ref[0] == 0)
        def _():
            swap_ref[side, :, span] = take(HL + 1)
            swap_ref[2 + side, :, span] = take(2 * HL + 1)

        span = pl.ds(pl.multiple_of(block * length, length), length)
        pair_ref[0, :, span] = take(HL + 2)
        pair_ref[1, :, span] = take(2 * HL + 2)

    whole = lambda array: pl.BlockSpec(array.shape, lambda p, c: (0,) * len(array.shape))
    swap_shape = jax.ShapeDtypeStruct((4, HD, tokens // 2), BF16)
    pair_shape = jax.ShapeDtypeStruct((2, HD, tokens), BF16)
    return pl.pallas_call(
        kernel,
        grid_spec=pltpu.PrefetchScalarGridSpec(
            num_scalar_prefetch=1,
            grid=(QUAD,),
            in_specs=[SCALAR] + [RESIDENT] * (len(pieces) + 4),
            out_specs=[
                pl.BlockSpec((length, width), lambda p, c: (c[0] ^ p, 0)),
                pl.BlockSpec((cols, length), lambda p, c: (0, c[0] ^ p)),
                whole(swap_shape),
                whole(pair_shape),
            ],
            scratch_shapes=[pltpu.VMEM((length, width), F32), pltpu.VMEM((cols, width), BF16)],
        ),
        out_shape=[
            jax.ShapeDtypeStruct((tokens, width), BF16),
            jax.ShapeDtypeStruct((cols, tokens), BF16),
            swap_shape,
            pair_shape,
        ],
        compiler_params=params(),
        cost_estimate=SHORT,
        name="enter",
    )(place, late, *pieces, weight, bias, gain, shift)


def softmax_blocks(q, keys, values, masked):
    following = dg(keys[0], q, 0, 0)
    for number, value in enumerate(values):
        scores = following
        if number + 1 < len(keys):
            following = dg(keys[number + 1], q, 0, 0)
        if masked and number == 0:
            row = lax.broadcasted_iota(jnp.int32, scores.shape, 0) // BLOCK
            col = lax.broadcasted_iota(jnp.int32, scores.shape, 1) // BLOCK
            scores = jnp.where(row <= col, scores, -1e30)
        top = jnp.max(scores, axis=0, keepdims=True)
        if number == 0:
            peak = top
            probs = jnp.exp(scores - peak)
            mass = jnp.sum(probs, axis=0, keepdims=True)
            total = dg(value, probs.astype(BF16), 1, 0)
        else:
            higher = jnp.maximum(peak, top)
            fade = jnp.exp(peak - higher)
            probs = jnp.exp(scores - higher)
            mass = mass * fade + jnp.sum(probs, axis=0, keepdims=True)
            total = total * fade + dg(value, probs.astype(BF16), 1, 0)
            peak = higher
    return total / mass, peak + jnp.log(mass)


WIDE = 2 * BLOCK


def own_forward(heads):
    tokens = heads.shape[2]

    def kernel(q_ref, k_ref, v_ref, o_ref, l_ref):
        for block in range(tokens // WIDE):
            order = [block, *range(block)]
            spans = [slice(i * WIDE, (i + 1) * WIDE) for i in order]
            out, level = softmax_blocks(
                q_ref[0, :, spans[0]],
                [k_ref[0, :, span] for span in spans],
                [v_ref[0, :, span] for span in spans],
                True,
            )
            o_ref[0, :, spans[0]] = out
            l_ref[0, :, spans[0]] = level

    spec = lambda first: pl.BlockSpec((1, HD, tokens), lambda h: (h + first, 0, 0))
    return pl.pallas_call(
        kernel,
        grid=(HL,),
        in_specs=[spec(0), spec(HL), spec(2 * HL)],
        out_specs=[spec(0), pl.BlockSpec((1, 1, tokens), lambda h: (h, 0, 0))],
        out_shape=[
            jax.ShapeDtypeStruct((HL, HD, tokens), F32),
            jax.ShapeDtypeStruct((HL, 1, tokens), F32),
        ],
        compiler_params=params(),
        cost_estimate=SHORT,
        name="own_forward",
    )(heads, heads, heads)


def late_unit(rows, tokens, first=0):
    return pl.BlockSpec(
        (1, rows, tokens // 2), lambda u: ((3 + first + u) // 2, 0, (3 + first + u) % 2)
    )


def unit(rows, tokens, first=0):
    return pl.BlockSpec((1, rows, tokens // 2), lambda u: (first + u, 0, 0))


def own_pair(tokens, first=0):
    spec = lambda part: pl.BlockSpec((1, HD, tokens), lambda u: (part * HL + (first + u) // 2, 0, 0))
    return [spec(1), spec(2)]


def late_pair(number, swapped, pair, ks, vs):
    half = ks.shape[1] // 2

    @pl.when(number == 0)
    def _():
        for side in range(2):
            ks[:, side * half : (side + 1) * half] = swapped[side]
            vs[:, side * half : (side + 1) * half] = swapped[2 + side]

    @pl.when(number > 0)
    def _():
        ks[...] = pair[0]
        vs[...] = pair[1]


SCALAR = pl.BlockSpec(memory_space=pltpu.SMEM)
RESIDENT = pl.BlockSpec(memory_space=pltpu.VMEM)
EXTRA = 16


def put_wide(ref, lead, row, cols, value):
    high = value.astype(BF16)
    ref[(*lead, slice(row, row + 1), cols)] = high
    ref[(*lead, slice(row + 1, row + 2), cols)] = (value - high.astype(F32)).astype(BF16)


def get_wide(ref, lead, row, cols):
    high = ref[(*lead, slice(row, row + 1), cols)].astype(F32)
    return high + ref[(*lead, slice(row + 1, row + 2), cols)].astype(F32)


def cross_forward(late, heads, swapped, pair=None, sent=None):
    tokens = heads.shape[2]
    first, count = (0, 1) if pair is None else (1, 2)

    def kernel(late_ref, q_own, q_got, k_own, v_own, got_ref, *refs):
        *more, o_ref, low_ref, l_ref, qs, ks, vs = refs

        @pl.when(late_ref[0] == 1)
        def _():
            qs[...] = q_own[0]
            if more:
                ks[...] = more[0][0]
                vs[...] = more[0][1]
            else:
                half = tokens // 2
                for side in range(2):
                    ks[:, side * half : (side + 1) * half] = got_ref[side]
                    vs[:, side * half : (side + 1) * half] = got_ref[2 + side]

        @pl.when(late_ref[0] == 0)
        def _():
            qs[...] = q_got[0]
            ks[...] = k_own[0]
            vs[...] = v_own[0]

        slot = pl.program_id(0) + first
        if more:

            @pl.when(slot == 1)
            def _():
                low_ref[0] = more[1][0]

        spans = [slice(i * WIDE, (i + 1) * WIDE) for i in range(tokens // WIDE)]

        @pl.loop(0, tokens // 2 // WIDE)
        def _(block):
            here = pl.ds(pl.multiple_of(block * WIDE, WIDE), WIDE)
            out, level = softmax_blocks(
                qs[:, here], [ks[:, span] for span in spans], [vs[:, span] for span in spans], False
            )
            o_ref[0, :, here] = out
            low_ref[slot, :HD, here] = out.astype(BF16)
            put_wide(low_ref, (slot,), HD, here, level)
            l_ref[0, :, here] = level

    low = (first + count, HD + EXTRA, tokens // 2)
    whole = lambda array: pl.BlockSpec(array.shape, lambda u: (0,) * len(array.shape))
    extra = [] if pair is None else [pair, sent]
    out_unit = lambda rows: pl.BlockSpec((1, rows, tokens // 2), lambda u: (u, 0, 0))
    return pl.pallas_call(
        kernel,
        grid=(count,),
        in_specs=[
            SCALAR,
            late_unit(HD, tokens, first),
            unit(HD, tokens, first),
            *own_pair(tokens, first),
            whole(swapped),
            *[whole(array) for array in extra],
        ],
        out_specs=[out_unit(HD), pl.BlockSpec(low, lambda u: (0, 0, 0)), out_unit(1)],
        out_shape=[
            jax.ShapeDtypeStruct((count, HD, tokens // 2), F32),
            jax.ShapeDtypeStruct(low, BF16),
            jax.ShapeDtypeStruct((count, 1, tokens // 2), F32),
        ],
        scratch_shapes=[
            pltpu.VMEM((HD, tokens // 2), BF16),
            pltpu.VMEM((HD, tokens), BF16),
            pltpu.VMEM((HD, tokens), BF16),
        ],
        compiler_params=params(),
        cost_estimate=SHORT,
        name="cross_forward",
    )(late, heads, swapped, heads, heads, swapped, *extra)


def merge(late, o_own, l_own, o_got, o_first, l_first, o_here, l_here):
    tokens = o_own.shape[2]
    length, half = tokens // QUAD, tokens // 2

    def kernel(late_ref, o_ref, l_ref, og_ref, of_ref, lf_ref, oh_ref, lh_ref, out_ref, low_ref, total_ref):
        is_late = late_ref[0] == 1
        for h in range(HL):
            for block in range(QUAD):
                side = block // 2
                number = 2 * h + side
                span = slice((block % 2) * length, (block % 2 + 1) * length)
                here = slice(block * length, (block + 1) * length)
                if number < 3:
                    other = og_ref[number, :HD, span].astype(F32)
                    level = get_wide(og_ref, (number,), HD, span)
                elif number == 3:
                    other, level = of_ref[0, :, span], lf_ref[0, :, span]
                else:
                    other, level = oh_ref[number - 4, :, span], lh_ref[number - 4, :, span]
                level = jnp.where(is_late, level, -1e30)
                own_level = l_ref[h, :, here]
                peak = jnp.maximum(own_level, level)
                own_part = jnp.exp(own_level - peak)
                part = jnp.exp(level - peak)
                mass = own_part + part
                out = o_ref[h, :, here] * (own_part / mass) + other * (part / mass)
                out_ref[block, h * HD : (h + 1) * HD] = out
                low_ref[block, h * HD : (h + 1) * HD] = out.astype(BF16)
                total_ref[h, :, here] = peak + jnp.log(mass)

    vmem = pl.BlockSpec(memory_space=pltpu.VMEM)
    return pl.pallas_call(
        kernel,
        in_specs=[SCALAR] + [vmem] * 7,
        out_specs=[vmem] * 3,
        out_shape=[
            jax.ShapeDtypeStruct((QUAD, HL * HD, length), F32),
            jax.ShapeDtypeStruct((QUAD, HL * HD, length), BF16),
            jax.ShapeDtypeStruct(l_own.shape, F32),
        ],
        compiler_params=params(),
        cost_estimate=SHORT,
        name="merge",
    )(late, o_own, l_own, o_got, o_first, l_first, o_here, l_here)


def prepare(grads, mixed, levels):
    _, _, length = grads.shape
    tokens = QUAD * length

    def kernel(g_ref, o_ref, l_ref, d_ref, gs_ref):
        for h in range(HL):
            rows = slice(h * HD, (h + 1) * HD)
            for block in range(QUAD):
                inner = jnp.sum(g_ref[block, rows].astype(F32) * o_ref[block, rows], axis=0, keepdims=True)
                d_ref[h, :, block * length : (block + 1) * length] = inner
        for number in range(3):
            h, side = number // 2, number % 2
            gs_ref[number, :, :HD] = g_ref[2 * side : 2 * side + 2, h * HD : (h + 1) * HD]
            for part in range(2):
                start = (2 * side + part) * length
                span = slice(start, start + length)
                put_wide(gs_ref, (number, part), HD, slice(None), l_ref[h, :, span])
                put_wide(gs_ref, (number, part), HD + 2, slice(None), d_ref[h, :, span])

    vmem = pl.BlockSpec(memory_space=pltpu.VMEM)
    return pl.pallas_call(
        kernel,
        in_specs=[vmem] * 3,
        out_specs=[vmem] * 2,
        out_shape=[
            jax.ShapeDtypeStruct(levels.shape, F32),
            jax.ShapeDtypeStruct((3, 2, HD + EXTRA, length), BF16),
        ],
        compiler_params=params(),
        cost_estimate=SHORT,
        name="prepare",
    )(grads, mixed, levels)


def grad_block(q, g, k, v, level, inner):
    probs = jnp.exp(dg(k, q, 0, 0) - level)
    score_grad = (probs * (dg(v, g, 0, 0) - inner)).astype(BF16)
    query_grad = dg(k, score_grad, 1, 0) * HD ** (-0.5)
    return query_grad, dg(q, score_grad, 1, 1), dg(g, probs.astype(BF16), 1, 1)


def own_backward(heads, grads, levels, inners, first, count):
    tokens = heads.shape[2]
    length = grads.shape[2]

    def kernel(q_ref, k_ref, v_ref, g_ref, l_ref, d_ref, dq_ref, dk_ref, dv_ref):
        dk_ref[...] = jnp.zeros_like(dk_ref)
        dv_ref[...] = jnp.zeros_like(dv_ref)

        for block in range(tokens // BLOCK):
            limit = (block + 1) * BLOCK
            here = slice(block * BLOCK, limit)
            start = block * BLOCK % length
            dq, dk, dv = grad_block(
                q_ref[0, :, here],
                g_ref[block * BLOCK // length, :, start : start + BLOCK],
                k_ref[0, :, :limit],
                v_ref[0, :, :limit],
                l_ref[0, :, here],
                d_ref[0, :, here],
            )
            dq_ref[0, :, here] = dq
            dk_ref[0, :, :limit] += dk
            dv_ref[0, :, :limit] += dv

    spec = lambda part: pl.BlockSpec((1, HD, tokens), lambda h: (h + part * HL + first, 0, 0))
    row = pl.BlockSpec((1, 1, tokens), lambda h: (h + first, 0, 0))
    out = pl.BlockSpec((1, HD, tokens), lambda h: (h, 0, 0))
    return pl.pallas_call(
        kernel,
        grid=(count,),
        in_specs=[
            spec(0),
            spec(1),
            spec(2),
            pl.BlockSpec((QUAD, HD, length), lambda h: (0, h + first, 0)),
            row,
            row,
        ],
        out_specs=[out] * 3,
        out_shape=[jax.ShapeDtypeStruct((count, HD, tokens), F32)] * 3,
        compiler_params=params(),
        cost_estimate=SHORT,
        name="own_backward",
    )(heads, heads, heads, grads, levels, inners)


def cross_backward(late, heads, grads, levels, inners, swapped, pair, g_sent):
    tokens = heads.shape[2]
    length = grads.shape[2]

    def kernel(
        late_ref, q_own, g_own, l_own, d_own, q_got, g_got, k_own, v_own, swap_ref, pair_got,
        dq_ref, low_ref, dk_ref, dv_ref, pair_ref, qs, gs, ls, ds, ks, vs,
    ):
        @pl.when(late_ref[0] == 1)
        def _():
            qs[...] = q_own[0]
            gs[...] = g_own[...]
            ls[...] = l_own[0]
            ds[...] = d_own[0]
            late_pair(pl.program_id(0), swap_ref, pair_got, ks, vs)

        @pl.when(late_ref[0] == 0)
        def _():
            qs[...] = q_got[0]
            gs[...] = g_got[0, :, :HD]
            for part in range(2):
                span = slice(part * length, (part + 1) * length)
                ls[:, span] = get_wide(g_got, (0, part), HD, slice(None))
                ds[:, span] = get_wide(g_got, (0, part), HD + 2, slice(None))
            ks[...] = k_own[0]
            vs[...] = v_own[0]

        number = pl.program_id(0)
        dk_ref[number] = jnp.zeros((HD, tokens), F32)
        dv_ref[number] = jnp.zeros((HD, tokens), F32)

        @pl.loop(0, tokens // 2 // BLOCK)
        def _(block):
            here = pl.ds(pl.multiple_of(block * BLOCK, BLOCK), BLOCK)
            there = pl.ds(pl.multiple_of(block * BLOCK % length, BLOCK), BLOCK)
            dq, dk, dv = grad_block(
                qs[:, here], gs[block * BLOCK // length, :, there], ks[...], vs[...], ls[:, here], ds[:, here]
            )
            dq_ref[0, :, here] = dq
            low_ref[0, :, here] = dq.astype(BF16)
            dk_ref[number] += dk
            dv_ref[number] += dv

        @pl.when(number == 2)
        def _():
            for first, ref in ((0, dk_ref), (2, dv_ref)):
                pair_ref[first] = ref[0].astype(BF16)
                pair_ref[first + 1] = (ref[1] + ref[2]).astype(BF16)

    whole = lambda count: pl.BlockSpec((count, HD, tokens), lambda u: (0, 0, 0))
    return pl.pallas_call(
        kernel,
        grid=(3,),
        in_specs=[
            SCALAR,
            late_unit(HD, tokens),
            pl.BlockSpec((2, HD, length), lambda u: ((3 + u) % 2, (3 + u) // 2, 0)),
            late_unit(1, tokens),
            late_unit(1, tokens),
            unit(HD, tokens),
            pl.BlockSpec((1, 2, HD + EXTRA, length), lambda u: (u, 0, 0, 0)),
            *own_pair(tokens),
            pl.BlockSpec(swapped.shape, lambda u: (0, 0, 0)),
            pl.BlockSpec(pair.shape, lambda u: (0, 0, 0)),
        ],
        out_specs=[unit(HD, tokens), unit(HD, tokens), whole(3), whole(3), whole(4)],
        out_shape=[
            jax.ShapeDtypeStruct((3, HD, tokens // 2), F32),
            jax.ShapeDtypeStruct((3, HD, tokens // 2), BF16),
            jax.ShapeDtypeStruct((3, HD, tokens), F32),
            jax.ShapeDtypeStruct((3, HD, tokens), F32),
            jax.ShapeDtypeStruct((4, HD, tokens), BF16),
        ],
        scratch_shapes=[
            pltpu.VMEM((HD, tokens // 2), BF16),
            pltpu.VMEM((2, HD, length), BF16),
            pltpu.VMEM((1, tokens // 2), F32),
            pltpu.VMEM((1, tokens // 2), F32),
            pltpu.VMEM((HD, tokens), BF16),
            pltpu.VMEM((HD, tokens), BF16),
        ],
        compiler_params=params(),
        cost_estimate=SHORT,
        name="cross_backward",
    )(
        late, heads, grads, levels, inners, swapped, g_sent, heads, heads, swapped, pair,
    )


def leave_tokens(place, late, own, here, dq_got, pair_got, weight):
    width = weight.shape[0]
    length = own[0].shape[2] // QUAD
    half = length // 2
    cols = 3 * HL * HD
    dq_here, dk_here, dv_here = here

    def kernel(
        place_ref, late_ref, dq0, dk0, dv0, dq1, dk1, dv1, dqh, dkh, dvh, dqg, pg, w_ref,
        keep, a1, a2, a3, b1, b2, b3, grads, sum_ref, backs,
    ):
        step = pl.program_id(0)
        block = place_ref[0] ^ step
        is_late = late_ref[0] == 1

        @pl.when(step == 0)
        def _():
            sum_ref[...] = jnp.zeros_like(sum_ref)

        early_heads = dq0.shape[0]
        head_of = lambda low, high, h: low[h] if h < early_heads else high[h - early_heads]
        side = block // 2
        span = pl.ds(pl.multiple_of((block % 2) * length, length), length)
        others = (
            dqg[side, :, span].astype(F32),
            jnp.where(side == 0, dqg[2, :, span].astype(F32), dqh[0, :, span]),
            dqh[1 + side, :, span],
        )
        for h in range(HL):
            mine = head_of(dq0, dq1, h)
            grads[h * HD : (h + 1) * HD] = (mine + jnp.where(is_late, others[h], 0.0)).astype(BF16)
        for part, (low, high, cross) in enumerate(((dk0, dk1, dkh), (dv0, dv1, dvh))):
            extra = (
                cross[0] + cross[1],
                cross[2] + pg[2 * part].astype(F32),
                pg[2 * part + 1].astype(F32),
            )
            for h in range(HL):
                first = ((1 + part) * HL + h) * HD
                mine = head_of(low, high, h)
                grads[first : first + HD] = (mine + jnp.where(is_late, 0.0, extra[h])).astype(BF16)

        grad = grads[...]
        sum_ref[...] += jnp.sum(grad.astype(F32), axis=1, keepdims=True)
        backs[...] = dg(grad, w_ref[:, :cols], 0, 1)

        @pl.when(step == 0)
        def _():
            keep[...] = backs[...]

        for number, (top, bottom) in enumerate(((a1, b1), (a2, b2), (a3, b3)), 1):

            @pl.when(step == number)
            def _():
                top[...] = backs[:half].astype(BF16)
                bottom[...] = backs[half:].astype(BF16)

    whole = lambda array: pl.BlockSpec(array.shape, lambda p, c: (0,) * len(array.shape))
    block_of = lambda count: pl.BlockSpec((count, HD, length), lambda p, c: (0, 0, c[0] ^ p))
    out_shape = [
        jax.ShapeDtypeStruct((length, width), F32),
        *[jax.ShapeDtypeStruct((half, width), BF16)] * 6,
        jax.ShapeDtypeStruct((cols, QUAD * length), BF16),
        jax.ShapeDtypeStruct((cols, 1), F32),
    ]
    out_specs = [whole(o) for o in out_shape]
    out_specs[7] = pl.BlockSpec((cols, length), lambda p, c: (0, c[0] ^ p))
    return pl.pallas_call(
        kernel,
        grid_spec=pltpu.PrefetchScalarGridSpec(
            num_scalar_prefetch=1,
            grid=(QUAD,),
            in_specs=[
                SCALAR,
                *[block_of(part.shape[0]) for part in own],
                RESIDENT,
                *[block_of(3)] * 2,
                RESIDENT,
                block_of(4),
                RESIDENT,
            ],
            out_specs=out_specs,
            scratch_shapes=[pltpu.VMEM((length, width), F32)],
        ),
        out_shape=out_shape,
        compiler_params=params(),
        cost_estimate=SHORT,
        name="leave_tokens",
    )(place, late, *own, dq_here, dk_here, dv_here, dq_got, pair_got, weight)


def unpack(place, rep, held, got):
    quads, rows, cols = held[0].shape
    part = cols // 9
    width = 2 * part

    def kernel(place_ref, rep_ref, *refs):
        ours, theirs, (wide_ref, outward_ref, narrow_ref) = refs[:QUAD], refs[QUAD:-3], refs[-3:]

        def emit(first, second):
            wide_ref[:, 0] = first[:, :, : 4 * width]
            outward_ref[:, 0, :, :part] = first[:, :, 4 * width :]
            outward_ref[:, 0, :, part:] = second[:, :, 4 * width :]
            for i in range(4):
                narrow_ref[:, 0, i] = second[:, :, i * width : (i + 1) * width]

        for j in range(QUAD):
            here = pl.program_id(0) == j
            pl.when(here & (rep_ref[0] == 0))(partial(emit, ours[j], theirs[j]))
            pl.when(here & (rep_ref[0] == 1))(partial(emit, theirs[j], ours[j]))

    group = quads

    def source(j):
        last = quads // group - 1
        index = lambda p, q, c: (jnp.where(p < j, 0, jnp.where(p == j, q, last)), 0, 0)
        return pl.BlockSpec((group, rows, cols), index)

    shards = QUAD * quads
    wide, outward, narrow = pl.pallas_call(
        kernel,
        grid_spec=pltpu.PrefetchScalarGridSpec(
            num_scalar_prefetch=1,
            grid=(QUAD, quads // group),
            in_specs=[SCALAR] + [source(j) for j in range(QUAD)] * 2,
            out_specs=[
                pl.BlockSpec((group, 1, rows, 4 * width), lambda p, q, c: (q, c[0] ^ p, 0, 0)),
                pl.BlockSpec((group, 1, rows, width), lambda p, q, c: (q, c[0] ^ p, 0, 0)),
                pl.BlockSpec((group, 1, 4, rows, width), lambda p, q, c: (q, c[0] ^ p, 0, 0, 0)),
            ],
        ),
        out_shape=[
            jax.ShapeDtypeStruct((quads, QUAD, rows, 4 * width), BF16),
            jax.ShapeDtypeStruct((quads, QUAD, rows, width), BF16),
            jax.ShapeDtypeStruct((quads, QUAD, 4, rows, width), BF16),
        ],
        compiler_params=params(),
        cost_estimate=SHORT,
        name="unpack",
    )(place, rep, *held, *got)
    depth = shards * rows
    return (
        wide.reshape(depth, 4 * width),
        outward.reshape(depth, width),
        narrow.reshape(4 * depth, width),
    )


def entry_payload(rep, qkv, vectors, flags, shards):
    depth, width = qkv.shape[0], qkv.shape[1] // 3
    rows = depth // 2
    part = width // QUAD
    chunks = flags.shape[0]

    def kernel(rep_ref, w_ref, *refs):
        *vector_refs, flag_ref, out_ref, slots = refs

        def emit(low):
            for member in range(QUAD):
                for i in range(3):
                    start = i * width + member * part
                    block = w_ref[low : low + rows, start : start + part]
                    for shard in range(member, shards, QUAD):
                        out_ref[shard, :, i * part : (i + 1) * part] = block

        pl.when(rep_ref[0] == 0)(partial(emit, 0))
        pl.when(rep_ref[0] == 1)(partial(emit, rows))
        slots[...] = jnp.zeros_like(slots)
        row = 0
        for ref in vector_refs:
            for start in range(0, ref.shape[1], depth):
                slots[row : row + 1, :depth] = ref[:, start : start + depth]
                row += 1
        counts = jnp.sum(flag_ref[...].astype(F32), axis=1, keepdims=True).astype(BF16)
        slots[row : row + chunks, :1] = counts
        for shard in range(shards):
            out_ref[shard, :, 3 * part :] = slots[...]

    vmem = pl.BlockSpec(memory_space=pltpu.VMEM)
    return pl.pallas_call(
        kernel,
        in_specs=[SCALAR] + [vmem] * (len(vectors) + 2),
        out_specs=vmem,
        out_shape=jax.ShapeDtypeStruct((shards, rows, 3 * part + 64), BF16),
        scratch_shapes=[pltpu.VMEM((rows, 64), BF16)],
        cost_estimate=SHORT,
        name="entry_payload",
    )(rep, qkv, *[v[None] for v in vectors], flags)


def rest_grads(first, place, shards, normed, pre_grad, hidden, branch_two, mixed, branch, share=None):
    length, width = normed.shape
    part = width // 2
    rows = width // shards
    quads = shards // QUAD
    steps = 4

    def kernel(first_ref, place_ref, n_ref, p_ref, h_ref, b_ref, m_ref, g_ref, *refs):
        *share_ref, out_ref, nt = refs
        step = pl.program_id(0)

        def store(number, shard, low, count, value):
            slot = ((shard % QUAD) ^ place_ref[0]) * quads + shard // QUAD
            here = pl.ds(pl.multiple_of(slot * rows, rows), rows)
            columns = pl.ds(low, count)
            if share_ref:
                value = value + share_ref[0][here, columns].astype(F32)
            out_ref[here, columns] = value.astype(BF16)

        def outward(low):
            block = dg(m_ref[...], g_ref[:, low : low + part], 1, 0)
            for shard in range(shards):
                store(shard, shard, 4 * width, part, block[shard * rows : (shard + 1) * rows])

        @pl.when(first_ref[0] == 1)
        def _():
            @pl.when(step == 0)
            def _():
                nt[...] = n_ref[...].T
                outward(0)

            block = dg(nt[...], p_ref[...], 1, 0)
            start = pl.multiple_of(step * width, width)
            for shard in range(shards):
                store(shard, shard, start, width, block[shard * rows : (shard + 1) * rows])

        @pl.when(first_ref[0] == 0)
        def _():
            @pl.when(step == 0)
            def _():
                outward(part)

            block = dg(h_ref[...].T, b_ref[...], 1, 0)
            for number in range(width // rows):
                shard = step * (width // (4 * rows)) + number // 4
                store(number, shard, number % 4 * width, width, block[number * rows : (number + 1) * rows])

    whole = lambda array: pl.BlockSpec(array.shape, lambda i: (0,) * len(array.shape))
    chunk = pl.BlockSpec((length, width), lambda i: (0, i))
    out_shape = jax.ShapeDtypeStruct((width, 9 * part), BF16)
    extra = [] if share is None else [share]
    return pl.pallas_call(
        kernel,
        grid=(steps,),
        in_specs=[SCALAR, SCALAR, RESIDENT, chunk, chunk, RESIDENT, RESIDENT, RESIDENT]
        + [RESIDENT] * len(extra),
        out_specs=whole(out_shape),
        out_shape=out_shape,
        scratch_shapes=[pltpu.VMEM((width, length), BF16)],
        compiler_params=params(),
        cost_estimate=SHORT,
        name="rest_grads",
    )(first, place, normed, pre_grad, hidden, branch_two, mixed, branch, *extra)


def quad_columns(rows, width):
    count = rows.shape[0]
    parts = rows.reshape(count, 3, QUAD, width // QUAD)
    return parts.transpose(2, 0, 1, 3).reshape(QUAD, count, 3 * width // QUAD)


def from_quad_columns(parts, width):
    count = parts.shape[1]
    split = parts.reshape(QUAD, count, 3, width // QUAD).transpose(1, 2, 0, 3)
    return split.reshape(count, 3 * width)


def swap_all(array):
    return lax.all_to_all(array, "shard", 0, 0, tiled=True)


def swap_quads(array):
    size = lax.axis_size("shard")
    groups = [[place + QUAD * q for q in range(size // QUAD)] for place in range(QUAD)]
    return lax.all_to_all(array, "shard", 0, 0, axis_index_groups=groups, tiled=True)


def swap_quad(array):
    size = lax.axis_size("shard")
    groups = [[QUAD * q + place for place in range(QUAD)] for q in range(size // QUAD)]
    return lax.all_to_all(array, "shard", 0, 0, axis_index_groups=groups, tiled=True)


def is_power(number):
    return number & (number - 1) == 0


def fetch_entry_plain(place, qkv, vectors, flags):
    width = qkv.shape[1] // 3
    mine = lax.dynamic_index_in_dim(
        quad_columns(lax.all_gather(qkv, "shard", axis=0, tiled=True), width), place, 0, False
    )
    whole = [lax.all_gather(v, "shard", axis=0, tiled=True) for v in vectors]
    count = lax.psum(jnp.sum(flags.astype(F32)), ("rep", "shard"))
    return jnp.pad(mine, ((0, 0), (0, 64))), whole, count


def fetch_entry_last(held, sizes, depth, chunks):
    shards, rows, cols = held.shape
    both = pair_in_order(lax.axis_index("rep"), held, trade_rep(held))
    weight = both.transpose(1, 0, 2, 3).reshape(shards * 2 * rows, cols)
    slots = both[..., cols - 64 :]
    whole, row = [], 0
    for size in sizes:
        count = size // depth
        whole.append(slots[0, :, row : row + count, :depth].reshape(-1))
        row += count
    counted = slots[:, :, row : row + chunks, 0]
    return weight, whole, jnp.sum(counted.astype(F32))


def split_low(values):
    high = lax.reduce_precision(values, 8, 7)
    return jnp.concatenate([high, values - high], axis=-2).astype(BF16)


def joined(slots):
    rows = slots.shape[-2] // 2
    slots = slots.astype(F32)
    return slots[..., :rows, :] + slots[..., rows:, :]


def reduce_entry(place, quad, weight_grad, vectors, squares, second):
    shards, reps = lax.axis_size("shard"), lax.axis_size("rep")
    quads = shards // QUAD
    width, cols = weight_grad.shape
    sizes = [v.shape[0] // shards for v in vectors]
    spread = jnp.concatenate([v.reshape(shards, -1) for v in vectors], axis=1)
    if reps != 2 or not is_power(quads):
        laid = jnp.zeros((QUAD, width, cols), BF16)
        laid = from_quad_columns(lax.dynamic_update_index_in_dim(laid, weight_grad, place, 0), width)
        grad = lax.psum_scatter(laid, "shard", scatter_dimension=0, tiled=True)
        grad = lax.psum(grad, "rep").astype(F32)
        total = lax.psum_scatter(spread.astype(BF16), "shard", scatter_dimension=0, tiled=True)
        total = lax.psum(total, "rep").astype(F32).reshape(-1)
        squares = lax.psum(squares, ("rep", "shard"))
        second = second()
    else:
        rep = lax.axis_index("rep")
        rows = width // shards // 2
        room = rows // 2 * 64
        spread = jnp.concatenate([spread, jnp.broadcast_to(squares, (shards, 1))], axis=1)
        spread = jnp.pad(spread, ((0, 0), (0, room - spread.shape[1])))
        slots = split_low(spread.reshape(shards, 1, rows // 2, 64))
        slots = jnp.broadcast_to(slots, (shards, 2, rows, 64))
        payload = jnp.concatenate([weight_grad.reshape(shards, 2, rows, cols), slots], axis=3)

        def add(arrays):
            total = sum(a[..., :cols].astype(F32) for a in arrays).astype(BF16)
            return jnp.concatenate([total, split_low(sum(joined(a[..., cols:]) for a in arrays))], axis=-1)

        side = lambda number: jnp.where(rep == 1, payload[:, number], payload[:, 1 - number])
        held = add([side(1), trade_rep(side(0))])
        held = swap_all(held.reshape(shards, rows, cols + 64)).reshape(quads, QUAD, rows, cols + 64)
        second = second()
        held, *second = together(held, *second)
        grad = sum(held[q, :, :, :cols].astype(F32) for q in range(quads)).astype(BF16)
        slots = sum(joined(held[q, :, :, cols:]) for q in range(quads))
        grad = from_quad_columns(grad, width)
        grad = pair_in_order(rep, grad, trade_rep(grad)).reshape(2 * rows, 3 * width).astype(F32)
        total = jnp.sum(slots, axis=0).reshape(-1)
        squares = total[sum(sizes)]
    whole, start = [], 0
    for size in sizes:
        whole.append(total[start : start + size])
        start += size
    return grad, whole, squares, second


def rep_part(array):
    reps = lax.axis_size("rep")
    rows = array.shape[0] // reps
    return lax.dynamic_slice_in_dim(array, lax.axis_index("rep") * rows, rows, 0)


def whole_tiles(rows):
    quads = lax.axis_size("shard") // QUAD
    return lax.axis_size("rep") == 2 and is_power(quads) and rows % 16 == 0


def pack_rest(wide, outward, narrow):
    rows = wide.shape[0]
    width = outward.shape[1]
    times = narrow.shape[0] // rows
    first = lax.axis_index("rep") == 0
    part = width // 2
    folded = narrow.reshape(times, rows, width).transpose(1, 0, 2).reshape(rows, times * width)
    return jnp.concatenate(
        [jnp.where(first, wide, folded), jnp.where(first, outward[:, :part], outward[:, part:])], axis=1
    )


def fetch_rest_plain(wide, outward, narrow):
    shards, reps = lax.axis_size("shard"), lax.axis_size("rep")
    wide, outward, narrow = rep_part(wide), rep_part(outward), rep_part(narrow)
    rows, ff = wide.shape
    width = outward.shape[1]
    times = narrow.shape[0] // rows
    folded = narrow.reshape(times, rows, width).transpose(1, 0, 2).reshape(rows, times * width)
    packed = jnp.concatenate([wide, outward, folded], axis=1)
    full = lax.all_gather(packed, ("shard", "rep"), axis=0, tiled=True)
    unfolded = full[:, ff + width :].reshape(shards * reps, rows, times, width).transpose(0, 2, 1, 3)
    return full[:, :ff], full[:, ff : ff + width], unfolded.reshape(ff, width)


def unpack_grads(mine):
    rows, cols = mine.shape
    part = cols // 9
    width, ff = 2 * part, 8 * part
    first, second = pair_in_order(lax.axis_index("rep"), mine, trade_rep(mine)).astype(F32)
    unfolded = second[:, :ff].reshape(rows, 4, width).transpose(1, 0, 2)
    return (
        first[:, :ff],
        jnp.concatenate([first[:, ff:], second[:, ff:]], axis=1),
        unfolded.reshape(rows * 4, width),
    )


def reduce_rest_plain(normed, pre_grad, hidden, branch_two, mixed, branch):
    shards, reps = lax.axis_size("shard"), lax.axis_size("rep")
    width, ff = normed.shape[1], hidden.shape[1]
    narrow = dg(hidden, branch_two, 0, 0).astype(BF16)
    wide = dg(normed, pre_grad, 0, 0).astype(BF16)
    outward = dg(mixed, branch, 1, 0).astype(BF16)
    devices = shards * reps
    rows = width // devices
    times = ff // width
    folded = narrow.reshape(devices, times, rows, width).transpose(0, 2, 1, 3).reshape(width, times * width)
    packed = jnp.concatenate([wide, outward, folded], axis=1)
    part = lax.psum_scatter(packed, ("shard", "rep"), scatter_dimension=0, tiled=True)
    full = lax.all_gather(part, "rep", axis=0, tiled=False).astype(F32)
    unfolded = full[:, :, ff + width :].reshape(reps, rows, times, width).transpose(0, 2, 1, 3)
    return (
        full[:, :, :ff].reshape(reps * rows, ff),
        full[:, :, ff : ff + width].reshape(reps * rows, width),
        unfolded.reshape(reps * rows * times, width),
    )


def local(
    incoming_tokens,
    mentor_outputs,
    counting_flags,
    opening_scale_factor,
    opening_offset_vector,
    query_key_value_map,
    asking_offset,
    content_offset,
    attend_result_map,
    attend_result_offset,
    latter_scale_factor,
    latter_offset_vector,
    widen_projection,
    hidden_offset,
    narrow_projection,
    narrow_offset,
):
    shards = lax.axis_size("shard")
    length, width = incoming_tokens.shape
    tokens = QUAD * length
    head_rows = HL * HD
    me = lax.axis_index("shard")
    place, quad = me % QUAD, me // QUAD
    place_arg = place.reshape(1).astype(jnp.int32)
    late = (quad % 2 == 0).reshape(1).astype(jnp.int32)
    quads = shards // QUAD
    fast = whole_tiles(query_key_value_map.shape[0])
    rep = lax.axis_index("rep")
    one = lambda number: number.reshape(1).astype(jnp.int32)
    flags = counting_flags.astype(F32)
    flag_rows = counting_flags.reshape(-1, min(256, length))
    vectors = [
        opening_scale_factor,
        opening_offset_vector,
        asking_offset,
        content_offset,
        attend_result_offset,
        latter_scale_factor,
        latter_offset_vector,
        narrow_offset,
        hidden_offset,
    ]
    rest_weights = (widen_projection, attend_result_map, narrow_projection)
    half = length // 2
    a, b = incoming_tokens[:half], incoming_tokens[half:]
    a1, b2 = trade(a, 1), trade(b, 2)
    if fast:
        payload = entry_payload(one(rep), query_key_value_map, vectors, flag_rows, shards)
        stack = pack_rest(*rest_weights)[None]
        a, b, a1, b2, payload = together(jnp.concatenate([a, a1]), jnp.concatenate([b, b2]), a1, b2, payload)
        a23, b13 = trade(a, 2), trade(b, 1)
        held = swap_all(payload)
        for bit in range(quads.bit_length() - 1):
            stack = pair_in_order((quad >> bit) & 1, stack, trade(stack, QUAD << bit))
            stack = stack.reshape(-1, *stack.shape[2:])
        a23, b13, held, stack = together(a23, b13, held, stack)
        rest_held = [stack] + [trade(stack, j) for j in range(1, QUAD)]
        sizes, depth = [v.shape[0] for v in vectors], query_key_value_map.shape[0]
        entry_weight, vectors, count_all = fetch_entry_last(held, sizes, depth, flag_rows.shape[0])
    else:
        entry_weight, vectors, count_all = fetch_entry_plain(place, query_key_value_map, vectors, flag_rows)
        wide_full, outward_full, narrow_full = fetch_rest_plain(*rest_weights)
        a23, b13 = trade(jnp.concatenate([a, a1]), 2), trade(jnp.concatenate([b, b2]), 1)
    pieces = [incoming_tokens, a1, b2, a23, b13]
    pregain, preshift, querybias, valuebias, outbias, midgain, midshift, shrinkbias, expandbias = (
        v.astype(F32) for v in vectors
    )
    own_rows = lambda v: lax.dynamic_slice_in_dim(v, place * head_rows, head_rows, 0)
    bias = jnp.concatenate([own_rows(querybias), jnp.zeros((head_rows,), F32), own_rows(valuebias)])
    normal_quad, projected, swap_send, pair_send = enter(
        place_arg, late, pieces, entry_weight, bias[:, None], pregain[None], preshift[None]
    )
    heads = projected.reshape(3 * HL, HD, tokens)
    swapped, pair = swap_sides(swap_send), to_late(pair_send)
    o_own, l_own = own_forward(heads)
    swapped, l_own = together(swapped, l_own)
    o_first, o_low, l_first = cross_forward(late, heads, swapped)
    pair, o_low = together(pair, o_low)
    o_here, o_low, l_here = cross_forward(late, heads, swapped, pair, o_low)
    o_got = to_late(o_low)
    if fast:
        o_got, *rest_held = together(o_got, *rest_held)
        rest_got = [trade_rep(array) for array in rest_held]
    mixed_wide, mixed_low, levels = merge(
        late, o_own, l_own, o_got, o_first, l_first, o_here, l_here
    )
    mixed = swap_quad(mixed_low).reshape(width, length)
    if fast:
        _, *rest_got = together(mixed_low, *rest_got)
        wide_full, outward_full, narrow_full = unpack(place_arg, one(rep), rest_held, rest_got)

    inputs = incoming_tokens.astype(F32)
    middle = inputs + (dg(mixed, outward_full, 0, 0) + outbias)
    normal_two, factor_two = normalize(middle)
    normed_two = (normal_two * midgain + midshift).astype(BF16)
    pre_act = dg(normed_two, wide_full, 1, 0) + expandbias
    activation, gelu_back = jax.vjp(partial(jax.nn.gelu, approximate=True), pre_act)
    hidden = activation.astype(BF16)
    output = middle + (dg(hidden, narrow_full, 1, 0) + shrinkbias)
    weight_rows = flags[:, None]
    mismatch = output - mentor_outputs.astype(F32)
    squares = jnp.sum(weight_rows * mismatch * mismatch)
    token_total = length * lax.axis_size("rep") * shards
    output_grad = 2.0 * token_total / count_all * weight_rows * mismatch

    branch_two_grad = output_grad.astype(BF16)
    shrinkbias_grad = column_sums(branch_two_grad)
    hidden_grad = dg(branch_two_grad, narrow_full, 1, 1)
    pre_grad = gelu_back(hidden_grad)[0].astype(BF16)
    expandbias_grad = column_sums(pre_grad)
    normed_two_grad = dg(pre_grad, wide_full, 1, 1)
    midgain_grad = jnp.sum(normed_two_grad * normal_two, axis=0)
    midshift_grad = jnp.sum(normed_two_grad, axis=0)
    scaled = normed_two_grad * midgain
    middle_grad = output_grad + factor_two * (
        scaled
        - jnp.mean(scaled, axis=-1, keepdims=True)
        - normal_two * jnp.mean(scaled * normal_two, axis=-1, keepdims=True)
    )
    branch_grad = middle_grad.astype(BF16)
    outbias_grad = column_sums(branch_grad)
    mixed_grad = dg(outward_full, branch_grad, 1, 1).astype(BF16)
    grads = swap_quad(mixed_grad.reshape(QUAD, head_rows, length))
    if fast:
        grads_of = lambda first, normed, other=None: rest_grads(
            one(first), place_arg, shards, normed, pre_grad, hidden, branch_two_grad, mixed, branch_grad, other
        )
        share = grads_of(rep == 1, normed_two)
        grads, share = together(grads, share)
        share = trade_rep(share)
    else:
        rest = reduce_rest_plain(normed_two, pre_grad, hidden, branch_two_grad, mixed, branch_grad)
    inners, g_send = prepare(grads, mixed_wide, levels)
    g_sent = to_early(g_send)
    own_first = own_backward(heads, grads, levels, inners, 0, 1)
    if fast:
        share, *own_first = together(share, *own_first)
        share = grads_of(rep == 0, normed_two, share)
        g_sent, share = together(g_sent, share)
        share = share.reshape(QUAD, quads, width // shards, -1)
        side = quads // 2
        got_a = trade(jnp.stack([share[1, :side], share[3, :side]]), 1)
        got_b = trade(share[2:, side:], 2)
    dq_here, dq_low, dk_here, dv_here, pair_back = cross_backward(
        late, heads, grads, levels, inners, swapped, pair, g_sent
    )
    levels, pair_back = together(levels, pair_back)
    dq_got, pair_got = to_late(dq_low), to_early(pair_back)
    if fast:
        last_a = (share[2, :side].astype(F32) + got_a[1].astype(F32)).astype(BF16)
        last_b = (share[1, side:].astype(F32) + got_b[1].astype(F32)).astype(BF16)
        levels, pair_back, last_a, last_b = together(levels, pair_back, last_a, last_b)
        last_a, last_b = trade(last_a, 2), trade(last_b, 1)
    own_last = own_backward(heads, grads, levels, inners, 1, HL - 1)
    own_last = together(*own_last, dq_got, pair_got)
    *own_last, dq_got, pair_got = own_last
    if fast:
        parts = (share[0, :side], got_a[0], last_a), (share[0, side:], got_b[0], last_b)
        share = jnp.concatenate([sum(p.astype(F32) for p in part).astype(BF16) for part in parts])
        dq_last, share = together(own_last[0], share)
        own_last = [dq_last, *own_last[1:]]
        share = swap_quads(share)
    *shares, heads_grad, bias_part = leave_tokens(
        place_arg,
        late,
        [*own_first, *own_last],
        (dq_here, dk_here, dv_here),
        dq_got,
        pair_got,
        entry_weight,
    )
    normal_grad = dg(normal_quad, heads_grad, 0, 1)
    grad_sums = bias_part[:, 0]
    weight_cols = entry_weight[:, : 3 * head_rows].astype(F32)
    inward_part = (pregain[:, None] * normal_grad + preshift[:, None] * grad_sums).astype(BF16)
    pregain_part = jnp.sum(weight_cols * normal_grad, axis=1)
    preshift_part = jnp.sum(weight_cols * grad_sums, axis=1)
    half = length // 2
    keep, a_parts, b_parts = shares[0], shares[1:4], shares[4:7]
    first_a, first_b = trade(a_parts[2], 1), trade(b_parts[2], 2)
    if fast:
        inward_part, share, first_a, first_b = together(inward_part, share, first_a, first_b)
    wide = lambda array: array.astype(F32)

    def second_step():
        return (
            trade(a_parts[0], 1),
            trade(b_parts[1], 2),
            trade((wide(a_parts[1]) + wide(first_a)).astype(BF16), 2),
            trade((wide(b_parts[0]) + wide(first_b)).astype(BF16), 1),
        )

    spread = lambda v: lax.dynamic_update_slice_in_dim(
        jnp.zeros((width,), F32), v, place * head_rows, 0
    )
    inward_grad, vector_grads, squares_all, arrived = reduce_entry(
        place,
        quad,
        inward_part,
        [
            pregain_part,
            preshift_part,
            spread(bias_part[:head_rows, 0]),
            spread(bias_part[2 * head_rows :, 0]),
            outbias_grad,
            midgain_grad,
            midshift_grad,
            shrinkbias_grad,
            expandbias_grad,
        ],
        squares,
        second_step,
    )
    normed_one_grad = jnp.concatenate(
        [
            keep[:half] + wide(arrived[0]) + wide(arrived[2]),
            keep[half:] + wide(arrived[1]) + wide(arrived[3]),
        ]
    )
    if fast:
        rest = unpack_grads(jnp.sum(share.astype(F32), axis=0).astype(BF16))
    distill_loss = squares_all / count_all
    normal_one, factor_one = normalize(inputs)
    scaled_one = normed_one_grad * pregain
    input_part = factor_one * (
        scaled_one
        - jnp.mean(scaled_one, axis=-1, keepdims=True)
        - normal_one * jnp.mean(scaled_one * normal_one, axis=-1, keepdims=True)
    )
    states_gradient = (middle_grad + input_part).astype(BF16)
    return (
        distill_loss,
        output.astype(BF16),
        states_gradient,
        vector_grads[0],
        vector_grads[1],
        inward_grad,
        vector_grads[2],
        vector_grads[3],
        rest[1],
        vector_grads[4],
        vector_grads[5],
        vector_grads[6],
        rest[0],
        vector_grads[8],
        rest[2],
        vector_grads[7],
    )


def solution(mesh):
    rows, vector, matrix = P(("rep", "shard"), None), P("shard"), P("shard", None)
    return jax.shard_map(
        local,
        mesh=mesh,
        in_specs=(
            rows,
            rows,
            P(("rep", "shard")),
            vector,
            vector,
            matrix,
            vector,
            vector,
            matrix,
            vector,
            vector,
            vector,
            matrix,
            vector,
            matrix,
            vector,
        ),
        out_specs=(
            P(),
            rows,
            rows,
            vector,
            vector,
            matrix,
            vector,
            vector,
            matrix,
            vector,
            vector,
            vector,
            matrix,
            vector,
            matrix,
            vector,
        ),
        check_vma=False,
    )
```

```python
from functools import partial

import jax
import jax.numpy as jnp
from jax import lax
from jax.experimental import pallas as pl
from jax.experimental.pallas import tpu as pltpu
from jax.sharding import PartitionSpec as P

H = 12
HD = 64
SPLIT = 8
BLOCK = 256
QUAD = SPLIT // 2
HL = H // QUAD
EPSILON = 1e-05
F32 = jnp.float32
BF16 = jnp.bfloat16
VMEM_LIMIT = 56 * 1024 * 1024


def dg(left, right, left_dim, right_dim):
    return lax.dot_general(
        left, right, (((left_dim,), (right_dim,)), ((), ())), preferred_element_type=F32
    )


def trade(array, mask):
    size = lax.axis_size("shard")
    return lax.ppermute(array, "shard", [(i, i ^ mask) for i in range(size)])


def trade_rep(array):
    return lax.ppermute(array, "rep", [(0, 1), (1, 0)])


def to_late(array):
    size = lax.axis_size("shard")
    pairs = [(i, (i + QUAD) % size) for i in range(size) if (i // QUAD) % 2 == 1]
    return lax.ppermute(array, "shard", pairs)


def to_early(array):
    size = lax.axis_size("shard")
    pairs = [(i, (i - QUAD) % size) for i in range(size) if (i // QUAD) % 2 == 0]
    return lax.ppermute(array, "shard", pairs)


def swap_sides(array):
    size = lax.axis_size("shard")
    step = lambda i: QUAD if (i // QUAD) % 2 == 1 else -QUAD
    return lax.ppermute(array, "shard", [(i, (i + step(i)) % size) for i in range(size)])


def in_order(pieces, place):
    step = 1
    while step < len(pieces):
        pieces = [
            jnp.where(place & step != 0, pieces[j ^ step], pieces[j]) for j in range(len(pieces))
        ]
        step *= 2
    return jnp.stack(pieces)


def together(*values):
    return lax.optimization_barrier(values)


def pair_in_order(bit, own, other):
    return jnp.where(bit == 1, jnp.stack([other, own]), jnp.stack([own, other]))


def normalize(values):
    center = values - jnp.mean(values, axis=-1, keepdims=True)
    spread = jnp.mean(center * center, axis=-1, keepdims=True)
    factor = lax.rsqrt(spread + EPSILON)
    return (center * factor, factor)


def column_sums(values):
    return jnp.sum(values.astype(F32), axis=0)


def params():
    return pltpu.CompilerParams(vmem_limit_bytes=VMEM_LIMIT)


SHORT = pl.CostEstimate(flops=1, transcendentals=0, bytes_accessed=1)


def load_tokens(step, refs, out):
    x_ref, a1, b2, a23, b13 = refs
    half = x_ref.shape[0] // 2
    low, high = slice(0, half), slice(half, 2 * half)
    sources = (
        (x_ref.at[low], x_ref.at[high]),
        (a1, b13.at[low]),
        (a23.at[low], b2),
        (a23.at[high], b13.at[high]),
    )
    for number, (top, bottom) in enumerate(sources):

        @pl.when(step == number)
        def _():
            out[low] = top[...].astype(F32)
            out[high] = bottom[...].astype(F32)


def enter(place, late, pieces, weight, bias, gain, shift):
    length, width = pieces[0].shape
    cols = 3 * HL * HD
    tokens = QUAD * length

    def kernel(
        place_ref, late_ref, x0, x1, x2, x3, x4, w_ref, bias_ref, gain_ref, shift_ref,
        n_ref, pt_ref, swap_ref, pair_ref, xs, wt,
    ):
        step = pl.program_id(0)
        block = place_ref[0] ^ step

        @pl.when(step == 0)
        def _():
            wt[...] = w_ref[:, :cols].T

        load_tokens(step, (x0, x1, x2, x3, x4), xs)
        normal, _ = normalize(xs[...])
        normed = (normal * gain_ref[...] + shift_ref[...]).astype(BF16)
        n_ref[...] = normal.astype(BF16)
        out = (dg(wt[...], normed, 1, 1) + bias_ref[...]).astype(BF16)
        head_rows = HL * HD
        queries = (out[:head_rows].astype(F32) * HD ** (-0.5)).astype(BF16)
        pt_ref[:head_rows] = queries
        pt_ref[head_rows:] = out[head_rows:]
        side = block // 2
        span = pl.ds(pl.multiple_of((block % 2) * length, length), length)
        take = lambda number: out[number * HD : (number + 1) * HD]

        @pl.when(late_ref[0] == 1)
        def _():
            swap_ref[side, :, span] = queries[:HD]

            @pl.when(side == 0)
            def _():
                swap_ref[2, :, span] = queries[HD : 2 * HD]
                swap_ref[3, :, span] = jnp.zeros_like(queries[:HD])

        @pl.when(late_ref[0] == 0)
        def _():
            swap_ref[side, :, span] = take(HL + 1)
            swap_ref[2 + side, :, span] = take(2 * HL + 1)

        span = pl.ds(pl.multiple_of(block * length, length), length)
        pair_ref[0, :, span] = take(HL + 2)
        pair_ref[1, :, span] = take(2 * HL + 2)

    whole = lambda array: pl.BlockSpec(array.shape, lambda p, c: (0,) * len(array.shape))
    swap_shape = jax.ShapeDtypeStruct((4, HD, tokens // 2), BF16)
    pair_shape = jax.ShapeDtypeStruct((2, HD, tokens), BF16)
    return pl.pallas_call(
        kernel,
        grid_spec=pltpu.PrefetchScalarGridSpec(
            num_scalar_prefetch=1,
            grid=(QUAD,),
            in_specs=[SCALAR] + [RESIDENT] * (len(pieces) + 4),
            out_specs=[
                pl.BlockSpec((length, width), lambda p, c: (c[0] ^ p, 0)),
                pl.BlockSpec((cols, length), lambda p, c: (0, c[0] ^ p)),
                whole(swap_shape),
                whole(pair_shape),
            ],
            scratch_shapes=[pltpu.VMEM((length, width), F32), pltpu.VMEM((cols, width), BF16)],
        ),
        out_shape=[
            jax.ShapeDtypeStruct((tokens, width), BF16),
            jax.ShapeDtypeStruct((cols, tokens), BF16),
            swap_shape,
            pair_shape,
        ],
        compiler_params=params(),
        cost_estimate=SHORT,
        name="enter",
    )(place, late, *pieces, weight, bias, gain, shift)


def softmax_blocks(q, keys, values, masked):
    following = dg(keys[0], q, 0, 0)
    for number, value in enumerate(values):
        scores = following
        if number + 1 < len(keys):
            following = dg(keys[number + 1], q, 0, 0)
        if masked and number == 0:
            row = lax.broadcasted_iota(jnp.int32, scores.shape, 0) // BLOCK
            col = lax.broadcasted_iota(jnp.int32, scores.shape, 1) // BLOCK
            scores = jnp.where(row <= col, scores, -1e30)
        top = jnp.max(scores, axis=0, keepdims=True)
        if number == 0:
            peak = top
            probs = jnp.exp(scores - peak)
            mass = jnp.sum(probs, axis=0, keepdims=True)
            total = dg(value, probs.astype(BF16), 1, 0)
        else:
            higher = jnp.maximum(peak, top)
            fade = jnp.exp(peak - higher)
            probs = jnp.exp(scores - higher)
            mass = mass * fade + jnp.sum(probs, axis=0, keepdims=True)
            total = total * fade + dg(value, probs.astype(BF16), 1, 0)
            peak = higher
    return total / mass, peak + jnp.log(mass)


WIDE = 2 * BLOCK


def own_forward(heads):
    tokens = heads.shape[2]

    def kernel(q_ref, k_ref, v_ref, o_ref, l_ref):
        for block in range(tokens // WIDE):
            order = [block, *range(block)]
            spans = [slice(i * WIDE, (i + 1) * WIDE) for i in order]
            out, level = softmax_blocks(
                q_ref[0, :, spans[0]],
                [k_ref[0, :, span] for span in spans],
                [v_ref[0, :, span] for span in spans],
                True,
            )
            o_ref[0, :, spans[0]] = out
            l_ref[0, :, spans[0]] = level

    spec = lambda first: pl.BlockSpec((1, HD, tokens), lambda h: (h + first, 0, 0))
    return pl.pallas_call(
        kernel,
        grid=(HL,),
        in_specs=[spec(0), spec(HL), spec(2 * HL)],
        out_specs=[spec(0), pl.BlockSpec((1, 1, tokens), lambda h: (h, 0, 0))],
        out_shape=[
            jax.ShapeDtypeStruct((HL, HD, tokens), F32),
            jax.ShapeDtypeStruct((HL, 1, tokens), F32),
        ],
        compiler_params=params(),
        cost_estimate=SHORT,
        name="own_forward",
    )(heads, heads, heads)


def late_unit(rows, tokens, first=0):
    return pl.BlockSpec(
        (1, rows, tokens // 2), lambda u: ((3 + first + u) // 2, 0, (3 + first + u) % 2)
    )


def unit(rows, tokens, first=0):
    return pl.BlockSpec((1, rows, tokens // 2), lambda u: (first + u, 0, 0))


def own_pair(tokens, first=0):
    spec = lambda part: pl.BlockSpec((1, HD, tokens), lambda u: (part * HL + (first + u) // 2, 0, 0))
    return [spec(1), spec(2)]


def late_pair(number, swapped, pair, ks, vs):
    half = ks.shape[1] // 2

    @pl.when(number == 0)
    def _():
        for side in range(2):
            ks[:, side * half : (side + 1) * half] = swapped[side]
            vs[:, side * half : (side + 1) * half] = swapped[2 + side]

    @pl.when(number > 0)
    def _():
        ks[...] = pair[0]
        vs[...] = pair[1]


SCALAR = pl.BlockSpec(memory_space=pltpu.SMEM)
RESIDENT = pl.BlockSpec(memory_space=pltpu.VMEM)
EXTRA = 16


def put_wide(ref, lead, row, cols, value):
    high = value.astype(BF16)
    ref[(*lead, slice(row, row + 1), cols)] = high
    ref[(*lead, slice(row + 1, row + 2), cols)] = (value - high.astype(F32)).astype(BF16)


def get_wide(ref, lead, row, cols):
    high = ref[(*lead, slice(row, row + 1), cols)].astype(F32)
    return high + ref[(*lead, slice(row + 1, row + 2), cols)].astype(F32)


def cross_forward(late, heads, swapped, pair=None, sent=None):
    tokens = heads.shape[2]
    first, count = (0, 1) if pair is None else (1, 2)

    def kernel(late_ref, q_own, q_got, k_own, v_own, got_ref, *refs):
        *more, o_ref, low_ref, l_ref, qs, ks, vs = refs

        @pl.when(late_ref[0] == 1)
        def _():
            qs[...] = q_own[0]
            if more:
                ks[...] = more[0][0]
                vs[...] = more[0][1]
            else:
                half = tokens // 2
                for side in range(2):
                    ks[:, side * half : (side + 1) * half] = got_ref[side]
                    vs[:, side * half : (side + 1) * half] = got_ref[2 + side]

        @pl.when(late_ref[0] == 0)
        def _():
            qs[...] = q_got[0]
            ks[...] = k_own[0]
            vs[...] = v_own[0]

        slot = pl.program_id(0) + first
        if more:

            @pl.when(slot == 1)
            def _():
                low_ref[0] = more[1][0]

        spans = [slice(i * WIDE, (i + 1) * WIDE) for i in range(tokens // WIDE)]

        @pl.loop(0, tokens // 2 // WIDE)
        def _(block):
            here = pl.ds(pl.multiple_of(block * WIDE, WIDE), WIDE)
            out, level = softmax_blocks(
                qs[:, here], [ks[:, span] for span in spans], [vs[:, span] for span in spans], False
            )
            o_ref[0, :, here] = out
            low_ref[slot, :HD, here] = out.astype(BF16)
            put_wide(low_ref, (slot,), HD, here, level)
            l_ref[0, :, here] = level

    low = (first + count, HD + EXTRA, tokens // 2)
    whole = lambda array: pl.BlockSpec(array.shape, lambda u: (0,) * len(array.shape))
    extra = [] if pair is None else [pair, sent]
    out_unit = lambda rows: pl.BlockSpec((1, rows, tokens // 2), lambda u: (u, 0, 0))
    return pl.pallas_call(
        kernel,
        grid=(count,),
        in_specs=[
            SCALAR,
            late_unit(HD, tokens, first),
            unit(HD, tokens, first),
            *own_pair(tokens, first),
            whole(swapped),
            *[whole(array) for array in extra],
        ],
        out_specs=[out_unit(HD), pl.BlockSpec(low, lambda u: (0, 0, 0)), out_unit(1)],
        out_shape=[
            jax.ShapeDtypeStruct((count, HD, tokens // 2), F32),
            jax.ShapeDtypeStruct(low, BF16),
            jax.ShapeDtypeStruct((count, 1, tokens // 2), F32),
        ],
        scratch_shapes=[
            pltpu.VMEM((HD, tokens // 2), BF16),
            pltpu.VMEM((HD, tokens), BF16),
            pltpu.VMEM((HD, tokens), BF16),
        ],
        compiler_params=params(),
        cost_estimate=SHORT,
        name="cross_forward",
    )(late, heads, swapped, heads, heads, swapped, *extra)


def merge(late, o_own, l_own, o_got, o_first, l_first, o_here, l_here):
    tokens = o_own.shape[2]
    length, half = tokens // QUAD, tokens // 2

    def kernel(late_ref, o_ref, l_ref, og_ref, of_ref, lf_ref, oh_ref, lh_ref, out_ref, low_ref, total_ref):
        is_late = late_ref[0] == 1
        for h in range(HL):
            for block in range(QUAD):
                side = block // 2
                number = 2 * h + side
                span = slice((block % 2) * length, (block % 2 + 1) * length)
                here = slice(block * length, (block + 1) * length)
                if number < 3:
                    other = og_ref[number, :HD, span].astype(F32)
                    level = get_wide(og_ref, (number,), HD, span)
                elif number == 3:
                    other, level = of_ref[0, :, span], lf_ref[0, :, span]
                else:
                    other, level = oh_ref[number - 4, :, span], lh_ref[number - 4, :, span]
                level = jnp.where(is_late, level, -1e30)
                own_level = l_ref[h, :, here]
                peak = jnp.maximum(own_level, level)
                own_part = jnp.exp(own_level - peak)
                part = jnp.exp(level - peak)
                mass = own_part + part
                out = o_ref[h, :, here] * (own_part / mass) + other * (part / mass)
                out_ref[block, h * HD : (h + 1) * HD] = out
                low_ref[block, h * HD : (h + 1) * HD] = out.astype(BF16)
                total_ref[h, :, here] = peak + jnp.log(mass)

    vmem = pl.BlockSpec(memory_space=pltpu.VMEM)
    return pl.pallas_call(
        kernel,
        in_specs=[SCALAR] + [vmem] * 7,
        out_specs=[vmem] * 3,
        out_shape=[
            jax.ShapeDtypeStruct((QUAD, HL * HD, length), F32),
            jax.ShapeDtypeStruct((QUAD, HL * HD, length), BF16),
            jax.ShapeDtypeStruct(l_own.shape, F32),
        ],
        compiler_params=params(),
        cost_estimate=SHORT,
        name="merge",
    )(late, o_own, l_own, o_got, o_first, l_first, o_here, l_here)


def prepare(grads, mixed, levels):
    _, _, length = grads.shape
    tokens = QUAD * length

    def kernel(g_ref, o_ref, l_ref, d_ref, gs_ref):
        for h in range(HL):
            rows = slice(h * HD, (h + 1) * HD)
            for block in range(QUAD):
                inner = jnp.sum(g_ref[block, rows].astype(F32) * o_ref[block, rows], axis=0, keepdims=True)
                d_ref[h, :, block * length : (block + 1) * length] = inner
        for number in range(3):
            h, side = number // 2, number % 2
            gs_ref[number, :, :HD] = g_ref[2 * side : 2 * side + 2, h * HD : (h + 1) * HD]
            for part in range(2):
                start = (2 * side + part) * length
                span = slice(start, start + length)
                put_wide(gs_ref, (number, part), HD, slice(None), l_ref[h, :, span])
                put_wide(gs_ref, (number, part), HD + 2, slice(None), d_ref[h, :, span])

    vmem = pl.BlockSpec(memory_space=pltpu.VMEM)
    return pl.pallas_call(
        kernel,
        in_specs=[vmem] * 3,
        out_specs=[vmem] * 2,
        out_shape=[
            jax.ShapeDtypeStruct(levels.shape, F32),
            jax.ShapeDtypeStruct((3, 2, HD + EXTRA, length), BF16),
        ],
        compiler_params=params(),
        cost_estimate=SHORT,
        name="prepare",
    )(grads, mixed, levels)


def grad_block(q, g, k, v, level, inner):
    probs = jnp.exp(dg(k, q, 0, 0) - level)
    score_grad = (probs * (dg(v, g, 0, 0) - inner)).astype(BF16)
    query_grad = dg(k, score_grad, 1, 0) * HD ** (-0.5)
    return query_grad, dg(q, score_grad, 1, 1), dg(g, probs.astype(BF16), 1, 1)


def own_backward(heads, grads, levels, inners, first, count):
    tokens = heads.shape[2]
    length = grads.shape[2]

    def kernel(q_ref, k_ref, v_ref, g_ref, l_ref, d_ref, dq_ref, dk_ref, dv_ref, dk_sum, dv_sum):
        dk_sum[...] = jnp.zeros_like(dk_sum)
        dv_sum[...] = jnp.zeros_like(dv_sum)

        for block in range(tokens // BLOCK):
            limit = (block + 1) * BLOCK
            here = slice(block * BLOCK, limit)
            start = block * BLOCK % length
            dq, dk, dv = grad_block(
                q_ref[0, :, here],
                g_ref[block * BLOCK // length, :, start : start + BLOCK],
                k_ref[0, :, :limit],
                v_ref[0, :, :limit],
                l_ref[0, :, here],
                d_ref[0, :, here],
            )
            dq_ref[0, :, here] = dq.astype(BF16)
            dk_sum[:, :limit] += dk
            dv_sum[:, :limit] += dv
        dk_ref[0] = dk_sum[...].astype(BF16)
        dv_ref[0] = dv_sum[...].astype(BF16)

    spec = lambda part: pl.BlockSpec((1, HD, tokens), lambda h: (h + part * HL + first, 0, 0))
    row = pl.BlockSpec((1, 1, tokens), lambda h: (h + first, 0, 0))
    out = pl.BlockSpec((1, HD, tokens), lambda h: (h, 0, 0))
    return pl.pallas_call(
        kernel,
        grid=(count,),
        in_specs=[
            spec(0),
            spec(1),
            spec(2),
            pl.BlockSpec((QUAD, HD, length), lambda h: (0, h + first, 0)),
            row,
            row,
        ],
        out_specs=[out] * 3,
        out_shape=[jax.ShapeDtypeStruct((count, HD, tokens), BF16)] * 3,
        scratch_shapes=[pltpu.VMEM((HD, tokens), F32)] * 2,
        compiler_params=params(),
        cost_estimate=SHORT,
        name="own_backward",
    )(heads, heads, heads, grads, levels, inners)


def cross_backward(late, heads, grads, levels, inners, swapped, pair, g_sent):
    tokens = heads.shape[2]
    length = grads.shape[2]

    def kernel(
        late_ref, q_own, g_own, l_own, d_own, q_got, g_got, k_own, v_own, swap_ref, pair_got,
        low_ref, early_ref, pair_ref, qs, gs, ls, ds, ks, vs, dk_ref, dv_ref,
    ):
        @pl.when(late_ref[0] == 1)
        def _():
            qs[...] = q_own[0]
            gs[...] = g_own[...]
            ls[...] = l_own[0]
            ds[...] = d_own[0]
            late_pair(pl.program_id(0), swap_ref, pair_got, ks, vs)

        @pl.when(late_ref[0] == 0)
        def _():
            qs[...] = q_got[0]
            gs[...] = g_got[0, :, :HD]
            for part in range(2):
                span = slice(part * length, (part + 1) * length)
                ls[:, span] = get_wide(g_got, (0, part), HD, slice(None))
                ds[:, span] = get_wide(g_got, (0, part), HD + 2, slice(None))
            ks[...] = k_own[0]
            vs[...] = v_own[0]

        number = pl.program_id(0)
        dk_ref[number] = jnp.zeros((HD, tokens), F32)
        dv_ref[number] = jnp.zeros((HD, tokens), F32)

        @pl.loop(0, tokens // 2 // BLOCK)
        def _(block):
            here = pl.ds(pl.multiple_of(block * BLOCK, BLOCK), BLOCK)
            there = pl.ds(pl.multiple_of(block * BLOCK % length, BLOCK), BLOCK)
            dq, dk, dv = grad_block(
                qs[:, here], gs[block * BLOCK // length, :, there], ks[...], vs[...], ls[:, here], ds[:, here]
            )
            low_ref[0, :, here] = dq.astype(BF16)
            dk_ref[number] += dk
            dv_ref[number] += dv

        @pl.when(number == 2)
        def _():
            for first, ref in ((0, dk_ref), (2, dv_ref)):
                pair_ref[first] = ref[0].astype(BF16)
                pair_ref[first + 1] = (ref[1] + ref[2]).astype(BF16)
                early_ref[first] = (ref[0] + ref[1]).astype(BF16)
                early_ref[first + 1] = ref[2].astype(BF16)

    whole = lambda count: pl.BlockSpec((count, HD, tokens), lambda u: (0, 0, 0))
    return pl.pallas_call(
        kernel,
        grid=(3,),
        in_specs=[
            SCALAR,
            late_unit(HD, tokens),
            pl.BlockSpec((2, HD, length), lambda u: ((3 + u) % 2, (3 + u) // 2, 0)),
            late_unit(1, tokens),
            late_unit(1, tokens),
            unit(HD, tokens),
            pl.BlockSpec((1, 2, HD + EXTRA, length), lambda u: (u, 0, 0, 0)),
            *own_pair(tokens),
            pl.BlockSpec(swapped.shape, lambda u: (0, 0, 0)),
            pl.BlockSpec(pair.shape, lambda u: (0, 0, 0)),
        ],
        out_specs=[unit(HD, tokens), whole(4), whole(4)],
        out_shape=[
            jax.ShapeDtypeStruct((3, HD, tokens // 2), BF16),
            jax.ShapeDtypeStruct((4, HD, tokens), BF16),
            jax.ShapeDtypeStruct((4, HD, tokens), BF16),
        ],
        scratch_shapes=[
            pltpu.VMEM((HD, tokens // 2), BF16),
            pltpu.VMEM((2, HD, length), BF16),
            pltpu.VMEM((1, tokens // 2), F32),
            pltpu.VMEM((1, tokens // 2), F32),
            pltpu.VMEM((HD, tokens), BF16),
            pltpu.VMEM((HD, tokens), BF16),
            pltpu.VMEM((3, HD, tokens), F32),
            pltpu.VMEM((3, HD, tokens), F32),
        ],
        compiler_params=params(),
        cost_estimate=SHORT,
        name="cross_backward",
    )(
        late, heads, grads, levels, inners, swapped, g_sent, heads, heads, swapped, pair,
    )


def leave_tokens(place, late, own, here, dq_got, pair_got, weight):
    width = weight.shape[0]
    length = own[0].shape[2] // QUAD
    half = length // 2
    cols = 3 * HL * HD
    dq_here, early_here = here

    def kernel(
        place_ref, late_ref, dq0, dk0, dv0, dq1, dk1, dv1, dqh, early, dqg, pg, w_ref,
        keep, a1, a2, a3, b1, b2, b3, grads, sum_ref, backs,
    ):
        step = pl.program_id(0)
        block = place_ref[0] ^ step
        is_late = late_ref[0] == 1

        @pl.when(step == 0)
        def _():
            sum_ref[...] = jnp.zeros_like(sum_ref)

        early_heads = dq0.shape[0]
        head_of = lambda low, high, h: low[h] if h < early_heads else high[h - early_heads]
        side = block // 2
        span = pl.ds(pl.multiple_of((block % 2) * length, length), length)
        others = (
            dqg[side, :, span],
            jnp.where(side == 0, dqg[2, :, span], dqh[0, :, span]),
            dqh[1 + side, :, span],
        )
        for h in range(HL):
            mine = head_of(dq0, dq1, h).astype(F32)
            other = jnp.where(is_late, others[h].astype(F32), 0.0)
            grads[h * HD : (h + 1) * HD] = (mine + other).astype(BF16)
        for part, (low, high) in enumerate(((dk0, dk1), (dv0, dv1))):
            extra = (
                early[2 * part].astype(F32),
                early[2 * part + 1].astype(F32) + pg[2 * part].astype(F32),
                pg[2 * part + 1].astype(F32),
            )
            for h in range(HL):
                first = ((1 + part) * HL + h) * HD
                mine = head_of(low, high, h).astype(F32)
                grads[first : first + HD] = (mine + jnp.where(is_late, 0.0, extra[h])).astype(BF16)

        grad = grads[...]
        sum_ref[...] += jnp.sum(grad.astype(F32), axis=1, keepdims=True)
        backs[...] = dg(grad, w_ref[:, :cols], 0, 1)

        @pl.when(step == 0)
        def _():
            keep[...] = backs[...]

        for number, (top, bottom) in enumerate(((a1, b1), (a2, b2), (a3, b3)), 1):

            @pl.when(step == number)
            def _():
                top[...] = backs[:half].astype(BF16)
                bottom[...] = backs[half:].astype(BF16)

    whole = lambda array: pl.BlockSpec(array.shape, lambda p, c: (0,) * len(array.shape))
    block_of = lambda count: pl.BlockSpec((count, HD, length), lambda p, c: (0, 0, c[0] ^ p))
    out_shape = [
        jax.ShapeDtypeStruct((length, width), F32),
        *[jax.ShapeDtypeStruct((half, width), BF16)] * 6,
        jax.ShapeDtypeStruct((cols, QUAD * length), BF16),
        jax.ShapeDtypeStruct((cols, 1), F32),
    ]
    out_specs = [whole(o) for o in out_shape]
    out_specs[7] = pl.BlockSpec((cols, length), lambda p, c: (0, c[0] ^ p))
    return pl.pallas_call(
        kernel,
        grid_spec=pltpu.PrefetchScalarGridSpec(
            num_scalar_prefetch=1,
            grid=(QUAD,),
            in_specs=[
                SCALAR,
                *[block_of(part.shape[0]) for part in own],
                RESIDENT,
                block_of(4),
                RESIDENT,
                block_of(4),
                RESIDENT,
            ],
            out_specs=out_specs,
            scratch_shapes=[pltpu.VMEM((length, width), F32)],
        ),
        out_shape=out_shape,
        compiler_params=params(),
        cost_estimate=SHORT,
        name="leave_tokens",
    )(place, late, *own, dq_here, early_here, dq_got, pair_got, weight)


def unpack(place, rep, held, got):
    quads, rows, cols = held[0].shape
    part = cols // 9
    width = 2 * part

    def kernel(place_ref, rep_ref, *refs):
        ours, theirs, (wide_ref, outward_ref, narrow_ref) = refs[:QUAD], refs[QUAD:-3], refs[-3:]

        def emit(first, second):
            wide_ref[:, 0] = first[:, :, : 4 * width]
            outward_ref[:, 0, :, :part] = first[:, :, 4 * width :]
            outward_ref[:, 0, :, part:] = second[:, :, 4 * width :]
            for i in range(4):
                narrow_ref[:, 0, i] = second[:, :, i * width : (i + 1) * width]

        for j in range(QUAD):
            here = pl.program_id(0) == j
            pl.when(here & (rep_ref[0] == 0))(partial(emit, ours[j], theirs[j]))
            pl.when(here & (rep_ref[0] == 1))(partial(emit, theirs[j], ours[j]))

    group = quads

    def source(j):
        last = quads // group - 1
        index = lambda p, q, c: (jnp.where(p < j, 0, jnp.where(p == j, q, last)), 0, 0)
        return pl.BlockSpec((group, rows, cols), index)

    shards = QUAD * quads
    wide, outward, narrow = pl.pallas_call(
        kernel,
        grid_spec=pltpu.PrefetchScalarGridSpec(
            num_scalar_prefetch=1,
            grid=(QUAD, quads // group),
            in_specs=[SCALAR] + [source(j) for j in range(QUAD)] * 2,
            out_specs=[
                pl.BlockSpec((group, 1, rows, 4 * width), lambda p, q, c: (q, c[0] ^ p, 0, 0)),
                pl.BlockSpec((group, 1, rows, width), lambda p, q, c: (q, c[0] ^ p, 0, 0)),
                pl.BlockSpec((group, 1, 4, rows, width), lambda p, q, c: (q, c[0] ^ p, 0, 0, 0)),
            ],
        ),
        out_shape=[
            jax.ShapeDtypeStruct((quads, QUAD, rows, 4 * width), BF16),
            jax.ShapeDtypeStruct((quads, QUAD, rows, width), BF16),
            jax.ShapeDtypeStruct((quads, QUAD, 4, rows, width), BF16),
        ],
        compiler_params=params(),
        cost_estimate=SHORT,
        name="unpack",
    )(place, rep, *held, *got)
    depth = shards * rows
    return (
        wide.reshape(depth, 4 * width),
        outward.reshape(depth, width),
        narrow.reshape(4 * depth, width),
    )


def entry_payload(rep, qkv, vectors, flags, shards):
    depth, width = qkv.shape[0], qkv.shape[1] // 3
    rows = depth // 2
    part = width // QUAD
    chunks = flags.shape[0]

    def kernel(rep_ref, w_ref, *refs):
        *vector_refs, flag_ref, out_ref, slots = refs

        def emit(low):
            for member in range(QUAD):
                for i in range(3):
                    start = i * width + member * part
                    block = w_ref[low : low + rows, start : start + part]
                    for shard in range(member, shards, QUAD):
                        out_ref[shard, :, i * part : (i + 1) * part] = block

        pl.when(rep_ref[0] == 0)(partial(emit, 0))
        pl.when(rep_ref[0] == 1)(partial(emit, rows))
        slots[...] = jnp.zeros_like(slots)
        row = 0
        for ref in vector_refs:
            for start in range(0, ref.shape[1], depth):
                slots[row : row + 1, :depth] = ref[:, start : start + depth]
                row += 1
        counts = jnp.sum(flag_ref[...].astype(F32), axis=1, keepdims=True).astype(BF16)
        slots[row : row + chunks, :1] = counts
        for shard in range(shards):
            out_ref[shard, :, 3 * part :] = slots[...]

    vmem = pl.BlockSpec(memory_space=pltpu.VMEM)
    return pl.pallas_call(
        kernel,
        in_specs=[SCALAR] + [vmem] * (len(vectors) + 2),
        out_specs=vmem,
        out_shape=jax.ShapeDtypeStruct((shards, rows, 3 * part + 64), BF16),
        scratch_shapes=[pltpu.VMEM((rows, 64), BF16)],
        cost_estimate=SHORT,
        name="entry_payload",
    )(rep, qkv, *[v[None] for v in vectors], flags)


def rest_grads(first, place, shards, normed, pre_grad, hidden, branch_two, mixed, branch, share=None):
    length, width = normed.shape
    part = width // 2
    rows = width // shards
    quads = shards // QUAD
    steps = 4

    def kernel(first_ref, place_ref, n_ref, p_ref, h_ref, b_ref, m_ref, g_ref, *refs):
        *share_ref, out_ref, nt = refs
        step = pl.program_id(0)

        def store(number, shard, low, count, value):
            slot = ((shard % QUAD) ^ place_ref[0]) * quads + shard // QUAD
            here = pl.ds(pl.multiple_of(slot * rows, rows), rows)
            columns = pl.ds(low, count)
            if share_ref:
                value = value + share_ref[0][here, columns].astype(F32)
            out_ref[here, columns] = value.astype(BF16)

        def outward(low):
            block = dg(m_ref[...], g_ref[:, low : low + part], 1, 0)
            for shard in range(shards):
                store(shard, shard, 4 * width, part, block[shard * rows : (shard + 1) * rows])

        @pl.when(first_ref[0] == 1)
        def _():
            @pl.when(step == 0)
            def _():
                nt[...] = n_ref[...].T
                outward(0)

            block = dg(nt[...], p_ref[...], 1, 0)
            start = pl.multiple_of(step * width, width)
            for shard in range(shards):
                store(shard, shard, start, width, block[shard * rows : (shard + 1) * rows])

        @pl.when(first_ref[0] == 0)
        def _():
            @pl.when(step == 0)
            def _():
                outward(part)

            block = dg(h_ref[...].T, b_ref[...], 1, 0)
            for number in range(width // rows):
                shard = step * (width // (4 * rows)) + number // 4
                store(number, shard, number % 4 * width, width, block[number * rows : (number + 1) * rows])

    whole = lambda array: pl.BlockSpec(array.shape, lambda i: (0,) * len(array.shape))
    chunk = pl.BlockSpec((length, width), lambda i: (0, i))
    out_shape = jax.ShapeDtypeStruct((width, 9 * part), BF16)
    extra = [] if share is None else [share]
    return pl.pallas_call(
        kernel,
        grid=(steps,),
        in_specs=[SCALAR, SCALAR, RESIDENT, chunk, chunk, RESIDENT, RESIDENT, RESIDENT]
        + [RESIDENT] * len(extra),
        out_specs=whole(out_shape),
        out_shape=out_shape,
        scratch_shapes=[pltpu.VMEM((width, length), BF16)],
        compiler_params=params(),
        cost_estimate=SHORT,
        name="rest_grads",
    )(first, place, normed, pre_grad, hidden, branch_two, mixed, branch, *extra)


def quad_columns(rows, width):
    count = rows.shape[0]
    parts = rows.reshape(count, 3, QUAD, width // QUAD)
    return parts.transpose(2, 0, 1, 3).reshape(QUAD, count, 3 * width // QUAD)


def from_quad_columns(parts, width):
    count = parts.shape[1]
    split = parts.reshape(QUAD, count, 3, width // QUAD).transpose(1, 2, 0, 3)
    return split.reshape(count, 3 * width)


def swap_all(array):
    return lax.all_to_all(array, "shard", 0, 0, tiled=True)


def swap_quads(array):
    size = lax.axis_size("shard")
    groups = [[place + QUAD * q for q in range(size // QUAD)] for place in range(QUAD)]
    return lax.all_to_all(array, "shard", 0, 0, axis_index_groups=groups, tiled=True)


def swap_quad(array):
    size = lax.axis_size("shard")
    groups = [[QUAD * q + place for place in range(QUAD)] for q in range(size // QUAD)]
    return lax.all_to_all(array, "shard", 0, 0, axis_index_groups=groups, tiled=True)


def is_power(number):
    return number & (number - 1) == 0


def fetch_entry_plain(place, qkv, vectors, flags):
    width = qkv.shape[1] // 3
    mine = lax.dynamic_index_in_dim(
        quad_columns(lax.all_gather(qkv, "shard", axis=0, tiled=True), width), place, 0, False
    )
    whole = [lax.all_gather(v, "shard", axis=0, tiled=True) for v in vectors]
    count = lax.psum(jnp.sum(flags.astype(F32)), ("rep", "shard"))
    return jnp.pad(mine, ((0, 0), (0, 64))), whole, count


def fetch_entry_last(held, sizes, depth, chunks):
    shards, rows, cols = held.shape
    both = pair_in_order(lax.axis_index("rep"), held, trade_rep(held))
    weight = both.transpose(1, 0, 2, 3).reshape(shards * 2 * rows, cols)
    slots = both[..., cols - 64 :]
    whole, row = [], 0
    for size in sizes:
        count = size // depth
        whole.append(slots[0, :, row : row + count, :depth].reshape(-1))
        row += count
    counted = slots[:, :, row : row + chunks, 0]
    return weight, whole, jnp.sum(counted.astype(F32))


def split_low(values):
    high = lax.reduce_precision(values, 8, 7)
    return jnp.concatenate([high, values - high], axis=-2).astype(BF16)


def joined(slots):
    rows = slots.shape[-2] // 2
    slots = slots.astype(F32)
    return slots[..., :rows, :] + slots[..., rows:, :]


def reduce_entry(place, quad, weight_grad, vectors, squares, second):
    shards, reps = lax.axis_size("shard"), lax.axis_size("rep")
    quads = shards // QUAD
    width, cols = weight_grad.shape
    sizes = [v.shape[0] // shards for v in vectors]
    spread = jnp.concatenate([v.reshape(shards, -1) for v in vectors], axis=1)
    if reps != 2 or not is_power(quads):
        laid = jnp.zeros((QUAD, width, cols), BF16)
        laid = from_quad_columns(lax.dynamic_update_index_in_dim(laid, weight_grad, place, 0), width)
        grad = lax.psum_scatter(laid, "shard", scatter_dimension=0, tiled=True)
        grad = lax.psum(grad, "rep").astype(F32)
        total = lax.psum_scatter(spread.astype(BF16), "shard", scatter_dimension=0, tiled=True)
        total = lax.psum(total, "rep").astype(F32).reshape(-1)
        squares = lax.psum(squares, ("rep", "shard"))
        second = second()
    else:
        rep = lax.axis_index("rep")
        rows = width // shards // 2
        room = rows // 2 * 64
        spread = jnp.concatenate([spread, jnp.broadcast_to(squares, (shards, 1))], axis=1)
        spread = jnp.pad(spread, ((0, 0), (0, room - spread.shape[1])))
        slots = split_low(spread.reshape(shards, 1, rows // 2, 64))
        slots = jnp.broadcast_to(slots, (shards, 2, rows, 64))
        payload = jnp.concatenate([weight_grad.reshape(shards, 2, rows, cols), slots], axis=3)

        def add(arrays):
            total = sum(a[..., :cols].astype(F32) for a in arrays).astype(BF16)
            return jnp.concatenate([total, split_low(sum(joined(a[..., cols:]) for a in arrays))], axis=-1)

        side = lambda number: jnp.where(rep == 1, payload[:, number], payload[:, 1 - number])
        held = add([side(1), trade_rep(side(0))])
        held = swap_all(held.reshape(shards, rows, cols + 64)).reshape(quads, QUAD, rows, cols + 64)
        second = second()
        held, *second = together(held, *second)
        grad = sum(held[q, :, :, :cols].astype(F32) for q in range(quads)).astype(BF16)
        slots = sum(joined(held[q, :, :, cols:]) for q in range(quads))
        grad = from_quad_columns(grad, width)
        grad = pair_in_order(rep, grad, trade_rep(grad)).reshape(2 * rows, 3 * width).astype(F32)
        total = jnp.sum(slots, axis=0).reshape(-1)
        squares = total[sum(sizes)]
    whole, start = [], 0
    for size in sizes:
        whole.append(total[start : start + size])
        start += size
    return grad, whole, squares, second


def rep_part(array):
    reps = lax.axis_size("rep")
    rows = array.shape[0] // reps
    return lax.dynamic_slice_in_dim(array, lax.axis_index("rep") * rows, rows, 0)


def whole_tiles(rows):
    quads = lax.axis_size("shard") // QUAD
    return lax.axis_size("rep") == 2 and is_power(quads) and rows % 16 == 0


def pack_rest(wide, outward, narrow):
    rows = wide.shape[0]
    width = outward.shape[1]
    times = narrow.shape[0] // rows
    first = lax.axis_index("rep") == 0
    part = width // 2
    folded = narrow.reshape(times, rows, width).transpose(1, 0, 2).reshape(rows, times * width)
    return jnp.concatenate(
        [jnp.where(first, wide, folded), jnp.where(first, outward[:, :part], outward[:, part:])], axis=1
    )


def fetch_rest_plain(wide, outward, narrow):
    shards, reps = lax.axis_size("shard"), lax.axis_size("rep")
    wide, outward, narrow = rep_part(wide), rep_part(outward), rep_part(narrow)
    rows, ff = wide.shape
    width = outward.shape[1]
    times = narrow.shape[0] // rows
    folded = narrow.reshape(times, rows, width).transpose(1, 0, 2).reshape(rows, times * width)
    packed = jnp.concatenate([wide, outward, folded], axis=1)
    full = lax.all_gather(packed, ("shard", "rep"), axis=0, tiled=True)
    unfolded = full[:, ff + width :].reshape(shards * reps, rows, times, width).transpose(0, 2, 1, 3)
    return full[:, :ff], full[:, ff : ff + width], unfolded.reshape(ff, width)


def unpack_grads(mine):
    rows, cols = mine.shape
    part = cols // 9
    width, ff = 2 * part, 8 * part
    first, second = pair_in_order(lax.axis_index("rep"), mine, trade_rep(mine)).astype(F32)
    unfolded = second[:, :ff].reshape(rows, 4, width).transpose(1, 0, 2)
    return (
        first[:, :ff],
        jnp.concatenate([first[:, ff:], second[:, ff:]], axis=1),
        unfolded.reshape(rows * 4, width),
    )


def reduce_rest_plain(normed, pre_grad, hidden, branch_two, mixed, branch):
    shards, reps = lax.axis_size("shard"), lax.axis_size("rep")
    width, ff = normed.shape[1], hidden.shape[1]
    narrow = dg(hidden, branch_two, 0, 0).astype(BF16)
    wide = dg(normed, pre_grad, 0, 0).astype(BF16)
    outward = dg(mixed, branch, 1, 0).astype(BF16)
    devices = shards * reps
    rows = width // devices
    times = ff // width
    folded = narrow.reshape(devices, times, rows, width).transpose(0, 2, 1, 3).reshape(width, times * width)
    packed = jnp.concatenate([wide, outward, folded], axis=1)
    part = lax.psum_scatter(packed, ("shard", "rep"), scatter_dimension=0, tiled=True)
    full = lax.all_gather(part, "rep", axis=0, tiled=False).astype(F32)
    unfolded = full[:, :, ff + width :].reshape(reps, rows, times, width).transpose(0, 2, 1, 3)
    return (
        full[:, :, :ff].reshape(reps * rows, ff),
        full[:, :, ff : ff + width].reshape(reps * rows, width),
        unfolded.reshape(reps * rows * times, width),
    )


def local(
    incoming_tokens,
    mentor_outputs,
    counting_flags,
    opening_scale_factor,
    opening_offset_vector,
    query_key_value_map,
    asking_offset,
    content_offset,
    attend_result_map,
    attend_result_offset,
    latter_scale_factor,
    latter_offset_vector,
    widen_projection,
    hidden_offset,
    narrow_projection,
    narrow_offset,
):
    shards = lax.axis_size("shard")
    length, width = incoming_tokens.shape
    tokens = QUAD * length
    head_rows = HL * HD
    me = lax.axis_index("shard")
    place, quad = me % QUAD, me // QUAD
    place_arg = place.reshape(1).astype(jnp.int32)
    late = (quad % 2 == 0).reshape(1).astype(jnp.int32)
    quads = shards // QUAD
    fast = whole_tiles(query_key_value_map.shape[0])
    rep = lax.axis_index("rep")
    one = lambda number: number.reshape(1).astype(jnp.int32)
    flags = counting_flags.astype(F32)
    flag_rows = counting_flags.reshape(-1, min(256, length))
    vectors = [
        opening_scale_factor,
        opening_offset_vector,
        asking_offset,
        content_offset,
        attend_result_offset,
        latter_scale_factor,
        latter_offset_vector,
        narrow_offset,
        hidden_offset,
    ]
    rest_weights = (widen_projection, attend_result_map, narrow_projection)
    half = length // 2
    a, b = incoming_tokens[:half], incoming_tokens[half:]
    a1, b2 = trade(a, 1), trade(b, 2)
    if fast:
        payload = entry_payload(one(rep), query_key_value_map, vectors, flag_rows, shards)
        stack = pack_rest(*rest_weights)[None]
        a, b, a1, b2, payload = together(jnp.concatenate([a, a1]), jnp.concatenate([b, b2]), a1, b2, payload)
        a23, b13 = trade(a, 2), trade(b, 1)
        held = swap_all(payload)
        for bit in range(quads.bit_length() - 1):
            stack = pair_in_order((quad >> bit) & 1, stack, trade(stack, QUAD << bit))
            stack = stack.reshape(-1, *stack.shape[2:])
        a23, b13, held, stack = together(a23, b13, held, stack)
        rest_held = [stack] + [trade(stack, j) for j in range(1, QUAD)]
        sizes, depth = [v.shape[0] for v in vectors], query_key_value_map.shape[0]
        entry_weight, vectors, count_all = fetch_entry_last(held, sizes, depth, flag_rows.shape[0])
    else:
        entry_weight, vectors, count_all = fetch_entry_plain(place, query_key_value_map, vectors, flag_rows)
        wide_full, outward_full, narrow_full = fetch_rest_plain(*rest_weights)
        a23, b13 = trade(jnp.concatenate([a, a1]), 2), trade(jnp.concatenate([b, b2]), 1)
    pieces = [incoming_tokens, a1, b2, a23, b13]
    pregain, preshift, querybias, valuebias, outbias, midgain, midshift, shrinkbias, expandbias = (
        v.astype(F32) for v in vectors
    )
    own_rows = lambda v: lax.dynamic_slice_in_dim(v, place * head_rows, head_rows, 0)
    bias = jnp.concatenate([own_rows(querybias), jnp.zeros((head_rows,), F32), own_rows(valuebias)])
    normal_quad, projected, swap_send, pair_send = enter(
        place_arg, late, pieces, entry_weight, bias[:, None], pregain[None], preshift[None]
    )
    heads = projected.reshape(3 * HL, HD, tokens)
    swapped, pair = swap_sides(swap_send), to_late(pair_send)
    o_own, l_own = own_forward(heads)
    swapped, l_own = together(swapped, l_own)
    o_first, o_low, l_first = cross_forward(late, heads, swapped)
    pair, o_low = together(pair, o_low)
    o_here, o_low, l_here = cross_forward(late, heads, swapped, pair, o_low)
    o_got = to_late(o_low)
    if fast:
        o_got, *rest_held = together(o_got, *rest_held)
        rest_got = [trade_rep(array) for array in rest_held]
    mixed_wide, mixed_low, levels = merge(
        late, o_own, l_own, o_got, o_first, l_first, o_here, l_here
    )
    mixed = swap_quad(mixed_low).reshape(width, length)
    if fast:
        _, *rest_got = together(mixed_low, *rest_got)
        wide_full, outward_full, narrow_full = unpack(place_arg, one(rep), rest_held, rest_got)

    inputs = incoming_tokens.astype(F32)
    middle = inputs + (dg(mixed, outward_full, 0, 0) + outbias)
    normal_two, factor_two = normalize(middle)
    normed_two = (normal_two * midgain + midshift).astype(BF16)
    pre_act = dg(normed_two, wide_full, 1, 0) + expandbias
    curve = 0.044715 * pre_act * pre_act
    bend = jnp.tanh((2 / jnp.pi) ** 0.5 * pre_act * (1.0 + curve))
    hidden = (0.5 * pre_act * (1.0 + bend)).astype(BF16)
    slope = 0.5 * (1.0 + bend) + (0.5 * (2 / jnp.pi) ** 0.5) * pre_act * (1.0 - bend * bend) * (1.0 + 3.0 * curve)
    hidden, slope = together(hidden, slope.astype(BF16))
    output = middle + (dg(hidden, narrow_full, 1, 0) + shrinkbias)
    weight_rows = flags[:, None]
    mismatch = output - mentor_outputs.astype(F32)
    squares = jnp.sum(weight_rows * mismatch * mismatch)
    token_total = length * lax.axis_size("rep") * shards
    output_grad = 2.0 * token_total / count_all * weight_rows * mismatch

    branch_two_grad = output_grad.astype(BF16)
    shrinkbias_grad = column_sums(branch_two_grad)
    hidden_grad = dg(branch_two_grad, narrow_full, 1, 1)
    pre_grad = (slope.astype(F32) * hidden_grad).astype(BF16)
    expandbias_grad = column_sums(pre_grad)
    normed_two_grad = dg(pre_grad, wide_full, 1, 1)
    midgain_grad = jnp.sum(normed_two_grad * normal_two, axis=0)
    midshift_grad = jnp.sum(normed_two_grad, axis=0)
    scaled = normed_two_grad * midgain
    middle_grad = output_grad + factor_two * (
        scaled
        - jnp.mean(scaled, axis=-1, keepdims=True)
        - normal_two * jnp.mean(scaled * normal_two, axis=-1, keepdims=True)
    )
    branch_grad = middle_grad.astype(BF16)
    outbias_grad = column_sums(branch_grad)
    mixed_grad = dg(outward_full, branch_grad, 1, 1).astype(BF16)
    grads = swap_quad(mixed_grad.reshape(QUAD, head_rows, length))
    if fast:
        grads_of = lambda first, normed, other=None: rest_grads(
            one(first), place_arg, shards, normed, pre_grad, hidden, branch_two_grad, mixed, branch_grad, other
        )
        share = grads_of(rep == 1, normed_two)
        grads, share = together(grads, share)
        share = trade_rep(share)
    else:
        rest = reduce_rest_plain(normed_two, pre_grad, hidden, branch_two_grad, mixed, branch_grad)
    inners, g_send = prepare(grads, mixed_wide, levels)
    g_sent = to_early(g_send)
    own_first = own_backward(heads, grads, levels, inners, 0, 1)
    if fast:
        share, *own_first = together(share, *own_first)
        share = grads_of(rep == 0, normed_two, share)
        g_sent, share = together(g_sent, share)
        share = share.reshape(QUAD, quads, width // shards, -1)
        side = quads // 2
        got_a = trade(jnp.stack([share[1, :side], share[3, :side]]), 1)
        got_b = trade(share[2:, side:], 2)
    dq_low, early_here, pair_back = cross_backward(
        late, heads, grads, levels, inners, swapped, pair, g_sent
    )
    levels, pair_back = together(levels, pair_back)
    dq_got, pair_got = to_late(dq_low), to_early(pair_back)
    if fast:
        last_a = (share[2, :side].astype(F32) + got_a[1].astype(F32)).astype(BF16)
        last_b = (share[1, side:].astype(F32) + got_b[1].astype(F32)).astype(BF16)
        levels, pair_back, last_a, last_b = together(levels, pair_back, last_a, last_b)
        last_a, last_b = trade(last_a, 2), trade(last_b, 1)
    own_last = own_backward(heads, grads, levels, inners, 1, HL - 1)
    own_last = together(*own_last, dq_got, pair_got)
    *own_last, dq_got, pair_got = own_last
    if fast:
        parts = (share[0, :side], got_a[0], last_a), (share[0, side:], got_b[0], last_b)
        share = jnp.concatenate([sum(p.astype(F32) for p in part).astype(BF16) for part in parts])
        dq_last, share = together(own_last[0], share)
        own_last = [dq_last, *own_last[1:]]
        share = swap_quads(share)
    *shares, heads_grad, bias_part = leave_tokens(
        place_arg,
        late,
        [*own_first, *own_last],
        (dq_low, early_here),
        dq_got,
        pair_got,
        entry_weight,
    )
    normal_grad = dg(normal_quad, heads_grad, 0, 1)
    grad_sums = bias_part[:, 0]
    weight_cols = entry_weight[:, : 3 * head_rows].astype(F32)
    inward_part = (pregain[:, None] * normal_grad + preshift[:, None] * grad_sums).astype(BF16)
    pregain_part = jnp.sum(weight_cols * normal_grad, axis=1)
    preshift_part = jnp.sum(weight_cols * grad_sums, axis=1)
    half = length // 2
    keep, a_parts, b_parts = shares[0], shares[1:4], shares[4:7]
    first_a, first_b = trade(a_parts[2], 1), trade(b_parts[2], 2)
    if fast:
        inward_part, share, first_a, first_b = together(inward_part, share, first_a, first_b)
    wide = lambda array: array.astype(F32)

    def second_step():
        return (
            trade(a_parts[0], 1),
            trade(b_parts[1], 2),
            trade((wide(a_parts[1]) + wide(first_a)).astype(BF16), 2),
            trade((wide(b_parts[0]) + wide(first_b)).astype(BF16), 1),
        )

    spread = lambda v: lax.dynamic_update_slice_in_dim(
        jnp.zeros((width,), F32), v, place * head_rows, 0
    )
    inward_grad, vector_grads, squares_all, arrived = reduce_entry(
        place,
        quad,
        inward_part,
        [
            pregain_part,
            preshift_part,
            spread(bias_part[:head_rows, 0]),
            spread(bias_part[2 * head_rows :, 0]),
            outbias_grad,
            midgain_grad,
            midshift_grad,
            shrinkbias_grad,
            expandbias_grad,
        ],
        squares,
        second_step,
    )
    normed_one_grad = jnp.concatenate(
        [
            keep[:half] + wide(arrived[0]) + wide(arrived[2]),
            keep[half:] + wide(arrived[1]) + wide(arrived[3]),
        ]
    )
    if fast:
        rest = unpack_grads(jnp.sum(share.astype(F32), axis=0).astype(BF16))
    distill_loss = squares_all / count_all
    normal_one, factor_one = normalize(inputs)
    scaled_one = normed_one_grad * pregain
    input_part = factor_one * (
        scaled_one
        - jnp.mean(scaled_one, axis=-1, keepdims=True)
        - normal_one * jnp.mean(scaled_one * normal_one, axis=-1, keepdims=True)
    )
    states_gradient = (middle_grad + input_part).astype(BF16)
    return (
        distill_loss,
        output.astype(BF16),
        states_gradient,
        vector_grads[0],
        vector_grads[1],
        inward_grad,
        vector_grads[2],
        vector_grads[3],
        rest[1],
        vector_grads[4],
        vector_grads[5],
        vector_grads[6],
        rest[0],
        vector_grads[8],
        rest[2],
        vector_grads[7],
    )


def solution(mesh):
    rows, vector, matrix = P(("rep", "shard"), None), P("shard"), P("shard", None)
    return jax.shard_map(
        local,
        mesh=mesh,
        in_specs=(
            rows,
            rows,
            P(("rep", "shard")),
            vector,
            vector,
            matrix,
            vector,
            vector,
            matrix,
            vector,
            vector,
            vector,
            matrix,
            vector,
            matrix,
            vector,
        ),
        out_specs=(
            P(),
            rows,
            rows,
            vector,
            vector,
            matrix,
            vector,
            vector,
            matrix,
            vector,
            vector,
            vector,
            matrix,
            vector,
            matrix,
            vector,
        ),
        check_vma=False,
    )
```
